32 devices in a mesh: expert: 16 (over z, y, core), dp: 2 (over x).
Axes of the slice: x: 2, y: 2, z: 4, core: 2. Of those that a mesh axis runs over, the one named last changes fastest.
Arguments:
- tokens: bfloat16 [2, 512, 2048], P('dp', 'expert'), may hold values from -6 to 6
- cotangent: bfloat16 [2, 512, 2048], P('dp', 'expert'), may hold values from -6 to 6
- expert_ids: int32 [2, 512, 8], P('dp', 'expert'), may hold values from 0 to 15, all different within a row; in each aligned block of 32 rows (0 to 31, 32 to 63, ..., all dimensions but the last counted through in order) at most 24 rows name the same one
- gate_probs: bfloat16 [2, 512, 8], P('dp', 'expert'), may hold values from 0.029907227 to 0.59765625
- alpha: float32 [1], replicated, may hold values from 0.4 to 1.2
- gamma: float32 [2048], replicated, may hold values from 0.5 to 1.5
- beta: float32 [2048], replicated, may hold values from -1.5 to 1.5
- w_in: bfloat16 [16, 2, 768, 2048], P('expert', None, 'dp'), may hold values from -0.125 to 0.125
- w_down: bfloat16 [16, 768, 2048], P('expert', 'dp'), may hold values from -0.21875 to 0.21875
Outputs:
- grad_tokens: bfloat16 [2, 512, 2048], P('dp', 'expert')
- grad_probs: bfloat16 [2, 512, 8], P('dp', 'expert')
- grad_down: bfloat16 [16, 768, 2048], P('expert', 'dp')
- grad_gamma: float32 [2048], replicated
- grad_beta: float32 [2048], replicated
- grad_alpha: float32 [1], replicated
The draws below stay inside these ranges and needn't reach their ends.
Inputs may be any that keep to these rules, and one draw needn't show every extreme that they name: `expert_ids`: each token names 8 different experts; among the 32 tokens of one block no expert is named by more than 24 tokens, and in some block some expert is named by exactly 24.
All inputs are finite; a program needn't handle non-finite values.
Results may differ from the reference program's by a relative error of at most 0.008.
Values may be sent and summed in bfloat16 or wider, within the bound.
No kernel may reach another device: no remote copies, remote signals or barrier semaphores. Data moves between devices by JAX's collectives and lax.ppermute only.
A program may use at most 64 MiB of HBM per device.

```python
import math
import jax
import jax.numpy as jnp
import numpy as np
from jax import lax

D = 2048
FF = 768
TOP = 8
TOK_DEV = 32
EXPERTS = 16
TOKENS = 512
BATCHES = 2
CAP = 24


def scaled_field(key):
    place = jnp.arange(TOKENS, dtype=jnp.float32) / TOKENS
    factor = (0.5 + place)[None, :, None]
    base = jnp.clip(jax.random.normal(key, (BATCHES, TOKENS, D), jnp.float32), -4.0, 4.0)
    return base * factor


def draw_tokens(key, part):
    return scaled_field(jax.random.fold_in(key, 11)).astype(jnp.bfloat16)


def draw_cotangent(key, part):
    return scaled_field(jax.random.fold_in(key, 23)).astype(jnp.bfloat16)


def block_scale(own_key, dims, split, low, top_value):
    loudness = 1.0
    for dim, parts in split:
        steps = jax.random.uniform(jax.random.fold_in(jax.random.fold_in(own_key, 6), dim), (parts,), jnp.float32, low / len(split), top_value / len(split))
        loudness = loudness * jnp.repeat(jnp.exp(steps), dims[dim] // parts).reshape((-1,) + (1,) * (len(dims) - 1 - dim))
    return loudness


def shared_out(stream_key, own, number, rows, amount, top, bound, skew):
    sequence = jax.random.permutation(stream_key, amount)
    heavy_load, usual = load_shares(amount, rows * top, bound, skew, True), load_shares(amount, rows * top, bound, skew, False)
    places = jnp.arange(amount)

    def named(sizes, offset_by):
        used = int((sizes > 0).sum())
        fixed = max(1, used // 4)
        shifted = fixed + (places - fixed + offset_by * (used - fixed)) % max(1, amount - fixed)
        return jnp.zeros((amount,), jnp.int32).at[sequence[jnp.where(places < fixed, places, shifted)]].set(jnp.asarray(sizes, jnp.int32))

    sizes = jnp.where(number % 4 == 0, named(heavy_load, number // 4), named(usual, number - number // 4 - 1))
    mixed = jax.random.permutation(jax.random.fold_in(own, 3), amount)
    donor, taker = mixed[0:amount // 2 * 2:2], mixed[1:amount // 2 * 2:2]
    slack = jnp.minimum(sizes[donor] - 1, bound - sizes[taker]) // 2
    slack = jnp.where((donor == sequence[0]) | (taker == sequence[0]) | (sizes[taker] == 0), 0, jnp.maximum(slack, 0))
    shifted = jax.random.randint(jax.random.fold_in(own, 4), (amount // 2,), 0, 1 << 20) % (slack + 1)
    sizes = sizes.at[donor].add(-shifted).at[taker].add(shifted)
    members = jnp.searchsorted(jnp.cumsum(sizes), jnp.arange(rows * top), side="right").astype(jnp.int32)
    grid = members.reshape(top, rows).T
    grid = grid[jax.random.permutation(jax.random.fold_in(own, 1), rows)]
    offset_by = jax.random.randint(jax.random.fold_in(own, 2), (rows, 1), 0, top)
    return jnp.take_along_axis(grid, (jnp.arange(top)[None, :] + offset_by) % top, axis=1)


def load_shares(count, total, bound, lean, full):
    weights = [(1 << 20) // math.isqrt(rank ** lean) + 1 for rank in range(1, count + 1)]
    largest = bound if full else min(bound, max(-(-total // count), total * weights[0] // sum(weights)))
    least = 1 if total - largest >= count - 1 else 0
    given, rest = [largest] + [least] * (count - 1), total - largest - least * (count - 1)
    while rest > 0:
        candidates = [i for i in range(1, count) if given[i] < largest] or [i for i in range(1, count) if given[i] < bound]
        pool, budget = sum([weights[i] for i in candidates]), rest
        for i in candidates:
            addition = min(bound - given[i], max(1, budget * weights[i] // pool), rest)
            given[i] = given[i] + addition
            rest = rest - addition
    return np.array(given)


def bell_draw(key, extent, deviation, limit, pieces=(), held_as=jnp.bfloat16):
    result = deviation * jax.random.normal(key, extent, jnp.float32)
    if pieces:
        result = result * block_scale(key, extent, pieces, -0.22, 0.18)
    return jnp.clip(result, -limit, limit).astype(held_as)


def setup_inputs(seed: int = 0) -> dict:
    seeds = jax.random.split(jax.random.key(seed), 10)
    tokens = draw_tokens(jax.random.fold_in(seeds[9], 71), 0)
    cotangent = draw_cotangent(jax.random.fold_in(seeds[9], 71), 0)
    expert_ids_keys = jax.random.split(jax.random.fold_in(seeds[2], 1), BATCHES * TOKENS // TOK_DEV)
    expert_ids_turns = jax.random.permutation(jax.random.fold_in(seeds[2], 3), BATCHES * TOKENS // TOK_DEV)
    expert_ids = jax.vmap(lambda own, number: shared_out(jax.random.fold_in(seeds[2], 2), own, number, TOK_DEV, EXPERTS, TOP, CAP, 2))(expert_ids_keys, expert_ids_turns).reshape((BATCHES, TOKENS, TOP))
    gate_probs = jnp.clip(jnp.exp(math.log(0.59765625) - 2.99491561 * jax.random.uniform(seeds[3], (BATCHES, TOKENS, TOP), jnp.float32) ** block_scale(seeds[3], (BATCHES, TOKENS, TOP), ((0, 2), (1, 16)), -0.2, 0.2)), 0.029907227, 0.59765625).astype(jnp.bfloat16)
    alpha = jnp.clip(jnp.exp(jax.random.uniform(seeds[4], (1,), jnp.float32, math.log(0.4), math.log(1.2))), 0.4, 1.2)
    gamma = jnp.clip(1.0 + 0.1 * jax.random.normal(seeds[5], (D,), jnp.float32), 0.5, 1.5)
    beta = bell_draw(seeds[6], (D,), 0.3, 1.5, (), jnp.float32)
    w_in = bell_draw(seeds[7], (EXPERTS, 2, FF, D), D ** -0.5, 0.125, ((0, 16), (2, 2)))
    w_down = bell_draw(seeds[8], (EXPERTS, FF, D), FF ** -0.5, 0.21875, ((0, 16), (1, 2)))
    return {"tokens": tokens, "cotangent": cotangent, "expert_ids": expert_ids, "gate_probs": gate_probs, "alpha": alpha, "gamma": gamma, "beta": beta, "w_in": w_in, "w_down": w_down}


residual_scale = 0.7071


def build_table(ids_batch):
    n_source = TOKENS // TOK_DEV
    labels = jnp.arange(EXPERTS, dtype=jnp.int32)
    onehot = (ids_batch[:, :, None] == labels[None, None, :]).astype(jnp.int32)
    picks = jnp.sum(onehot, axis=1).astype(jnp.int32).reshape(n_source, TOK_DEV, EXPERTS)
    before = (jnp.cumsum(picks, axis=1).astype(jnp.int32) - picks).reshape(TOKENS, EXPERTS)
    slots = jnp.sum(onehot * before[:, None, :], axis=2).astype(jnp.int32)
    source = (jnp.arange(TOKENS, dtype=jnp.int32) // TOK_DEV)[:, None]
    position = (ids_batch * n_source + source) * CAP + slots
    table = jnp.full((EXPERTS * n_source * CAP,), TOKENS * TOP, jnp.int32)
    table = table.at[position.reshape(-1)].set(jnp.arange(TOKENS * TOP, dtype=jnp.int32))
    return table.reshape(EXPERTS, n_source * CAP)


def reference(tokens, cotangent, expert_ids, gate_probs, alpha, gamma, beta, w_in, w_down):
    inputs = tokens.astype(jnp.float32)
    squashed = jnp.tanh(alpha[0] * inputs)
    normed = (gamma * squashed + beta).astype(jnp.bfloat16)
    tables = jax.vmap(build_table)(expert_ids)
    zero_rows = jnp.zeros((BATCHES, 1, D), jnp.bfloat16)
    normed_pad = jnp.concatenate([normed, zero_rows], axis=1)
    cot_pad = jnp.concatenate([cotangent, zero_rows], axis=1)
    prob_pad = jnp.concatenate([gate_probs.reshape(BATCHES, TOKENS * TOP), jnp.zeros((BATCHES, 1), jnp.bfloat16)], axis=1)
    batch_index = jnp.arange(BATCHES, dtype=jnp.int32)[:, None]
    slots_each = TOKENS // TOK_DEV * CAP

    def per_expert(carry, items):
        grad_acc, prob_acc = carry
        table_e, gate_up, lower = items
        token_index = (table_e // TOP).astype(jnp.int32)
        in_rows = normed_pad[batch_index, token_index].reshape(BATCHES * slots_each, D)
        cot_rows = cot_pad[batch_index, token_index].reshape(BATCHES * slots_each, D)
        prob_rows = prob_pad[batch_index, table_e].reshape(BATCHES * slots_each).astype(jnp.float32)
        w_gate = gate_up[0]
        w_upper = gate_up[1]
        gate_pre = jnp.dot(in_rows, w_gate.T, preferred_element_type=jnp.float32)
        up_value = jnp.dot(in_rows, w_upper.T, preferred_element_type=jnp.float32)
        sigma = jax.nn.sigmoid(gate_pre)
        activation = (gate_pre * sigma * up_value).astype(jnp.bfloat16)
        back = jnp.dot(cot_rows, lower.T, preferred_element_type=jnp.float32)
        weight_row = residual_scale * prob_rows
        scaled_cot = (weight_row[:, None] * cot_rows.astype(jnp.float32)).astype(jnp.bfloat16)
        d_act = weight_row[:, None] * back
        d_gate = (d_act * up_value * sigma * (1.0 + gate_pre * (1.0 - sigma))).astype(jnp.bfloat16)
        d_up = (d_act * gate_pre * sigma).astype(jnp.bfloat16)
        d_rows = (jnp.dot(d_gate, w_gate, preferred_element_type=jnp.float32) + jnp.dot(d_up, w_upper, preferred_element_type=jnp.float32)).astype(jnp.bfloat16)
        outputs = jnp.dot(activation, lower, preferred_element_type=jnp.float32)
        row_grad = (residual_scale * jnp.sum(cot_rows.astype(jnp.float32) * outputs, axis=1)).astype(jnp.bfloat16)
        partial_grad = jnp.einsum("bmf,bmd->bfd", activation.reshape(BATCHES, slots_each, FF).astype(jnp.float32), scaled_cot.reshape(BATCHES, slots_each, D).astype(jnp.float32), precision=lax.Precision.HIGHEST)
        rounded = lax.optimization_barrier(partial_grad.astype(jnp.bfloat16))
        total = jnp.sum(rounded.astype(jnp.float32), axis=0).astype(jnp.bfloat16)
        grad_acc = grad_acc.at[batch_index, token_index].add(d_rows.reshape(BATCHES, slots_each, D).astype(jnp.float32))
        prob_acc = prob_acc.at[batch_index, table_e].set(row_grad.reshape(BATCHES, slots_each))
        return (grad_acc, prob_acc), total

    grad_init = jnp.zeros((BATCHES, TOKENS + 1, D), jnp.float32)
    prob_init = jnp.zeros((BATCHES, TOKENS * TOP + 1), jnp.bfloat16)
    (grad_acc, prob_acc), grad_down = lax.scan(per_expert, (grad_init, prob_init), (jnp.swapaxes(tables, 0, 1), w_in, w_down))
    grad_normed = grad_acc[:, :TOKENS]
    grad_probs = prob_acc[:, :TOKENS * TOP].reshape(BATCHES, TOKENS, TOP)
    grad_gamma = jnp.sum(grad_normed * squashed, axis=(0, 1))
    grad_beta = jnp.sum(grad_normed, axis=(0, 1))
    pre_grad = grad_normed * gamma * (1.0 - squashed * squashed)
    grad_alpha = jnp.sum(pre_grad * inputs).reshape(1)
    grad_tokens = (cotangent.astype(jnp.float32) + alpha[0] * pre_grad).astype(jnp.bfloat16)
    return (grad_tokens, grad_probs, grad_down, grad_gamma, grad_beta, grad_alpha)
```

```python
import functools
import jax
import jax.numpy as jnp
from jax import lax
from jax.experimental import pallas as pl
from jax.experimental.pallas import tpu as pltpu
from jax.sharding import PartitionSpec as P

residual_scale = 0.7071
LANES = 128
f32 = jnp.float32
bf16 = jnp.bfloat16


def contract_width(left, right):
    return lax.dot_general(
        left, right, (((1,), (1,)), ((), ())), preferred_element_type=f32
    )


def add16(left, right):
    return (left.astype(f32) + right.astype(f32)).astype(bf16)


def rows_kernel(segments, width, hidden, *refs):
    count = len(segments)
    blocks = refs[:count]
    (w_in, w_down, gamma, beta, alpha, expert) = refs[count : count + 6]
    (grads_out, act_out, scaled_out, tail_out) = refs[count + 6 : count + 10]
    (normed, cot, weight) = refs[count + 10 :]
    rows = normed.shape[0]
    gain = alpha[0]
    mine = expert[0]
    gamma_row = gamma[...]
    beta_row = beta[...]
    for source, places in zip(blocks, segments):
        size = source.shape[0] // len(places)
        for part, to in enumerate(places):
            here, there = slice(part * size, (part + 1) * size), slice(to, to + size)
            squashed = jnp.tanh(gain * source[here, 0:width].astype(f32))
            normed[there, :] = (gamma_row * squashed + beta_row).astype(bf16)
            rows_cot = source[here, width : 2 * width]
            cot[there, :] = rows_cot
            gates = source[here, 2 * width :].astype(f32)
            lane = lax.broadcasted_iota(jnp.int32, gates.shape, 1)
            own = jnp.sum(jnp.where(lane == mine, gates, 0.0), axis=1, keepdims=True)
            own = residual_scale * own
            weight[there, :] = jnp.broadcast_to(own, (size, LANES))
            scaled_out[there, :] = (own * rows_cot.astype(f32)).astype(bf16)
    pre = contract_width(normed[...], w_in[...])
    back = contract_width(cot[...], w_down[...])
    gate_pre = pre[:, :hidden]
    up_value = pre[:, hidden:]
    sigma = jax.nn.sigmoid(gate_pre)
    silu = gate_pre * sigma
    activation = (silu * up_value).astype(bf16)
    act_out[...] = activation
    row_grad = residual_scale * jnp.sum(activation.astype(f32) * back, axis=1, keepdims=True)
    d_act = weight[:, 0:1] * back
    d_gate = d_act * up_value * sigma * (1.0 + gate_pre * (1.0 - sigma))
    grads_out[:, :hidden] = d_gate.astype(bf16)
    grads_out[:, hidden:] = (d_act * gate_pre * sigma).astype(bf16)
    lane = lax.broadcasted_iota(jnp.int32, (rows, LANES), 1)
    tail_out[...] = jnp.where(lane == mine, row_grad, 0.0).astype(bf16)


def grad_kernel(segments, half, *refs):
    count = len(segments)
    blocks = refs[:count]
    (near, far, w_near, w_far, tail, alpha, side) = refs[count : count + 7]
    (d_own, d_other, sums) = refs[count + 7 : count + 10]
    (squash, slope) = refs[count + 10 :]
    rows = near.shape[0]
    block = rows // 8
    gain = alpha[0]
    start = pl.multiple_of(side[0] * half, half)
    for source, places in zip(blocks, segments):
        size = source.shape[0] // len(places)
        for part, to in enumerate(places):
            inputs = source[part * size : (part + 1) * size, pl.ds(start, half)].astype(f32)
            squashed = jnp.tanh(gain * inputs)
            squash[to : to + size, :] = squashed
            slope[to : to + size, :] = (1.0 - squashed * squashed) * inputs
    mirrored = jnp.concatenate([far[rows // 2 :, :], far[: rows // 2, :]], axis=0)

    def place(cols, value):
        for x in range(2):
            for y in range(2):
                row = (x * 4 + y) * block
                d_own[x, y, :, cols] = value[row : row + block]
                row = (x * 4 + 2 + y) * block
                d_other[x, y, :, cols] = value[row : row + block]

    place(slice(half, half + LANES), tail[...])
    step = 512
    for at in range(0, half, step):
        cols = slice(at, at + step)
        part = jnp.dot(near[...], w_near[:, cols], preferred_element_type=f32)
        part = part + jnp.dot(mirrored, w_far[:, cols], preferred_element_type=f32)
        short = part.astype(bf16)
        place(cols, short)
        part = short.astype(f32)
        sums[0:1, cols] = jnp.sum(part, axis=0, keepdims=True)
        sums[1:2, cols] = jnp.sum(part * squash[:, cols], axis=0, keepdims=True)
        sums[2:3, cols] = jnp.sum(part * slope[:, cols], axis=0, keepdims=True)
        sums[3:8, cols] = jnp.zeros((5, step), f32)


def down_kernel(count, *refs):
    acts = refs[:count]
    scaled = refs[count : 2 * count]
    out = refs[2 * count]
    left, right = refs[2 * count + 1 :]
    half = acts[0].shape[0] // 2
    total = None
    for batch in range(2):
        for k in range(count):
            left[k * half : (k + 1) * half, :] = acts[k][batch * half : (batch + 1) * half, :]
            right[k * half : (k + 1) * half, :] = scaled[k][batch * half : (batch + 1) * half, :]
        term = lax.dot_general(
            left[...], right[...], (((0,), (0,)), ((), ())), preferred_element_type=f32
        )
        term = term.astype(bf16).astype(f32)
        total = term if total is None else total + term
    out[...] = total.astype(bf16)


def whole():
    return pl.BlockSpec(memory_space=pltpu.VMEM)


def scalar():
    return pl.BlockSpec(memory_space=pltpu.SMEM)


def dense_shards(tokens, cotangent, expert_ids, gate_probs, alpha, gamma, beta, w_in, w_down):
    experts = lax.axis_size("expert")
    planes = experts // 4
    block = tokens.shape[1]
    width = tokens.shape[2]
    hidden = w_down.shape[1]
    rows = 8 * block
    me = lax.axis_index("expert")

    def go_x(v):
        return lax.ppermute(v, "dp", [(0, 1), (1, 0)])

    def go_y(v):
        return lax.ppermute(v, "expert", [(e, e ^ 2) for e in range(experts)])

    def go_core(v):
        return lax.ppermute(v, "expert", [(e, e ^ 1) for e in range(experts)])

    def go_z(v):
        return lax.ppermute(v, "expert", [(e, (e + 4) % experts) for e in range(experts)])

    lanes = jnp.arange(LANES, dtype=jnp.int32)
    picks = expert_ids[0][:, :, None] == lanes[None, None, :]
    gates = jnp.sum(jnp.where(picks, gate_probs[0].astype(f32)[:, :, None], 0.0), axis=1)
    own = jnp.concatenate([tokens[0], cotangent[0], gates.astype(bf16)], axis=1)

    flat_in = w_in[0].reshape(2 * hidden, width)
    flat_down = w_down[0]
    gamma_row = gamma.reshape(1, width)
    beta_row = beta.reshape(1, width)
    mine = me.reshape(1).astype(jnp.int32)
    half = width // 2
    side = lax.axis_index("dp").astype(jnp.int32)
    w_near = lax.dynamic_slice_in_dim(flat_in, side * half, half, axis=1)
    w_send = lax.dynamic_slice_in_dim(flat_in, (1 - side) * half, half, axis=1)

    segments = tuple(
        tuple((x * 4 + core * 2 + y) * block for x in range(2))
        for core in range(2)
        for y in range(2)
    )
    params = pltpu.CompilerParams(vmem_limit_bytes=40 << 20)

    def first_half(arrays):
        return pl.pallas_call(
            functools.partial(rows_kernel, segments, width, hidden),
            out_shape=(
                jax.ShapeDtypeStruct((rows, 2 * hidden), bf16),
                jax.ShapeDtypeStruct((rows, hidden), bf16),
                jax.ShapeDtypeStruct((rows, width), bf16),
                jax.ShapeDtypeStruct((rows, LANES), bf16),
            ),
            in_specs=[whole()] * 8 + [scalar(), scalar()],
            out_specs=(whole(),) * 4,
            scratch_shapes=[
                pltpu.VMEM((rows, width), bf16),
                pltpu.VMEM((rows, width), bf16),
                pltpu.VMEM((rows, LANES), f32),
            ],
            compiler_params=params,
            name="rows",
        )(*arrays, flat_in, flat_down, gamma_row, beta_row, alpha, mine)

    def second_half(arrays, near, far, w_far, tail):
        return pl.pallas_call(
            functools.partial(grad_kernel, segments, half),
            out_shape=(
                jax.ShapeDtypeStruct((2, 2, block, half + LANES), bf16),
                jax.ShapeDtypeStruct((2, 2, block, half + LANES), bf16),
                jax.ShapeDtypeStruct((8, half), f32),
            ),
            in_specs=[whole()] * 9 + [scalar(), scalar()],
            out_specs=(whole(),) * 3,
            scratch_shapes=[
                pltpu.VMEM((rows, half), f32),
                pltpu.VMEM((rows, half), f32),
            ],
            compiler_params=params,
            name="grads",
        )(*arrays, near, far, w_near, w_far, tail, alpha, side.reshape(1))

    def settle(d_own, d_other):
        got = go_core(d_other)
        send = add16(d_own[:, 1], got[:, 1])
        keep = d_own[:, 0].astype(f32) + got[:, 0].astype(f32)
        return keep + go_y(send).astype(f32)

    own = jnp.concatenate([own, go_x(own)], axis=0)
    own, w_send = lax.optimization_barrier((own, w_send))
    w_far = go_x(w_send)
    planed = [own]
    for _ in range(planes - 1):
        planed.append(go_z(planed[-1]))
    order = list(range(planes))
    arrays, acts, scaled, totals, ready = {}, {}, {}, [], {}
    for k in order:
        far = go_y(planed[k])
        arrays[k] = (planed[k], far, go_core(planed[k]), go_core(far))
        grads, acts[k], scaled[k], tail = first_half(arrays[k])
        ready[k] = (grads, go_x(grads), w_far, tail)
    carry = None
    for k in order[1:] + order[:1]:
        d_own, d_other, sums = second_half(arrays[k], *ready[k])
        totals.append(sums)
        value = settle(d_own, d_other)
        if carry is not None:
            value = value + go_z(carry).astype(f32)
        carry = value.astype(bf16)
    acts = [acts[k] for k in order]
    scaled = [scaled[k] for k in order]
    other = go_x(carry[1]).astype(f32)
    first = jnp.where(side == 0, value[0, :, :half], other[:, :half])
    last = jnp.where(side == 0, other[:, :half], value[0, :, :half])
    grad_normed = jnp.concatenate([first, last], axis=1)
    row_grads = value[0, :, half:] + other[:, half:]

    sums = sum(totals[1:], totals[0])
    for go in (go_core, go_y):
        sums = sums + go(sums)
    hop = 4
    while hop < experts:
        sums = sums + lax.ppermute(sums, "expert", [(e, e ^ hop) for e in range(experts)])
        hop *= 2
    crossed = go_x(sums)
    sums = jnp.concatenate(
        [jnp.where(side == 0, sums, crossed), jnp.where(side == 0, crossed, sums)], axis=1
    )

    grad_down = pl.pallas_call(
        functools.partial(down_kernel, planes),
        out_shape=jax.ShapeDtypeStruct((hidden, width), bf16),
        in_specs=[whole()] * (2 * planes),
        out_specs=whole(),
        scratch_shapes=[
            pltpu.VMEM((planes * rows // 2, hidden), bf16),
            pltpu.VMEM((planes * rows // 2, width), bf16),
        ],
        compiler_params=pltpu.CompilerParams(vmem_limit_bytes=40 << 20),
        name="down",
    )(*acts, *scaled)

    inputs = tokens[0].astype(f32)
    squashed = jnp.tanh(alpha[0] * inputs)
    pre_grad = grad_normed * gamma * (1.0 - squashed * squashed)
    grad_tokens = (cotangent[0].astype(f32) + alpha[0] * pre_grad).astype(bf16)
    grad_probs = jnp.sum(jnp.where(picks, row_grads[:, None, :], 0.0), axis=2).astype(bf16)
    grad_beta = sums[0]
    grad_gamma = sums[1]
    grad_alpha = jnp.sum(sums[2] * gamma).reshape(1)
    return (
        grad_tokens[None],
        grad_probs[None],
        grad_down[None],
        grad_gamma,
        grad_beta,
        grad_alpha,
    )


def slot_layout(ids_local, expert_count, capacity):
    token_count, top_count = ids_local.shape
    labels = jnp.arange(expert_count, dtype=jnp.int32)
    onehot = (ids_local[:, :, None] == labels[None, None, :]).astype(jnp.int32)
    picks = jnp.sum(onehot, axis=1)
    order = jnp.arange(token_count, dtype=jnp.int32)
    earlier = (order[None, :] < order[:, None]).astype(f32)
    before = jnp.dot(earlier, picks.astype(f32), precision=lax.Precision.HIGHEST)
    slots = jnp.sum(onehot * before.astype(jnp.int32)[:, None, :], axis=2)
    position = ids_local * capacity + slots
    pairs = jnp.arange(token_count * top_count, dtype=jnp.int32)
    table = jnp.full((expert_count * capacity,), token_count * top_count, jnp.int32)
    table = table.at[position.reshape(-1)].set(pairs)
    return (position, table)


def routed_shards(tokens, cotangent, expert_ids, gate_probs, alpha, gamma, beta, w_in, w_down):
    expert_count = lax.axis_size("expert")
    token_count = tokens.shape[1]
    top_count = expert_ids.shape[2]
    width = tokens.shape[2]
    capacity = 3 * token_count * top_count // (2 * expert_count)
    rows_total = expert_count * capacity
    inputs = tokens[0].astype(jnp.float32)
    squashed = jnp.tanh(alpha[0] * inputs)
    normed = (gamma * squashed + beta).astype(jnp.bfloat16)
    position, table = slot_layout(expert_ids[0], expert_count, capacity)
    source_token = table // top_count
    zero_row = jnp.zeros((1, width), jnp.bfloat16)
    normed_pad = jnp.concatenate([normed, zero_row], axis=0)
    cot_pad = jnp.concatenate([cotangent[0], zero_row], axis=0)
    prob_pad = jnp.concatenate([gate_probs[0].reshape(-1), jnp.zeros((1,), jnp.bfloat16)], axis=0)
    send_rows = normed_pad[source_token].reshape(expert_count, capacity, width)
    send_cot = cot_pad[source_token].reshape(expert_count, capacity, width)
    send_prob = prob_pad[table].reshape(expert_count, capacity)

    def swap(value):
        return lax.all_to_all(value, "expert", split_axis=0, concat_axis=0, tiled=True)

    in_rows = swap(send_rows).reshape(rows_total, width)
    cot_rows = swap(send_cot).reshape(rows_total, width)
    prob_rows = swap(send_prob).reshape(rows_total).astype(jnp.float32)
    gate_up = lax.all_gather(w_in, "dp", axis=2, tiled=True)
    w_lower = lax.all_gather(w_down, "dp", axis=1, tiled=True)[0]
    w_gate = gate_up[0, 0]
    w_upper = gate_up[0, 1]
    gate_pre = contract_width(in_rows, w_gate)
    up_value = contract_width(in_rows, w_upper)
    sigma = jax.nn.sigmoid(gate_pre)
    activation = (gate_pre * sigma * up_value).astype(jnp.bfloat16)
    back = contract_width(cot_rows, w_lower)
    weight_row = residual_scale * prob_rows
    scaled_cot = (weight_row[:, None] * cot_rows.astype(jnp.float32)).astype(jnp.bfloat16)
    row_grad = residual_scale * jnp.sum(activation.astype(jnp.float32) * back, axis=1)
    d_act = weight_row[:, None] * back
    d_gate = (d_act * up_value * sigma * (1.0 + gate_pre * (1.0 - sigma))).astype(jnp.bfloat16)
    d_up = (d_act * gate_pre * sigma).astype(jnp.bfloat16)
    d_rows = (
        jnp.dot(d_gate, w_gate, preferred_element_type=jnp.float32)
        + jnp.dot(d_up, w_upper, preferred_element_type=jnp.float32)
    ).astype(jnp.bfloat16)
    back_rows = swap(d_rows.reshape(expert_count, capacity, width))
    back_probs = swap(row_grad.astype(jnp.bfloat16).reshape(expert_count, capacity))
    partial_grad = lax.dot_general(
        activation, scaled_cot, (((0,), (0,)), ((), ())), preferred_element_type=jnp.float32
    )
    grad_down = lax.psum_scatter(
        partial_grad[None].astype(jnp.bfloat16), "dp", scatter_dimension=1, tiled=True
    )
    picked = back_rows.reshape(rows_total, width)[position]
    grad_normed = jnp.sum(picked.astype(jnp.float32), axis=1)
    grad_probs = back_probs.reshape(rows_total)[position]
    gamma_part = jnp.sum(grad_normed * squashed, axis=0)
    beta_part = jnp.sum(grad_normed, axis=0)
    pre_grad = grad_normed * gamma * (1.0 - squashed * squashed)
    alpha_part = jnp.sum(pre_grad * inputs).reshape(1)
    grad_gamma, grad_beta, grad_alpha = lax.psum(
        (gamma_part, beta_part, alpha_part), ("expert", "dp")
    )
    grad_tokens = (cotangent[0].astype(jnp.float32) + alpha[0] * pre_grad).astype(jnp.bfloat16)
    return (grad_tokens[None], grad_probs[None], grad_down, grad_gamma, grad_beta, grad_alpha)


def shards(*arrays):
    experts = lax.axis_size("expert")
    top_count = arrays[2].shape[2]
    dense = (
        lax.axis_size("dp") == 2
        and experts % 4 == 0
        and (experts & (experts - 1)) == 0
        and experts <= LANES
        and 2 * top_count >= experts
    )
    return (dense_shards if dense else routed_shards)(*arrays)


def solution(mesh):
    placed = (
        P("dp", "expert", None),
        P("dp", "expert", None),
        P("dp", "expert", None),
        P("dp", "expert", None),
        P(),
        P(),
        P(),
        P("expert", None, "dp", None),
        P("expert", "dp", None),
    )
    return jax.shard_map(
        shards,
        mesh=mesh,
        in_specs=placed,
        out_specs=(
            P("dp", "expert", None),
            P("dp", "expert", None),
            P("expert", "dp", None),
            P(),
            P(),
            P(),
        ),
        check_vma=False,
    )
```

```python
import functools
import jax
import jax.numpy as jnp
from jax import lax
from jax.experimental import pallas as pl
from jax.experimental.pallas import tpu as pltpu
from jax.sharding import PartitionSpec as P

residual_scale = 0.7071
LANES = 128
f32 = jnp.float32
bf16 = jnp.bfloat16


def contract_width(left, right):
    return lax.dot_general(
        left, right, (((1,), (1,)), ((), ())), preferred_element_type=f32
    )


def add16(left, right):
    return (left.astype(f32) + right.astype(f32)).astype(bf16)


def rows_kernel(segments, width, hidden, *refs):
    count = len(segments)
    blocks = refs[:count]
    (w_in, w_down, gamma, beta, alpha, expert) = refs[count : count + 6]
    (grads_out, act_out, scaled_out, tail_out) = refs[count + 6 : count + 10]
    (normed, cot, weight) = refs[count + 10 :]
    rows = normed.shape[0]
    gain = alpha[0]
    mine = expert[0]
    gamma_row = gamma[...]
    beta_row = beta[...]
    for source, places in zip(blocks, segments):
        size = source.shape[0] // len(places)
        for part, to in enumerate(places):
            here, there = slice(part * size, (part + 1) * size), slice(to, to + size)
            squashed = jnp.tanh(gain * source[here, 0:width].astype(f32))
            normed[there, :] = (gamma_row * squashed + beta_row).astype(bf16)
            rows_cot = source[here, width : 2 * width]
            cot[there, :] = rows_cot
            gates = source[here, 2 * width :].astype(f32)
            lane = lax.broadcasted_iota(jnp.int32, gates.shape, 1)
            own = jnp.sum(jnp.where(lane == mine, gates, 0.0), axis=1, keepdims=True)
            own = residual_scale * own
            weight[there, :] = jnp.broadcast_to(own, (size, LANES))
            scaled_out[there, :] = (own * rows_cot.astype(f32)).astype(bf16)
    pre = contract_width(normed[...], w_in[...])
    back = contract_width(cot[...], w_down[...])
    gate_pre = pre[:, :hidden]
    up_value = pre[:, hidden:]
    sigma = jax.nn.sigmoid(gate_pre)
    silu = gate_pre * sigma
    activation = (silu * up_value).astype(bf16)
    act_out[...] = activation
    row_grad = residual_scale * jnp.sum(activation.astype(f32) * back, axis=1, keepdims=True)
    d_act = weight[:, 0:1] * back
    d_gate = d_act * up_value * sigma * (1.0 + gate_pre * (1.0 - sigma))
    grads_out[:, :hidden] = d_gate.astype(bf16)
    grads_out[:, hidden:] = (d_act * gate_pre * sigma).astype(bf16)
    lane = lax.broadcasted_iota(jnp.int32, (rows, LANES), 1)
    tail_out[...] = jnp.where(lane == mine, row_grad, 0.0).astype(bf16)


def grad_kernel(segments, half, parts, *refs):
    count = len(segments)
    blocks = refs[:count]
    (near, far, w_in, *w_far) = refs[count : count + 3 + parts]
    (tail, alpha, side, d_own, d_other, sums, squash, slope) = refs[count + 3 + parts :]
    rows = near.shape[0]
    block = rows // 8
    gain = alpha[0]
    start = pl.multiple_of(side[0] * half, half)
    for source, places in zip(blocks, segments):
        size = source.shape[0] // len(places)
        for part, to in enumerate(places):
            inputs = source[part * size : (part + 1) * size, pl.ds(start, half)].astype(f32)
            squashed = jnp.tanh(gain * inputs)
            squash[to : to + size, :] = squashed
            slope[to : to + size, :] = (1.0 - squashed * squashed) * inputs
    mirrored = jnp.concatenate([far[rows // 2 :, :], far[: rows // 2, :]], axis=0)

    def place(cols, value):
        for x in range(2):
            for y in range(2):
                row = (x * 4 + y) * block
                d_own[x, y, :, cols] = value[row : row + block]
                row = (x * 4 + 2 + y) * block
                d_other[x, y, :, cols] = value[row : row + block]

    place(slice(half, half + LANES), tail[...])
    step = 512
    for at in range(0, half, step):
        cols = slice(at, at + step)
        part = jnp.dot(
            near[...],
            w_in[:, pl.ds(pl.multiple_of(start + at, step), step)],
            preferred_element_type=f32,
        )
        for index, held in enumerate(w_far):
            deep = held.shape[0]
            part = part + jnp.dot(
                mirrored[:, index * deep : (index + 1) * deep],
                held[:, cols],
                preferred_element_type=f32,
            )
        short = part.astype(bf16)
        place(cols, short)
        part = short.astype(f32)
        sums[0:1, cols] = jnp.sum(part, axis=0, keepdims=True)
        sums[1:2, cols] = jnp.sum(part * squash[:, cols], axis=0, keepdims=True)
        sums[2:3, cols] = jnp.sum(part * slope[:, cols], axis=0, keepdims=True)
        sums[3:8, cols] = jnp.zeros((5, step), f32)


def down_kernel(count, *refs):
    acts = refs[:count]
    scaled = refs[count : 2 * count]
    out = refs[2 * count]
    left, right = refs[2 * count + 1 :]
    half = acts[0].shape[0] // 2
    total = None
    for batch in range(2):
        for k in range(count):
            left[k * half : (k + 1) * half, :] = acts[k][batch * half : (batch + 1) * half, :]
            right[k * half : (k + 1) * half, :] = scaled[k][batch * half : (batch + 1) * half, :]
        term = lax.dot_general(
            left[...], right[...], (((0,), (0,)), ((), ())), preferred_element_type=f32
        )
        term = term.astype(bf16).astype(f32)
        total = term if total is None else total + term
    out[...] = total.astype(bf16)


def whole():
    return pl.BlockSpec(memory_space=pltpu.VMEM)


def scalar():
    return pl.BlockSpec(memory_space=pltpu.SMEM)


def dense_shards(tokens, cotangent, expert_ids, gate_probs, alpha, gamma, beta, w_in, w_down):
    experts = lax.axis_size("expert")
    planes = experts // 4
    block = tokens.shape[1]
    width = tokens.shape[2]
    hidden = w_down.shape[1]
    rows = 8 * block
    me = lax.axis_index("expert")

    def go_x(v):
        return lax.ppermute(v, "dp", [(0, 1), (1, 0)])

    def go_y(v):
        return lax.ppermute(v, "expert", [(e, e ^ 2) for e in range(experts)])

    def go_core(v):
        return lax.ppermute(v, "expert", [(e, e ^ 1) for e in range(experts)])

    def go_z(v):
        return lax.ppermute(v, "expert", [(e, (e + 4) % experts) for e in range(experts)])

    lanes = jnp.arange(LANES, dtype=jnp.int32)
    picks = expert_ids[0][:, :, None] == lanes[None, None, :]
    gates = jnp.sum(jnp.where(picks, gate_probs[0].astype(f32)[:, :, None], 0.0), axis=1)
    own = jnp.concatenate([tokens[0], cotangent[0], gates.astype(bf16)], axis=1)

    flat_in = w_in[0].reshape(2 * hidden, width)
    flat_down = w_down[0]
    gamma_row = gamma.reshape(1, width)
    beta_row = beta.reshape(1, width)
    mine = me.reshape(1).astype(jnp.int32)
    half = width // 2
    side = lax.axis_index("dp").astype(jnp.int32)
    w_send = lax.dynamic_slice_in_dim(flat_in, (1 - side) * half, half, axis=1)

    segments = tuple(
        tuple((x * 4 + core * 2 + y) * block for x in range(2))
        for core in range(2)
        for y in range(2)
    )
    params = pltpu.CompilerParams(vmem_limit_bytes=40 << 20)

    def first_half(arrays):
        return pl.pallas_call(
            functools.partial(rows_kernel, segments, width, hidden),
            out_shape=(
                jax.ShapeDtypeStruct((rows, 2 * hidden), bf16),
                jax.ShapeDtypeStruct((rows, hidden), bf16),
                jax.ShapeDtypeStruct((rows, width), bf16),
                jax.ShapeDtypeStruct((rows, LANES), bf16),
            ),
            in_specs=[whole()] * 8 + [scalar(), scalar()],
            out_specs=(whole(),) * 4,
            scratch_shapes=[
                pltpu.VMEM((rows, width), bf16),
                pltpu.VMEM((rows, width), bf16),
                pltpu.VMEM((rows, LANES), f32),
            ],
            compiler_params=params,
            name="rows",
        )(*arrays, flat_in, flat_down, gamma_row, beta_row, alpha, mine)

    def second_half(arrays, near, far, w_far, tail):
        return pl.pallas_call(
            functools.partial(grad_kernel, segments, half, len(w_far)),
            out_shape=(
                jax.ShapeDtypeStruct((2, 2, block, half + LANES), bf16),
                jax.ShapeDtypeStruct((2, 2, block, half + LANES), bf16),
                jax.ShapeDtypeStruct((8, half), f32),
            ),
            in_specs=[whole()] * (8 + len(w_far)) + [scalar(), scalar()],
            out_specs=(whole(),) * 3,
            scratch_shapes=[
                pltpu.VMEM((rows, half), f32),
                pltpu.VMEM((rows, half), f32),
            ],
            compiler_params=params,
            name="grads",
        )(*arrays, near, far, flat_in, *w_far, tail, alpha, side.reshape(1))

    def settle(d_own, d_other):
        got = go_core(d_other)
        send = add16(d_own[:, 1], got[:, 1])
        keep = d_own[:, 0].astype(f32) + got[:, 0].astype(f32)
        return keep + go_y(send).astype(f32)

    fence = lax.optimization_barrier
    own = jnp.concatenate([own, go_x(own)], axis=0)
    parts = planes - 1
    deep = 2 * hidden // parts
    w_parts = [w_send[k * deep : (k + 1) * deep] for k in range(parts)]
    near, far, near_c, far_c, w_far = {0: own}, {}, {}, {}, []
    near[0], w_parts = fence((near[0], w_parts))
    first, other, acts, scaled, totals = {}, {}, {}, {}, []

    def rows_of(k):
        arrays = (near[k], far[k], near_c[k], far_c[k])
        grads, acts[k], scaled[k], tail = first_half(arrays)
        first[k] = (arrays, grads, tail)

    for k in range(planes):
        if k < parts:
            near[k + 1] = go_z(near[k])
        far[k] = go_y(near[k])
        if k < parts:
            w_far.append(go_x(w_parts[k]))
        near_c[k] = go_core(near[k])
        if k:
            far_c[k - 1] = go_core(far[k - 1])
            rows_of(k - 1)
        if k == parts:
            for j in range(k - 1):
                other[j] = go_x(first[j][1])
        near, far, near_c, far_c, w_far, first, other = fence(
            (near, far, near_c, far_c, w_far, first, other)
        )
    last = planes - 1
    far_c[last] = go_core(far[last])
    other[last - 1] = go_x(first[last - 1][1])
    rows_of(last)
    first, other = fence((first, other))
    other[last] = go_x(first[last][1])

    carry = None
    order = list(range(planes))
    for k in order[1:] + order[:1]:
        arrays, grads, tail = first[k]
        d_own, d_other, sums = second_half(arrays, grads, other[k], w_far, tail)
        totals.append(sums)
        value = settle(d_own, d_other)
        if carry is not None:
            value = value + go_z(carry).astype(f32)
        carry = value.astype(bf16)
    acts = [acts[k] for k in order]
    scaled = [scaled[k] for k in order]
    crossed = go_x(carry[1]).astype(f32)
    left = jnp.where(side == 0, value[0, :, :half], crossed[:, :half])
    right = jnp.where(side == 0, crossed[:, :half], value[0, :, :half])
    grad_normed = jnp.concatenate([left, right], axis=1)
    row_grads = value[0, :, half:] + crossed[:, half:]

    sums = sum(totals[1:], totals[0])
    for go in (go_core, go_y):
        sums = sums + go(sums)
    hop = 4
    while hop < experts:
        sums = sums + lax.ppermute(sums, "expert", [(e, e ^ hop) for e in range(experts)])
        hop *= 2
    crossed = go_x(sums)
    sums = jnp.concatenate(
        [jnp.where(side == 0, sums, crossed), jnp.where(side == 0, crossed, sums)], axis=1
    )

    grad_down = pl.pallas_call(
        functools.partial(down_kernel, planes),
        out_shape=jax.ShapeDtypeStruct((hidden, width), bf16),
        in_specs=[whole()] * (2 * planes),
        out_specs=whole(),
        scratch_shapes=[
            pltpu.VMEM((planes * rows // 2, hidden), bf16),
            pltpu.VMEM((planes * rows // 2, width), bf16),
        ],
        compiler_params=pltpu.CompilerParams(vmem_limit_bytes=40 << 20),
        name="down",
    )(*acts, *scaled)

    inputs = tokens[0].astype(f32)
    squashed = jnp.tanh(alpha[0] * inputs)
    pre_grad = grad_normed * gamma * (1.0 - squashed * squashed)
    grad_tokens = (cotangent[0].astype(f32) + alpha[0] * pre_grad).astype(bf16)
    grad_probs = jnp.sum(jnp.where(picks, row_grads[:, None, :], 0.0), axis=2).astype(bf16)
    grad_beta = sums[0]
    grad_gamma = sums[1]
    grad_alpha = jnp.sum(sums[2] * gamma).reshape(1)
    return (
        grad_tokens[None],
        grad_probs[None],
        grad_down[None],
        grad_gamma,
        grad_beta,
        grad_alpha,
    )


def slot_layout(ids_local, expert_count, capacity):
    token_count, top_count = ids_local.shape
    labels = jnp.arange(expert_count, dtype=jnp.int32)
    onehot = (ids_local[:, :, None] == labels[None, None, :]).astype(jnp.int32)
    picks = jnp.sum(onehot, axis=1)
    order = jnp.arange(token_count, dtype=jnp.int32)
    earlier = (order[None, :] < order[:, None]).astype(f32)
    before = jnp.dot(earlier, picks.astype(f32), precision=lax.Precision.HIGHEST)
    slots = jnp.sum(onehot * before.astype(jnp.int32)[:, None, :], axis=2)
    position = ids_local * capacity + slots
    pairs = jnp.arange(token_count * top_count, dtype=jnp.int32)
    table = jnp.full((expert_count * capacity,), token_count * top_count, jnp.int32)
    table = table.at[position.reshape(-1)].set(pairs)
    return (position, table)


def routed_shards(tokens, cotangent, expert_ids, gate_probs, alpha, gamma, beta, w_in, w_down):
    expert_count = lax.axis_size("expert")
    token_count = tokens.shape[1]
    top_count = expert_ids.shape[2]
    width = tokens.shape[2]
    capacity = 3 * token_count * top_count // (2 * expert_count)
    rows_total = expert_count * capacity
    inputs = tokens[0].astype(jnp.float32)
    squashed = jnp.tanh(alpha[0] * inputs)
    normed = (gamma * squashed + beta).astype(jnp.bfloat16)
    position, table = slot_layout(expert_ids[0], expert_count, capacity)
    source_token = table // top_count
    zero_row = jnp.zeros((1, width), jnp.bfloat16)
    normed_pad = jnp.concatenate([normed, zero_row], axis=0)
    cot_pad = jnp.concatenate([cotangent[0], zero_row], axis=0)
    prob_pad = jnp.concatenate([gate_probs[0].reshape(-1), jnp.zeros((1,), jnp.bfloat16)], axis=0)
    send_rows = normed_pad[source_token].reshape(expert_count, capacity, width)
    send_cot = cot_pad[source_token].reshape(expert_count, capacity, width)
    send_prob = prob_pad[table].reshape(expert_count, capacity)

    def swap(value):
        return lax.all_to_all(value, "expert", split_axis=0, concat_axis=0, tiled=True)

    in_rows = swap(send_rows).reshape(rows_total, width)
    cot_rows = swap(send_cot).reshape(rows_total, width)
    prob_rows = swap(send_prob).reshape(rows_total).astype(jnp.float32)
    gate_up = lax.all_gather(w_in, "dp", axis=2, tiled=True)
    w_lower = lax.all_gather(w_down, "dp", axis=1, tiled=True)[0]
    w_gate = gate_up[0, 0]
    w_upper = gate_up[0, 1]
    gate_pre = contract_width(in_rows, w_gate)
    up_value = contract_width(in_rows, w_upper)
    sigma = jax.nn.sigmoid(gate_pre)
    activation = (gate_pre * sigma * up_value).astype(jnp.bfloat16)
    back = contract_width(cot_rows, w_lower)
    weight_row = residual_scale * prob_rows
    scaled_cot = (weight_row[:, None] * cot_rows.astype(jnp.float32)).astype(jnp.bfloat16)
    row_grad = residual_scale * jnp.sum(activation.astype(jnp.float32) * back, axis=1)
    d_act = weight_row[:, None] * back
    d_gate = (d_act * up_value * sigma * (1.0 + gate_pre * (1.0 - sigma))).astype(jnp.bfloat16)
    d_up = (d_act * gate_pre * sigma).astype(jnp.bfloat16)
    d_rows = (
        jnp.dot(d_gate, w_gate, preferred_element_type=jnp.float32)
        + jnp.dot(d_up, w_upper, preferred_element_type=jnp.float32)
    ).astype(jnp.bfloat16)
    back_rows = swap(d_rows.reshape(expert_count, capacity, width))
    back_probs = swap(row_grad.astype(jnp.bfloat16).reshape(expert_count, capacity))
    partial_grad = lax.dot_general(
        activation, scaled_cot, (((0,), (0,)), ((), ())), preferred_element_type=jnp.float32
    )
    grad_down = lax.psum_scatter(
        partial_grad[None].astype(jnp.bfloat16), "dp", scatter_dimension=1, tiled=True
    )
    picked = back_rows.reshape(rows_total, width)[position]
    grad_normed = jnp.sum(picked.astype(jnp.float32), axis=1)
    grad_probs = back_probs.reshape(rows_total)[position]
    gamma_part = jnp.sum(grad_normed * squashed, axis=0)
    beta_part = jnp.sum(grad_normed, axis=0)
    pre_grad = grad_normed * gamma * (1.0 - squashed * squashed)
    alpha_part = jnp.sum(pre_grad * inputs).reshape(1)
    grad_gamma, grad_beta, grad_alpha = lax.psum(
        (gamma_part, beta_part, alpha_part), ("expert", "dp")
    )
    grad_tokens = (cotangent[0].astype(jnp.float32) + alpha[0] * pre_grad).astype(jnp.bfloat16)
    return (grad_tokens[None], grad_probs[None], grad_down, grad_gamma, grad_beta, grad_alpha)


def shards(*arrays):
    experts = lax.axis_size("expert")
    top_count = arrays[2].shape[2]
    dense = (
        lax.axis_size("dp") == 2
        and experts % 4 == 0
        and (experts & (experts - 1)) == 0
        and experts <= LANES
        and 2 * top_count >= experts
        and 2 * arrays[8].shape[1] % (16 * (experts // 4 - 1)) == 0
    )
    return (dense_shards if dense else routed_shards)(*arrays)


def solution(mesh):
    placed = (
        P("dp", "expert", None),
        P("dp", "expert", None),
        P("dp", "expert", None),
        P("dp", "expert", None),
        P(),
        P(),
        P(),
        P("expert", None, "dp", None),
        P("expert", "dp", None),
    )
    return jax.shard_map(
        shards,
        mesh=mesh,
        in_specs=placed,
        out_specs=(
            P("dp", "expert", None),
            P("dp", "expert", None),
            P("expert", "dp", None),
            P(),
            P(),
            P(),
        ),
        check_vma=False,
    )
```

```python
import functools
import jax
import jax.numpy as jnp
from jax import lax
from jax.experimental import pallas as pl
from jax.experimental.pallas import tpu as pltpu
from jax.sharding import PartitionSpec as P

residual_scale = 0.7071
LANES = 128
f32 = jnp.float32
bf16 = jnp.bfloat16


def contract_width(left, right):
    return lax.dot_general(
        left, right, (((1,), (1,)), ((), ())), preferred_element_type=f32
    )


def add16(left, right):
    return (left.astype(f32) + right.astype(f32)).astype(bf16)


def rows_kernel(segments, width, hidden, *refs):
    count = len(segments)
    blocks = refs[:count]
    (w_in, w_down, gamma, beta, alpha, expert) = refs[count : count + 6]
    (grads_out, kept_out, tail_out) = refs[count + 6 : count + 9]
    (normed, cot, weight, kept, sems) = refs[count + 9 :]
    rows = normed.shape[0]
    gain = alpha[0]
    mine = expert[0]
    gamma_row = gamma[...]
    beta_row = beta[...]
    for source, places in zip(blocks, segments):
        size = source.shape[0] // len(places)
        for part, to in enumerate(places):
            here, there = slice(part * size, (part + 1) * size), slice(to, to + size)
            squashed = jnp.tanh(gain * source[here, 0:width].astype(f32))
            normed[there, :] = (gamma_row * squashed + beta_row).astype(bf16)
            rows_cot = source[here, width : 2 * width]
            cot[there, :] = rows_cot
            gates = source[here, 2 * width :].astype(f32)
            lane = lax.broadcasted_iota(jnp.int32, gates.shape, 1)
            own = jnp.sum(jnp.where(lane == mine, gates, 0.0), axis=1, keepdims=True)
            own = residual_scale * own
            weight[there, :] = jnp.broadcast_to(own, (size, LANES))
            kept[there, hidden:] = (own * rows_cot.astype(f32)).astype(bf16)
    wide = slice(hidden, hidden + width)
    save_cot = pltpu.make_async_copy(kept.at[:, wide], kept_out.at[:, wide], sems.at[0])
    save_cot.start()
    pre = contract_width(normed[...], w_in[...])
    back = contract_width(cot[...], w_down[...])
    gate_pre = pre[:, :hidden]
    up_value = pre[:, hidden:]
    sigma = jax.nn.sigmoid(gate_pre)
    silu = gate_pre * sigma
    activation = (silu * up_value).astype(bf16)
    kept[:, :hidden] = activation
    save_act = pltpu.make_async_copy(
        kept.at[:, :hidden], kept_out.at[:, :hidden], sems.at[1]
    )
    save_act.start()
    row_grad = residual_scale * jnp.sum(activation.astype(f32) * back, axis=1, keepdims=True)
    d_act = weight[:, 0:1] * back
    d_gate = d_act * up_value * sigma * (1.0 + gate_pre * (1.0 - sigma))
    grads_out[:, :hidden] = d_gate.astype(bf16)
    grads_out[:, hidden:] = (d_act * gate_pre * sigma).astype(bf16)
    lane = lax.broadcasted_iota(jnp.int32, (rows, LANES), 1)
    tail_out[...] = jnp.where(lane == mine, row_grad, 0.0).astype(bf16)
    save_cot.wait()
    save_act.wait()


def grad_kernel(segments, half, parts, *refs):
    count = len(segments)
    blocks = refs[:count]
    (near, far, w_in, *w_far) = refs[count : count + 3 + parts]
    (tail, alpha, side, d_own, d_other, sums, squash, slope) = refs[count + 3 + parts :]
    rows = near.shape[0]
    block = rows // 8
    gain = alpha[0]
    start = pl.multiple_of(side[0] * half, half)
    for source, places in zip(blocks, segments):
        size = source.shape[0] // len(places)
        for part, to in enumerate(places):
            inputs = source[part * size : (part + 1) * size, pl.ds(start, half)].astype(f32)
            squashed = jnp.tanh(gain * inputs)
            squash[to : to + size, :] = squashed
            slope[to : to + size, :] = (1.0 - squashed * squashed) * inputs
    mirrored = jnp.concatenate([far[rows // 2 :, :], far[: rows // 2, :]], axis=0)

    def place(cols, value):
        for x in range(2):
            for y in range(2):
                row = (x * 4 + y) * block
                d_own[x, y, :, cols] = value[row : row + block]
                row = (x * 4 + 2 + y) * block
                d_other[x, y, :, cols] = value[row : row + block]

    place(slice(half, half + LANES), tail[...])
    at = 0
    for held in w_far:
        step = held.shape[1]
        cols = slice(at, at + step)
        part = jnp.dot(
            near[...],
            w_in[:, pl.ds(pl.multiple_of(start + at, LANES), step)],
            preferred_element_type=f32,
        )
        part = part + jnp.dot(mirrored, held[...], preferred_element_type=f32)
        short = part.astype(bf16)
        place(cols, short)
        part = short.astype(f32)
        sums[0:1, cols] = jnp.sum(part, axis=0, keepdims=True)
        sums[1:2, cols] = jnp.sum(part * squash[:, cols], axis=0, keepdims=True)
        sums[2:3, cols] = jnp.sum(part * slope[:, cols], axis=0, keepdims=True)
        sums[3:8, cols] = jnp.zeros((5, step), f32)
        at += step


def pack_kernel(tokens, cotangent, ids, probs, out):
    width = tokens.shape[1]
    top, block = ids.shape
    names = ids[...]
    shares = probs[...].astype(f32)
    label = lax.broadcasted_iota(jnp.int32, (LANES, block), 0)
    table = jnp.zeros((LANES, block), f32)
    for k in range(top):
        table = table + jnp.where(label == names[k : k + 1, :], shares[k : k + 1, :], 0.0)
    row = lax.broadcasted_iota(jnp.int32, (block, block), 0)
    column = lax.broadcasted_iota(jnp.int32, (block, block), 1)
    unit = jnp.where(row == column, 1.0, 0.0).astype(bf16)
    out[:, 2 * width :] = contract_width(unit, table.astype(bf16)).astype(bf16)
    out[:, :width] = tokens[...]
    out[:, width : 2 * width] = cotangent[...]


def down_kernel(count, hidden, *refs):
    kept = refs[:count]
    out, held, sems = refs[count:]
    half = kept[0].shape[0] // 2
    copies = []
    for batch in range(2):
        for k in range(count):
            copy = pltpu.make_async_copy(
                kept[k].at[batch * half : (batch + 1) * half, :],
                held.at[batch, k * half : (k + 1) * half, :],
                sems.at[batch, k],
            )
            copy.start()
            copies.append(copy)
    total = None
    for batch in range(2):
        for copy in copies[batch * count : (batch + 1) * count]:
            copy.wait()
        term = lax.dot_general(
            held[batch, :, :hidden],
            held[batch, :, hidden:],
            (((0,), (0,)), ((), ())),
            preferred_element_type=f32,
        )
        term = term.astype(bf16).astype(f32)
        total = term if total is None else total + term
    out[...] = total.astype(bf16)


def whole():
    return pl.BlockSpec(memory_space=pltpu.VMEM)


def scalar():
    return pl.BlockSpec(memory_space=pltpu.SMEM)


def dense_shards(tokens, cotangent, expert_ids, gate_probs, alpha, gamma, beta, w_in, w_down):
    experts = lax.axis_size("expert")
    planes = experts // 4
    block = tokens.shape[1]
    width = tokens.shape[2]
    hidden = w_down.shape[1]
    rows = 8 * block
    me = lax.axis_index("expert")

    def go_x(v):
        return lax.ppermute(v, "dp", [(0, 1), (1, 0)])

    def go_y(v):
        return lax.ppermute(v, "expert", [(e, e ^ 2) for e in range(experts)])

    def go_core(v):
        return lax.ppermute(v, "expert", [(e, e ^ 1) for e in range(experts)])

    def go_z(v):
        return lax.ppermute(v, "expert", [(e, (e + 4) % experts) for e in range(experts)])

    def go_jump(v, by):
        return lax.ppermute(v, "expert", [(e, e ^ by) for e in range(experts)])

    lanes = jnp.arange(LANES, dtype=jnp.int32)
    picks = expert_ids[0][:, :, None] == lanes[None, None, :]
    own = pl.pallas_call(
        pack_kernel,
        out_shape=jax.ShapeDtypeStruct((block, 2 * width + LANES), bf16),
        in_specs=[whole()] * 4,
        out_specs=whole(),
        name="pack",
    )(tokens[0], cotangent[0], expert_ids[0].T, gate_probs[0].T)

    flat_in = w_in[0].reshape(2 * hidden, width)
    flat_down = w_down[0]
    gamma_row = gamma.reshape(1, width)
    beta_row = beta.reshape(1, width)
    mine = me.reshape(1).astype(jnp.int32)
    half = width // 2
    side = lax.axis_index("dp").astype(jnp.int32)
    w_send = lax.dynamic_slice_in_dim(flat_in, (1 - side) * half, half, axis=1)

    segments = tuple(
        tuple((x * 4 + core * 2 + y) * block for x in range(2))
        for core in range(2)
        for y in range(2)
    )
    params = pltpu.CompilerParams(vmem_limit_bytes=14 << 20)

    def first_half(arrays):
        return pl.pallas_call(
            functools.partial(rows_kernel, segments, width, hidden),
            out_shape=(
                jax.ShapeDtypeStruct((rows, 2 * hidden), bf16),
                jax.ShapeDtypeStruct((rows, hidden + width), bf16),
                jax.ShapeDtypeStruct((rows, LANES), bf16),
            ),
            in_specs=[whole()] * 8 + [scalar(), scalar()],
            out_specs=(whole(), pl.BlockSpec(memory_space=pl.ANY), whole()),
            scratch_shapes=[
                pltpu.VMEM((rows, width), bf16),
                pltpu.VMEM((rows, width), bf16),
                pltpu.VMEM((rows, LANES), f32),
                pltpu.VMEM((rows, hidden + width), bf16),
                pltpu.SemaphoreType.DMA((2,)),
            ],
            compiler_params=params,
            name="rows",
        )(*arrays, flat_in, flat_down, gamma_row, beta_row, alpha, mine)

    def second_half(arrays, near, far, w_far, tail):
        return pl.pallas_call(
            functools.partial(grad_kernel, segments, half, len(w_far)),
            out_shape=(
                jax.ShapeDtypeStruct((2, 2, block, half + LANES), bf16),
                jax.ShapeDtypeStruct((2, 2, block, half + LANES), bf16),
                jax.ShapeDtypeStruct((8, half), f32),
            ),
            in_specs=[whole()] * (8 + len(w_far)) + [scalar(), scalar()],
            out_specs=(whole(),) * 3,
            scratch_shapes=[
                pltpu.VMEM((rows, half), f32),
                pltpu.VMEM((rows, half), f32),
            ],
            compiler_params=params,
            name="grads",
        )(*arrays, near, far, flat_in, *w_far, tail, alpha, side.reshape(1))

    fence = lax.optimization_barrier
    own = jnp.concatenate([own, go_x(own)], axis=0)
    most = 3 * half // 8
    w_parts = [w_send[:, k * most : min((k + 1) * most, half)] for k in range(3)]
    near, far, near_c, far_c, w_far = {0: own}, {}, {}, {}, []
    state = {"near": near, "far": far, "near_c": near_c, "far_c": far_c, "w": w_far}
    grads, kept, tails, other = {}, {}, {}, {}
    state.update(grads=grads, other=other)
    d_own, d_got, totals, sent, value = {}, {}, {}, {}, {}
    state.update(d_own=d_own, d_got=d_got, totals=totals, sent=sent, value=value)
    near[0], w_parts = fence((near[0], w_parts))

    def make_down(held):
        return pl.pallas_call(
            functools.partial(down_kernel, planes, hidden),
            out_shape=jax.ShapeDtypeStruct((hidden, width), bf16),
            in_specs=[pl.BlockSpec(memory_space=pl.ANY)] * planes,
            out_specs=whole(),
            scratch_shapes=[
                pltpu.VMEM((2, planes * rows // 2, hidden + width), bf16),
                pltpu.SemaphoreType.DMA((2, planes)),
            ],
            compiler_params=pltpu.CompilerParams(vmem_limit_bytes=20 << 20),
            name="down",
        )(*held)

    def step():
        new = fence(state)
        for name, held in state.items():
            if isinstance(held, dict):
                held.update(new[name])
            else:
                held[:] = new[name]

    def rows_of(k):
        arrays = (near[k], far[k], near_c[k], far_c[k])
        grads[k], kept[k], tails[k] = first_half(arrays)

    def grads_of(k):
        arrays = (near[k], far[k], near_c[k], far_c[k])
        d_own[k], moved, totals[k] = second_half(arrays, grads[k], other[k], w_far, tails[k])
        d_got[k] = go_core(moved)

    def send_y(k):
        sent[k] = go_y(add16(d_own[k][:, 1], d_got[k][:, 1]))

    def total_of(k):
        kept = d_own[k][:, 0].astype(f32) + d_got[k][:, 0].astype(f32)
        return kept + sent[k].astype(f32)

    def hop(k):
        carried = total_of(k)
        if k > 1:
            carried = carried + value[k].astype(f32)
        value[(k + 1) % planes] = go_z(carried.astype(bf16))

    for k in range(3):
        w_far.append(go_x(w_parts[k]))
        near[k + 1] = go_z(near[k])
        far[k] = go_y(near[k])
        near_c[k] = go_core(near[k])
        if k:
            far_c[k - 1] = go_core(far[k - 1])
            rows_of(k - 1)
        if k == 2:
            other[0] = go_x(grads[0])
        step()
    other[1] = go_x(grads[1])
    far[3] = go_y(near[3])
    near_c[3] = go_core(near[3])
    far_c[2] = go_core(far[2])
    rows_of(2)
    grads_of(0)
    step()
    other[2] = go_x(grads[2])
    far_c[3] = go_core(far[3])
    rows_of(3)
    grads_of(1)
    step()
    other[3] = go_x(grads[3])
    send_y(1)
    grads_of(2)
    send_y(0)
    step()
    send_y(2)
    hop(1)
    grads_of(3)
    step()
    pool = [sum(totals[k] for k in range(1, planes)) + totals[0]]
    state["pool"] = pool
    send_y(3)
    hop(2)
    pool[0] = pool[0] + go_core(pool[0])
    step()
    hop(3)
    pool[0] = pool[0] + go_y(pool[0])
    grad_down = make_down([kept[k] for k in range(planes)])
    state["down"] = [grad_down]
    step()
    grad_down = state["down"][0]
    pool[0] = pool[0] + go_jump(pool[0], 4)
    sums = pool[0]
    final = total_of(0) + value[0].astype(f32)
    crossed = go_x(final[1].astype(bf16)).astype(f32)
    left = jnp.where(side == 0, final[0, :, :half], crossed[:, :half])
    right = jnp.where(side == 0, crossed[:, :half], final[0, :, :half])
    grad_normed = jnp.concatenate([left, right], axis=1)
    row_grads = final[0, :, half:] + crossed[:, half:]
    sums = sums + go_jump(sums, 8)
    crossed = go_x(sums)
    sums = jnp.concatenate(
        [jnp.where(side == 0, sums, crossed), jnp.where(side == 0, crossed, sums)], axis=1
    )

    inputs = tokens[0].astype(f32)
    squashed = jnp.tanh(alpha[0] * inputs)
    pre_grad = grad_normed * gamma * (1.0 - squashed * squashed)
    grad_tokens = (cotangent[0].astype(f32) + alpha[0] * pre_grad).astype(bf16)
    grad_probs = jnp.sum(jnp.where(picks, row_grads[:, None, :], 0.0), axis=2).astype(bf16)
    grad_beta = sums[0]
    grad_gamma = sums[1]
    grad_alpha = jnp.sum(sums[2] * gamma).reshape(1)
    return (
        grad_tokens[None],
        grad_probs[None],
        grad_down[None],
        grad_gamma,
        grad_beta,
        grad_alpha,
    )


def slot_layout(ids_local, expert_count, capacity):
    token_count, top_count = ids_local.shape
    labels = jnp.arange(expert_count, dtype=jnp.int32)
    onehot = (ids_local[:, :, None] == labels[None, None, :]).astype(jnp.int32)
    picks = jnp.sum(onehot, axis=1)
    order = jnp.arange(token_count, dtype=jnp.int32)
    earlier = (order[None, :] < order[:, None]).astype(f32)
    before = jnp.dot(earlier, picks.astype(f32), precision=lax.Precision.HIGHEST)
    slots = jnp.sum(onehot * before.astype(jnp.int32)[:, None, :], axis=2)
    position = ids_local * capacity + slots
    pairs = jnp.arange(token_count * top_count, dtype=jnp.int32)
    table = jnp.full((expert_count * capacity,), token_count * top_count, jnp.int32)
    table = table.at[position.reshape(-1)].set(pairs)
    return (position, table)


def routed_shards(tokens, cotangent, expert_ids, gate_probs, alpha, gamma, beta, w_in, w_down):
    expert_count = lax.axis_size("expert")
    token_count = tokens.shape[1]
    top_count = expert_ids.shape[2]
    width = tokens.shape[2]
    capacity = 3 * token_count * top_count // (2 * expert_count)
    rows_total = expert_count * capacity
    inputs = tokens[0].astype(jnp.float32)
    squashed = jnp.tanh(alpha[0] * inputs)
    normed = (gamma * squashed + beta).astype(jnp.bfloat16)
    position, table = slot_layout(expert_ids[0], expert_count, capacity)
    source_token = table // top_count
    zero_row = jnp.zeros((1, width), jnp.bfloat16)
    normed_pad = jnp.concatenate([normed, zero_row], axis=0)
    cot_pad = jnp.concatenate([cotangent[0], zero_row], axis=0)
    prob_pad = jnp.concatenate([gate_probs[0].reshape(-1), jnp.zeros((1,), jnp.bfloat16)], axis=0)
    send_rows = normed_pad[source_token].reshape(expert_count, capacity, width)
    send_cot = cot_pad[source_token].reshape(expert_count, capacity, width)
    send_prob = prob_pad[table].reshape(expert_count, capacity)

    def swap(value):
        return lax.all_to_all(value, "expert", split_axis=0, concat_axis=0, tiled=True)

    in_rows = swap(send_rows).reshape(rows_total, width)
    cot_rows = swap(send_cot).reshape(rows_total, width)
    prob_rows = swap(send_prob).reshape(rows_total).astype(jnp.float32)
    gate_up = lax.all_gather(w_in, "dp", axis=2, tiled=True)
    w_lower = lax.all_gather(w_down, "dp", axis=1, tiled=True)[0]
    w_gate = gate_up[0, 0]
    w_upper = gate_up[0, 1]
    gate_pre = contract_width(in_rows, w_gate)
    up_value = contract_width(in_rows, w_upper)
    sigma = jax.nn.sigmoid(gate_pre)
    activation = (gate_pre * sigma * up_value).astype(jnp.bfloat16)
    back = contract_width(cot_rows, w_lower)
    weight_row = residual_scale * prob_rows
    scaled_cot = (weight_row[:, None] * cot_rows.astype(jnp.float32)).astype(jnp.bfloat16)
    row_grad = residual_scale * jnp.sum(activation.astype(jnp.float32) * back, axis=1)
    d_act = weight_row[:, None] * back
    d_gate = (d_act * up_value * sigma * (1.0 + gate_pre * (1.0 - sigma))).astype(jnp.bfloat16)
    d_up = (d_act * gate_pre * sigma).astype(jnp.bfloat16)
    d_rows = (
        jnp.dot(d_gate, w_gate, preferred_element_type=jnp.float32)
        + jnp.dot(d_up, w_upper, preferred_element_type=jnp.float32)
    ).astype(jnp.bfloat16)
    back_rows = swap(d_rows.reshape(expert_count, capacity, width))
    back_probs = swap(row_grad.astype(jnp.bfloat16).reshape(expert_count, capacity))
    partial_grad = lax.dot_general(
        activation, scaled_cot, (((0,), (0,)), ((), ())), preferred_element_type=jnp.float32
    )
    grad_down = lax.psum_scatter(
        partial_grad[None].astype(jnp.bfloat16), "dp", scatter_dimension=1, tiled=True
    )
    picked = back_rows.reshape(rows_total, width)[position]
    grad_normed = jnp.sum(picked.astype(jnp.float32), axis=1)
    grad_probs = back_probs.reshape(rows_total)[position]
    gamma_part = jnp.sum(grad_normed * squashed, axis=0)
    beta_part = jnp.sum(grad_normed, axis=0)
    pre_grad = grad_normed * gamma * (1.0 - squashed * squashed)
    alpha_part = jnp.sum(pre_grad * inputs).reshape(1)
    grad_gamma, grad_beta, grad_alpha = lax.psum(
        (gamma_part, beta_part, alpha_part), ("expert", "dp")
    )
    grad_tokens = (cotangent[0].astype(jnp.float32) + alpha[0] * pre_grad).astype(jnp.bfloat16)
    return (grad_tokens[None], grad_probs[None], grad_down, grad_gamma, grad_beta, grad_alpha)


def shards(*arrays):
    experts = lax.axis_size("expert")
    top_count = arrays[2].shape[2]
    dense = (
        lax.axis_size("dp") == 2
        and experts == 16
        and 2 * top_count >= experts
        and arrays[0].shape[2] % 2048 == 0
    )
    return (dense_shards if dense else routed_shards)(*arrays)


def solution(mesh):
    placed = (
        P("dp", "expert", None),
        P("dp", "expert", None),
        P("dp", "expert", None),
        P("dp", "expert", None),
        P(),
        P(),
        P(),
        P("expert", None, "dp", None),
        P("expert", "dp", None),
    )
    return jax.shard_map(
        shards,
        mesh=mesh,
        in_specs=placed,
        out_specs=(
            P("dp", "expert", None),
            P("dp", "expert", None),
            P("expert", "dp", None),
            P(),
            P(),
            P(),
        ),
        check_vma=False,
    )
```

```python
import functools
import jax
import jax.numpy as jnp
from jax import lax
from jax.experimental import pallas as pl
from jax.experimental.pallas import tpu as pltpu
from jax.sharding import PartitionSpec as P

residual_scale = 0.7071
LANES = 128
f32 = jnp.float32
bf16 = jnp.bfloat16


def contract_width(left, right):
    return lax.dot_general(
        left, right, (((1,), (1,)), ((), ())), preferred_element_type=f32
    )


def add16(left, right):
    return (left.astype(f32) + right.astype(f32)).astype(bf16)


def rows_kernel(segments, width, hidden, *refs):
    count = len(segments)
    blocks = refs[:count]
    (w_in, w_down, gamma, beta, alpha, expert) = refs[count : count + 6]
    (grads_out, kept_out, tail_out) = refs[count + 6 : count + 9]
    (normed, cot, weight, kept, sems) = refs[count + 9 :]
    rows = normed.shape[0]
    gain = alpha[0]
    mine = expert[0]
    gamma_row = gamma[...]
    beta_row = beta[...]
    for source, places in zip(blocks, segments):
        size = source.shape[0] // len(places)
        for part, to in enumerate(places):
            here, there = slice(part * size, (part + 1) * size), slice(to, to + size)
            squashed = jnp.tanh(gain * source[here, 0:width].astype(f32))
            normed[there, :] = (gamma_row * squashed + beta_row).astype(bf16)
            rows_cot = source[here, width : 2 * width]
            cot[there, :] = rows_cot
            gates = source[here, 2 * width :].astype(f32)
            lane = lax.broadcasted_iota(jnp.int32, gates.shape, 1)
            own = jnp.sum(jnp.where(lane == mine, gates, 0.0), axis=1, keepdims=True)
            own = residual_scale * own
            weight[there, :] = jnp.broadcast_to(own, (size, LANES))
            kept[there, hidden:] = (own * rows_cot.astype(f32)).astype(bf16)
    wide = slice(hidden, hidden + width)
    save_cot = pltpu.make_async_copy(kept.at[:, wide], kept_out.at[:, wide], sems.at[0])
    save_cot.start()
    pre = contract_width(normed[...], w_in[...])
    back = contract_width(cot[...], w_down[...])
    gate_pre = pre[:, :hidden]
    up_value = pre[:, hidden:]
    sigma = jax.nn.sigmoid(gate_pre)
    silu = gate_pre * sigma
    activation = (silu * up_value).astype(bf16)
    kept[:, :hidden] = activation
    save_act = pltpu.make_async_copy(
        kept.at[:, :hidden], kept_out.at[:, :hidden], sems.at[1]
    )
    save_act.start()
    row_grad = residual_scale * jnp.sum(activation.astype(f32) * back, axis=1, keepdims=True)
    d_act = weight[:, 0:1] * back
    d_gate = d_act * up_value * sigma * (1.0 + gate_pre * (1.0 - sigma))
    grads_out[:, :hidden] = d_gate.astype(bf16)
    grads_out[:, hidden:] = (d_act * gate_pre * sigma).astype(bf16)
    lane = lax.broadcasted_iota(jnp.int32, (rows, LANES), 1)
    tail_out[...] = jnp.where(lane == mine, row_grad, 0.0).astype(bf16)
    save_cot.wait()
    save_act.wait()


def grad_kernel(segments, half, *refs):
    count = len(segments)
    blocks = refs[:count]
    (near, far, w_in, w_far, tail, alpha, side) = refs[count : count + 7]
    (d_own, d_other, sums, squash, slope) = refs[count + 7 :]
    rows = near.shape[0]
    block = rows // 8
    gain = alpha[0]
    start = pl.multiple_of(side[0] * half, half)
    for source, places in zip(blocks, segments):
        size = source.shape[0] // len(places)
        for part, to in enumerate(places):
            inputs = source[part * size : (part + 1) * size, pl.ds(start, half)].astype(f32)
            squashed = jnp.tanh(gain * inputs)
            squash[to : to + size, :] = squashed
            slope[to : to + size, :] = (1.0 - squashed * squashed) * inputs
    mirrored = jnp.concatenate([far[rows // 2 :, :], far[: rows // 2, :]], axis=0)

    def place(cols, value):
        for x in range(2):
            for y in range(2):
                row = (x * 4 + y) * block
                d_own[x, y, :, cols] = value[row : row + block]
                row = (x * 4 + 2 + y) * block
                d_other[x, y, :, cols] = value[row : row + block]

    place(slice(half, half + LANES), tail[...])
    step = 512
    for at in range(0, half, step):
        cols = slice(at, at + step)
        part = jnp.dot(
            near[...],
            w_in[:, pl.ds(pl.multiple_of(start + at, step), step)],
            preferred_element_type=f32,
        )
        part = part + jnp.dot(mirrored, w_far[:, cols], preferred_element_type=f32)
        short = part.astype(bf16)
        place(cols, short)
        part = short.astype(f32)
        sums[0:1, cols] = jnp.sum(part, axis=0, keepdims=True)
        sums[1:2, cols] = jnp.sum(part * squash[:, cols], axis=0, keepdims=True)
        sums[2:3, cols] = jnp.sum(part * slope[:, cols], axis=0, keepdims=True)
        sums[3:8, cols] = jnp.zeros((5, step), f32)


def pack_kernel(tokens, cotangent, ids, probs, out):
    width = tokens.shape[1]
    top, block = ids.shape
    names = ids[...]
    shares = probs[...].astype(f32)
    label = lax.broadcasted_iota(jnp.int32, (LANES, block), 0)
    table = jnp.zeros((LANES, block), f32)
    for k in range(top):
        table = table + jnp.where(label == names[k : k + 1, :], shares[k : k + 1, :], 0.0)
    row = lax.broadcasted_iota(jnp.int32, (block, block), 0)
    column = lax.broadcasted_iota(jnp.int32, (block, block), 1)
    unit = jnp.where(row == column, 1.0, 0.0).astype(bf16)
    out[:, 2 * width :] = contract_width(unit, table.astype(bf16)).astype(bf16)
    out[:, :width] = tokens[...]
    out[:, width : 2 * width] = cotangent[...]


def down_kernel(count, hidden, *refs):
    kept = refs[:count]
    out, held, sems = refs[count:]
    half = kept[0].shape[0] // 2
    copies = []
    for batch in range(2):
        for k in range(count):
            copy = pltpu.make_async_copy(
                kept[k].at[batch * half : (batch + 1) * half, :],
                held.at[batch, k * half : (k + 1) * half, :],
                sems.at[batch, k],
            )
            copy.start()
            copies.append(copy)
    total = None
    for batch in range(2):
        for copy in copies[batch * count : (batch + 1) * count]:
            copy.wait()
        term = lax.dot_general(
            held[batch, :, :hidden],
            held[batch, :, hidden:],
            (((0,), (0,)), ((), ())),
            preferred_element_type=f32,
        )
        term = term.astype(bf16).astype(f32)
        total = term if total is None else total + term
    out[...] = total.astype(bf16)


def whole():
    return pl.BlockSpec(memory_space=pltpu.VMEM)


def scalar():
    return pl.BlockSpec(memory_space=pltpu.SMEM)


def dense_shards(tokens, cotangent, expert_ids, gate_probs, alpha, gamma, beta, w_in, w_down):
    experts = lax.axis_size("expert")
    planes = experts // 4
    block = tokens.shape[1]
    width = tokens.shape[2]
    hidden = w_down.shape[1]
    rows = 8 * block
    me = lax.axis_index("expert")

    def go_x(v):
        return lax.ppermute(v, "dp", [(0, 1), (1, 0)])

    def go_y(v):
        return lax.ppermute(v, "expert", [(e, e ^ 2) for e in range(experts)])

    def go_core(v):
        return lax.ppermute(v, "expert", [(e, e ^ 1) for e in range(experts)])

    def go_z(v):
        return lax.ppermute(v, "expert", [(e, (e + 4) % experts) for e in range(experts)])

    def go_jump(v, by):
        return lax.ppermute(v, "expert", [(e, e ^ by) for e in range(experts)])

    def go_far(v, by):
        pairs = [
            (2 * e + x, 2 * (e ^ by) + 1 - x) for e in range(experts) for x in range(2)
        ]
        return lax.ppermute(v, ("expert", "dp"), pairs)

    lanes = jnp.arange(LANES, dtype=jnp.int32)
    picks = expert_ids[0][:, :, None] == lanes[None, None, :]
    own = pl.pallas_call(
        pack_kernel,
        out_shape=jax.ShapeDtypeStruct((block, 2 * width + LANES), bf16),
        in_specs=[whole()] * 4,
        out_specs=whole(),
        name="pack",
    )(tokens[0], cotangent[0], expert_ids[0].T, gate_probs[0].T)

    flat_in = w_in[0].reshape(2 * hidden, width)
    flat_down = w_down[0]
    gamma_row = gamma.reshape(1, width)
    beta_row = beta.reshape(1, width)
    mine = me.reshape(1).astype(jnp.int32)
    half = width // 2
    side = lax.axis_index("dp").astype(jnp.int32)
    w_send = lax.dynamic_slice_in_dim(flat_in, (1 - side) * half, half, axis=1)

    segments = tuple(
        tuple((x * 4 + core * 2 + y) * block for x in range(2))
        for core in range(2)
        for y in range(2)
    )
    params = pltpu.CompilerParams(vmem_limit_bytes=14 << 20)

    def first_half(arrays):
        return pl.pallas_call(
            functools.partial(rows_kernel, segments, width, hidden),
            out_shape=(
                jax.ShapeDtypeStruct((rows, 2 * hidden), bf16),
                jax.ShapeDtypeStruct((rows, hidden + width), bf16),
                jax.ShapeDtypeStruct((rows, LANES), bf16),
            ),
            in_specs=[whole()] * 8 + [scalar(), scalar()],
            out_specs=(whole(), pl.BlockSpec(memory_space=pl.ANY), whole()),
            scratch_shapes=[
                pltpu.VMEM((rows, width), bf16),
                pltpu.VMEM((rows, width), bf16),
                pltpu.VMEM((rows, LANES), f32),
                pltpu.VMEM((rows, hidden + width), bf16),
                pltpu.SemaphoreType.DMA((2,)),
            ],
            compiler_params=params,
            name="rows",
        )(*arrays, flat_in, flat_down, gamma_row, beta_row, alpha, mine)

    def second_half(arrays, near, far, w_far, tail):
        return pl.pallas_call(
            functools.partial(grad_kernel, segments, half),
            out_shape=(
                jax.ShapeDtypeStruct((2, 2, block, half + LANES), bf16),
                jax.ShapeDtypeStruct((2, 2, block, half + LANES), bf16),
                jax.ShapeDtypeStruct((8, half), f32),
            ),
            in_specs=[whole()] * 9 + [scalar(), scalar()],
            out_specs=(whole(),) * 3,
            scratch_shapes=[
                pltpu.VMEM((rows, half), f32),
                pltpu.VMEM((rows, half), f32),
            ],
            compiler_params=params,
            name="grads",
        )(*arrays, near, far, flat_in, w_far, tail, alpha, side.reshape(1))

    fence = lax.optimization_barrier
    own = jnp.concatenate([own, go_x(own)], axis=0)
    near, far, near_c, far_c, w_far = {0: own}, {}, {}, {}, {}
    state = {"near": near, "far": far, "near_c": near_c, "far_c": far_c, "w": w_far}
    grads, kept, tails, other = {}, {}, {}, {}
    state.update(grads=grads, other=other)
    d_own, d_got, totals, sent, value = {}, {}, {}, {}, {}
    state.update(d_own=d_own, d_got=d_got, totals=totals, sent=sent, value=value)
    near[0], w_send = fence((near[0], w_send))
    w_far[0] = go_x(w_send)

    def make_down(held):
        return pl.pallas_call(
            functools.partial(down_kernel, planes, hidden),
            out_shape=jax.ShapeDtypeStruct((hidden, width), bf16),
            in_specs=[pl.BlockSpec(memory_space=pl.ANY)] * planes,
            out_specs=whole(),
            scratch_shapes=[
                pltpu.VMEM((2, planes * rows // 2, hidden + width), bf16),
                pltpu.SemaphoreType.DMA((2, planes)),
            ],
            compiler_params=pltpu.CompilerParams(vmem_limit_bytes=20 << 20),
            name="down",
        )(*held)

    def step(*late):
        now = {
            name: {k: v for k, v in held.items() if (name, k) not in late}
            for name, held in state.items()
        }
        new = fence(now)
        for name, held in state.items():
            held.update(new[name])

    def rows_of(k):
        arrays = (near[k], far[k], near_c[k], far_c[k])
        grads[k], kept[k], tails[k] = first_half(arrays)

    def grads_of(k):
        arrays = (near[k], far[k], near_c[k], far_c[k])
        d_own[k], moved, totals[k] = second_half(arrays, grads[k], other[k], w_far[0], tails[k])
        d_got[k] = go_core(moved)

    def send_y(k):
        sent[k] = go_y(add16(d_own[k][:, 1], d_got[k][:, 1]))

    def total_of(k):
        kept = d_own[k][:, 0].astype(f32) + d_got[k][:, 0].astype(f32)
        return kept + sent[k].astype(f32)

    def hop(k):
        carried = total_of(k)
        if k > 1:
            carried = carried + value[k].astype(f32)
        value[(k + 1) % planes] = go_z(carried.astype(bf16))

    for k in range(3):
        near[k + 1] = go_z(near[k])
        far[k] = go_y(near[k])
        near_c[k] = go_core(near[k])
        if k:
            far_c[k - 1] = go_core(far[k - 1])
            rows_of(k - 1)
        if k == 2:
            other[0] = go_x(grads[0])
        step(*([("w", 0)] if k == 0 else []))
    other[1] = go_x(grads[1])
    far[3] = go_y(near[3])
    near_c[3] = go_core(near[3])
    far_c[2] = go_core(far[2])
    rows_of(2)
    grads_of(0)
    step()
    other[2] = go_x(grads[2])
    far_c[3] = go_core(far[3])
    rows_of(3)
    other[1], far_c[3] = fence((other[1], far_c[3]))
    grads_of(1)
    step(("other", 2))
    other[3] = go_x(grads[3])
    send_y(1)
    send_y(0)
    other[2], sent[1] = fence((other[2], sent[1]))
    grads_of(2)
    hop(1)
    send_y(2)
    step(("sent", 2), ("value", 2))
    grads_of(3)
    hop(2)
    pool = {}
    pool[0] = sum(totals[k] for k in range(1, planes)) + totals[0]
    pool[0] = pool[0] + go_core(pool[0])
    state["pool"] = pool
    step(("value", 3), ("sent", 2), ("value", 2))
    send_y(3)
    pool[0] = pool[0] + go_y(pool[0])
    step()
    hop(3)
    pool[0] = pool[0] + go_jump(pool[0], 4)
    step()
    final = total_of(0) + value[0].astype(f32)
    crossed = go_x(final[1].astype(bf16)).astype(f32)
    left = jnp.where(side == 0, final[0, :, :half], crossed[:, :half])
    right = jnp.where(side == 0, crossed[:, :half], final[0, :, :half])
    grad_normed = jnp.concatenate([left, right], axis=1)
    row_grads = final[0, :, half:] + crossed[:, half:]
    grad_down = make_down([kept[k] for k in range(planes)])
    part = pool[0]
    mine_sums = part + go_jump(part, 8)
    crossed = go_x(part) + go_far(part, 8)
    sums = jnp.concatenate(
        [jnp.where(side == 0, mine_sums, crossed), jnp.where(side == 0, crossed, mine_sums)],
        axis=1,
    )

    inputs = tokens[0].astype(f32)
    squashed = jnp.tanh(alpha[0] * inputs)
    pre_grad = grad_normed * gamma * (1.0 - squashed * squashed)
    grad_tokens = (cotangent[0].astype(f32) + alpha[0] * pre_grad).astype(bf16)
    grad_probs = jnp.sum(jnp.where(picks, row_grads[:, None, :], 0.0), axis=2).astype(bf16)
    grad_beta = sums[0]
    grad_gamma = sums[1]
    grad_alpha = jnp.sum(sums[2] * gamma).reshape(1)
    return (
        grad_tokens[None],
        grad_probs[None],
        grad_down[None],
        grad_gamma,
        grad_beta,
        grad_alpha,
    )


def slot_layout(ids_local, expert_count, capacity):
    token_count, top_count = ids_local.shape
    labels = jnp.arange(expert_count, dtype=jnp.int32)
    onehot = (ids_local[:, :, None] == labels[None, None, :]).astype(jnp.int32)
    picks = jnp.sum(onehot, axis=1)
    order = jnp.arange(token_count, dtype=jnp.int32)
    earlier = (order[None, :] < order[:, None]).astype(f32)
    before = jnp.dot(earlier, picks.astype(f32), precision=lax.Precision.HIGHEST)
    slots = jnp.sum(onehot * before.astype(jnp.int32)[:, None, :], axis=2)
    position = ids_local * capacity + slots
    pairs = jnp.arange(token_count * top_count, dtype=jnp.int32)
    table = jnp.full((expert_count * capacity,), token_count * top_count, jnp.int32)
    table = table.at[position.reshape(-1)].set(pairs)
    return (position, table)


def routed_shards(tokens, cotangent, expert_ids, gate_probs, alpha, gamma, beta, w_in, w_down):
    expert_count = lax.axis_size("expert")
    token_count = tokens.shape[1]
    top_count = expert_ids.shape[2]
    width = tokens.shape[2]
    capacity = 3 * token_count * top_count // (2 * expert_count)
    rows_total = expert_count * capacity
    inputs = tokens[0].astype(jnp.float32)
    squashed = jnp.tanh(alpha[0] * inputs)
    normed = (gamma * squashed + beta).astype(jnp.bfloat16)
    position, table = slot_layout(expert_ids[0], expert_count, capacity)
    source_token = table // top_count
    zero_row = jnp.zeros((1, width), jnp.bfloat16)
    normed_pad = jnp.concatenate([normed, zero_row], axis=0)
    cot_pad = jnp.concatenate([cotangent[0], zero_row], axis=0)
    prob_pad = jnp.concatenate([gate_probs[0].reshape(-1), jnp.zeros((1,), jnp.bfloat16)], axis=0)
    send_rows = normed_pad[source_token].reshape(expert_count, capacity, width)
    send_cot = cot_pad[source_token].reshape(expert_count, capacity, width)
    send_prob = prob_pad[table].reshape(expert_count, capacity)

    def swap(value):
        return lax.all_to_all(value, "expert", split_axis=0, concat_axis=0, tiled=True)

    in_rows = swap(send_rows).reshape(rows_total, width)
    cot_rows = swap(send_cot).reshape(rows_total, width)
    prob_rows = swap(send_prob).reshape(rows_total).astype(jnp.float32)
    gate_up = lax.all_gather(w_in, "dp", axis=2, tiled=True)
    w_lower = lax.all_gather(w_down, "dp", axis=1, tiled=True)[0]
    w_gate = gate_up[0, 0]
    w_upper = gate_up[0, 1]
    gate_pre = contract_width(in_rows, w_gate)
    up_value = contract_width(in_rows, w_upper)
    sigma = jax.nn.sigmoid(gate_pre)
    activation = (gate_pre * sigma * up_value).astype(jnp.bfloat16)
    back = contract_width(cot_rows, w_lower)
    weight_row = residual_scale * prob_rows
    scaled_cot = (weight_row[:, None] * cot_rows.astype(jnp.float32)).astype(jnp.bfloat16)
    row_grad = residual_scale * jnp.sum(activation.astype(jnp.float32) * back, axis=1)
    d_act = weight_row[:, None] * back
    d_gate = (d_act * up_value * sigma * (1.0 + gate_pre * (1.0 - sigma))).astype(jnp.bfloat16)
    d_up = (d_act * gate_pre * sigma).astype(jnp.bfloat16)
    d_rows = (
        jnp.dot(d_gate, w_gate, preferred_element_type=jnp.float32)
        + jnp.dot(d_up, w_upper, preferred_element_type=jnp.float32)
    ).astype(jnp.bfloat16)
    back_rows = swap(d_rows.reshape(expert_count, capacity, width))
    back_probs = swap(row_grad.astype(jnp.bfloat16).reshape(expert_count, capacity))
    partial_grad = lax.dot_general(
        activation, scaled_cot, (((0,), (0,)), ((), ())), preferred_element_type=jnp.float32
    )
    grad_down = lax.psum_scatter(
        partial_grad[None].astype(jnp.bfloat16), "dp", scatter_dimension=1, tiled=True
    )
    picked = back_rows.reshape(rows_total, width)[position]
    grad_normed = jnp.sum(picked.astype(jnp.float32), axis=1)
    grad_probs = back_probs.reshape(rows_total)[position]
    gamma_part = jnp.sum(grad_normed * squashed, axis=0)
    beta_part = jnp.sum(grad_normed, axis=0)
    pre_grad = grad_normed * gamma * (1.0 - squashed * squashed)
    alpha_part = jnp.sum(pre_grad * inputs).reshape(1)
    grad_gamma, grad_beta, grad_alpha = lax.psum(
        (gamma_part, beta_part, alpha_part), ("expert", "dp")
    )
    grad_tokens = (cotangent[0].astype(jnp.float32) + alpha[0] * pre_grad).astype(jnp.bfloat16)
    return (grad_tokens[None], grad_probs[None], grad_down, grad_gamma, grad_beta, grad_alpha)


def shards(*arrays):
    experts = lax.axis_size("expert")
    top_count = arrays[2].shape[2]
    dense = (
        lax.axis_size("dp") == 2
        and experts == 16
        and 2 * top_count >= experts
        and arrays[0].shape[2] % 2048 == 0
    )
    return (dense_shards if dense else routed_shards)(*arrays)


def solution(mesh):
    placed = (
        P("dp", "expert", None),
        P("dp", "expert", None),
        P("dp", "expert", None),
        P("dp", "expert", None),
        P(),
        P(),
        P(),
        P("expert", None, "dp", None),
        P("expert", "dp", None),
    )
    return jax.shard_map(
        shards,
        mesh=mesh,
        in_specs=placed,
        out_specs=(
            P("dp", "expert", None),
            P("dp", "expert", None),
            P("expert", "dp", None),
            P(),
            P(),
            P(),
        ),
        check_vma=False,
    )
```

```python
import functools
import jax
import jax.numpy as jnp
from jax import lax
from jax.experimental import pallas as pl
from jax.experimental.pallas import tpu as pltpu
from jax.sharding import PartitionSpec as P

residual_scale = 0.7071
LANES = 128
f32 = jnp.float32
bf16 = jnp.bfloat16


def contract_width(left, right):
    return lax.dot_general(
        left, right, (((1,), (1,)), ((), ())), preferred_element_type=f32
    )


def add16(left, right):
    return (left.astype(f32) + right.astype(f32)).astype(bf16)


def rows_kernel(segments, width, hidden, *refs):
    count = len(segments)
    blocks = refs[:count]
    (w_in, w_down, gamma, beta, alpha, expert) = refs[count : count + 6]
    (grads_out, kept_out, tail_out) = refs[count + 6 : count + 9]
    (normed, cot, weight, kept, sems) = refs[count + 9 :]
    rows = normed.shape[0]
    gain = alpha[0]
    mine = expert[0]
    gamma_row = gamma[...]
    beta_row = beta[...]
    for source, places in zip(blocks, segments):
        size = source.shape[0] // len(places)
        for part, to in enumerate(places):
            here, there = slice(part * size, (part + 1) * size), slice(to, to + size)
            squashed = jnp.tanh(gain * source[here, 0:width].astype(f32))
            normed[there, :] = (gamma_row * squashed + beta_row).astype(bf16)
            rows_cot = source[here, width : 2 * width]
            cot[there, :] = rows_cot
            gates = source[here, 2 * width :].astype(f32)
            lane = lax.broadcasted_iota(jnp.int32, gates.shape, 1)
            own = jnp.sum(jnp.where(lane == mine, gates, 0.0), axis=1, keepdims=True)
            own = residual_scale * own
            weight[there, :] = jnp.broadcast_to(own, (size, LANES))
            kept[there, hidden:] = (own * rows_cot.astype(f32)).astype(bf16)
    wide = slice(hidden, hidden + width)
    save_cot = pltpu.make_async_copy(kept.at[:, wide], kept_out.at[:, wide], sems.at[0])
    save_cot.start()
    pre = contract_width(normed[...], w_in[...])
    back = contract_width(cot[...], w_down[...])
    gate_pre = pre[:, :hidden]
    up_value = pre[:, hidden:]
    sigma = jax.nn.sigmoid(gate_pre)
    silu = gate_pre * sigma
    activation = (silu * up_value).astype(bf16)
    kept[:, :hidden] = activation
    save_act = pltpu.make_async_copy(
        kept.at[:, :hidden], kept_out.at[:, :hidden], sems.at[1]
    )
    save_act.start()
    row_grad = residual_scale * jnp.sum(activation.astype(f32) * back, axis=1, keepdims=True)
    d_act = weight[:, 0:1] * back
    d_gate = d_act * up_value * sigma * (1.0 + gate_pre * (1.0 - sigma))
    grads_out[:, :hidden] = d_gate.astype(bf16)
    grads_out[:, hidden:] = (d_act * gate_pre * sigma).astype(bf16)
    lane = lax.broadcasted_iota(jnp.int32, (rows, LANES), 1)
    tail_out[...] = jnp.where(lane == mine, row_grad, 0.0).astype(bf16)
    save_cot.wait()
    save_act.wait()


def grad_kernel(segments, half, *refs):
    count = len(segments)
    blocks = refs[:count]
    (near, far, w_in, w_far, tail, alpha, side) = refs[count : count + 7]
    (d_own, d_other, sums, squash, slope) = refs[count + 7 :]
    rows = near.shape[0]
    block = rows // 8
    gain = alpha[0]
    start = pl.multiple_of(side[0] * half, half)
    for source, places in zip(blocks, segments):
        size = source.shape[0] // len(places)
        for part, to in enumerate(places):
            inputs = source[part * size : (part + 1) * size, pl.ds(start, half)].astype(f32)
            squashed = jnp.tanh(gain * inputs)
            squash[to : to + size, :] = squashed
            slope[to : to + size, :] = (1.0 - squashed * squashed) * inputs
    mirrored = jnp.concatenate([far[rows // 2 :, :], far[: rows // 2, :]], axis=0)

    def place(cols, value):
        for x in range(2):
            for y in range(2):
                row = (x * 4 + y) * block
                d_own[x, y, :, cols] = value[row : row + block]
                row = (x * 4 + 2 + y) * block
                d_other[x, y, :, cols] = value[row : row + block]

    place(slice(half, half + LANES), tail[...])
    step = 512
    for at in range(0, half, step):
        cols = slice(at, at + step)
        part = jnp.dot(
            near[...],
            w_in[:, pl.ds(pl.multiple_of(start + at, step), step)],
            preferred_element_type=f32,
        )
        part = part + jnp.dot(mirrored, w_far[:, cols], preferred_element_type=f32)
        short = part.astype(bf16)
        place(cols, short)
        part = short.astype(f32)
        sums[0:1, cols] = jnp.sum(part, axis=0, keepdims=True)
        sums[1:2, cols] = jnp.sum(part * squash[:, cols], axis=0, keepdims=True)
        sums[2:3, cols] = jnp.sum(part * slope[:, cols], axis=0, keepdims=True)
        sums[3:8, cols] = jnp.zeros((5, step), f32)


def pack_kernel(tokens, cotangent, ids, probs, out):
    width = tokens.shape[1]
    top, block = ids.shape
    names = ids[...]
    shares = probs[...].astype(f32)
    label = lax.broadcasted_iota(jnp.int32, (LANES, block), 0)
    table = jnp.zeros((LANES, block), f32)
    for k in range(top):
        table = table + jnp.where(label == names[k : k + 1, :], shares[k : k + 1, :], 0.0)
    row = lax.broadcasted_iota(jnp.int32, (block, block), 0)
    column = lax.broadcasted_iota(jnp.int32, (block, block), 1)
    unit = jnp.where(row == column, 1.0, 0.0).astype(bf16)
    out[:, 2 * width :] = contract_width(unit, table.astype(bf16)).astype(bf16)
    out[:, :width] = tokens[...]
    out[:, width : 2 * width] = cotangent[...]


def down_kernel(count, hidden, *refs):
    kept = refs[:count]
    out, held, sems = refs[count:]
    half = kept[0].shape[0] // 2
    copies = []
    for batch in range(2):
        for k in range(count):
            copy = pltpu.make_async_copy(
                kept[k].at[batch * half : (batch + 1) * half, :],
                held.at[batch, k * half : (k + 1) * half, :],
                sems.at[batch, k],
            )
            copy.start()
            copies.append(copy)
    total = None
    for batch in range(2):
        for copy in copies[batch * count : (batch + 1) * count]:
            copy.wait()
        term = lax.dot_general(
            held[batch, :, :hidden],
            held[batch, :, hidden:],
            (((0,), (0,)), ((), ())),
            preferred_element_type=f32,
        )
        term = term.astype(bf16).astype(f32)
        total = term if total is None else total + term
    out[...] = total.astype(bf16)


def whole():
    return pl.BlockSpec(memory_space=pltpu.VMEM)


def scalar():
    return pl.BlockSpec(memory_space=pltpu.SMEM)


def dense_shards(tokens, cotangent, expert_ids, gate_probs, alpha, gamma, beta, w_in, w_down):
    experts = lax.axis_size("expert")
    planes = experts // 4
    block = tokens.shape[1]
    width = tokens.shape[2]
    hidden = w_down.shape[1]
    rows = 8 * block
    me = lax.axis_index("expert")

    def go_x(v):
        return lax.ppermute(v, "dp", [(0, 1), (1, 0)])

    def go_y(v):
        return lax.ppermute(v, "expert", [(e, e ^ 2) for e in range(experts)])

    def go_core(v):
        return lax.ppermute(v, "expert", [(e, e ^ 1) for e in range(experts)])

    def go_z(v):
        return lax.ppermute(v, "expert", [(e, (e + 4) % experts) for e in range(experts)])

    def go_jump(v, by):
        return lax.ppermute(v, "expert", [(e, e ^ by) for e in range(experts)])

    def go_far(v, by):
        pairs = [
            (2 * e + x, 2 * (e ^ by) + 1 - x) for e in range(experts) for x in range(2)
        ]
        return lax.ppermute(v, ("expert", "dp"), pairs)

    lanes = jnp.arange(LANES, dtype=jnp.int32)
    picks = expert_ids[0][:, :, None] == lanes[None, None, :]
    own = pl.pallas_call(
        pack_kernel,
        out_shape=jax.ShapeDtypeStruct((block, 2 * width + LANES), bf16),
        in_specs=[whole()] * 4,
        out_specs=whole(),
        name="pack",
    )(tokens[0], cotangent[0], expert_ids[0].T, gate_probs[0].T)

    flat_in = w_in[0].reshape(2 * hidden, width)
    flat_down = w_down[0]
    gamma_row = gamma.reshape(1, width)
    beta_row = beta.reshape(1, width)
    mine = me.reshape(1).astype(jnp.int32)
    half = width // 2
    side = lax.axis_index("dp").astype(jnp.int32)
    w_send = lax.dynamic_slice_in_dim(flat_in, (1 - side) * half, half, axis=1)

    segments = tuple(
        tuple((x * 4 + core * 2 + y) * block for x in range(2))
        for core in range(2)
        for y in range(2)
    )
    params = pltpu.CompilerParams(vmem_limit_bytes=14 << 20)

    def first_half(arrays):
        return pl.pallas_call(
            functools.partial(rows_kernel, segments, width, hidden),
            out_shape=(
                jax.ShapeDtypeStruct((rows, 2 * hidden), bf16),
                jax.ShapeDtypeStruct((rows, hidden + width), bf16),
                jax.ShapeDtypeStruct((rows, LANES), bf16),
            ),
            in_specs=[whole()] * 8 + [scalar(), scalar()],
            out_specs=(whole(), pl.BlockSpec(memory_space=pltpu.HBM), whole()),
            scratch_shapes=[
                pltpu.VMEM((rows, width), bf16),
                pltpu.VMEM((rows, width), bf16),
                pltpu.VMEM((rows, LANES), f32),
                pltpu.VMEM((rows, hidden + width), bf16),
                pltpu.SemaphoreType.DMA((2,)),
            ],
            compiler_params=params,
            name="rows",
        )(*arrays, flat_in, flat_down, gamma_row, beta_row, alpha, mine)

    def second_half(arrays, near, far, w_far, tail):
        return pl.pallas_call(
            functools.partial(grad_kernel, segments, half),
            out_shape=(
                jax.ShapeDtypeStruct((2, 2, block, half + LANES), bf16),
                jax.ShapeDtypeStruct((2, 2, block, half + LANES), bf16),
                jax.ShapeDtypeStruct((8, half), f32),
            ),
            in_specs=[whole()] * 9 + [scalar(), scalar()],
            out_specs=(whole(),) * 3,
            scratch_shapes=[
                pltpu.VMEM((rows, half), f32),
                pltpu.VMEM((rows, half), f32),
            ],
            compiler_params=params,
            name="grads",
        )(*arrays, near, far, flat_in, w_far, tail, alpha, side.reshape(1))

    fence = lax.optimization_barrier
    own = jnp.concatenate([own, go_x(own)], axis=0)
    near, far, near_c, far_c, w_far = {0: own}, {}, {}, {}, {}
    state = {"a": near, "b": far, "c": near_c, "d": far_c, "w": w_far}
    grads, kept, tails, other = {}, {}, {}, {}
    state.update(grads=grads, other=other)
    d_own, d_got, totals, sent, value = {}, {}, {}, {}, {}
    state.update(d_own=d_own, d_got=d_got, totals=totals, sent=sent, value=value)
    near[0], w_send = fence((near[0], w_send))
    w_far[0] = go_x(w_send)

    def make_down(held):
        return pl.pallas_call(
            functools.partial(down_kernel, planes, hidden),
            out_shape=jax.ShapeDtypeStruct((hidden, width), bf16),
            in_specs=[pl.BlockSpec(memory_space=pltpu.HBM)] * planes,
            out_specs=whole(),
            scratch_shapes=[
                pltpu.VMEM((2, planes * rows // 2, hidden + width), bf16),
                pltpu.SemaphoreType.DMA((2, planes)),
            ],
            compiler_params=pltpu.CompilerParams(vmem_limit_bytes=20 << 20),
            name="down",
        )(*held)

    def step(*late):
        now = {
            name: {k: v for k, v in held.items() if (name, k) not in late}
            for name, held in state.items()
        }
        new = fence(now)
        for name, held in state.items():
            held.update(new[name])

    def rows_of(k):
        arrays = (near[k], far[k], near_c[k], far_c[k])
        grads[k], kept[k], tails[k] = first_half(arrays)

    def grads_of(k):
        arrays = (near[k], far[k], near_c[k], far_c[k])
        d_own[k], moved, totals[k] = second_half(arrays, grads[k], other[k], w_far[0], tails[k])
        d_got[k] = go_core(moved)

    def send_y(k):
        sent[k] = go_y(add16(d_own[k][:, 1], d_got[k][:, 1]))

    def total_of(k):
        kept = d_own[k][:, 0].astype(f32) + d_got[k][:, 0].astype(f32)
        return kept + sent[k].astype(f32)

    def hop(k):
        carried = total_of(k)
        if k > 1:
            carried = carried + value[k].astype(f32)
        value[(k + 1) % planes] = go_z(carried.astype(bf16))

    for k in range(3):
        near[k + 1] = go_z(near[k])
        far[k] = go_y(near[k])
        near_c[k] = go_core(near[k])
        if k:
            far_c[k - 1] = go_core(far[k - 1])
            rows_of(k - 1)
        if k == 2:
            other[0] = go_x(grads[0])
        step(*([("w", 0)] if k == 0 else []))
    other[1] = go_x(grads[1])
    far[3] = go_y(near[3])
    near_c[3] = go_core(near[3])
    far_c[2] = go_core(far[2])
    rows_of(2)
    grads_of(0)
    step()
    other[2] = go_x(grads[2])
    far_c[3] = go_core(far[3])
    rows_of(3)
    other[1], far_c[3] = fence((other[1], far_c[3]))
    grads_of(1)
    step(("other", 2))
    other[3] = go_x(grads[3])
    send_y(1)
    send_y(0)
    other[2], sent[1], kept[3] = fence((other[2], sent[1], kept[3]))
    grads_of(2)
    hop(1)
    send_y(2)
    down = {0: make_down([kept[k] for k in range(planes)])}
    state["down"] = down
    step(("sent", 2), ("value", 2))
    grads_of(3)
    hop(2)
    pool = {}
    pool[0] = sum(totals[k] for k in range(1, planes)) + totals[0]
    pool[0] = pool[0] + go_core(pool[0])
    state["pool"] = pool
    step(("value", 3), ("sent", 2), ("value", 2))
    send_y(3)
    part = pool[0]
    mine_sums = part + go_y(part)
    cross_sums = go_x(part) + go_far(part, 2)
    pool[0] = jnp.concatenate([mine_sums, cross_sums], axis=0)
    step()
    hop(3)
    pool[0] = pool[0] + go_jump(pool[0], 4)
    step()
    final = total_of(0) + value[0].astype(f32)
    crossed = go_x(final[1].astype(bf16)).astype(f32)
    left = jnp.where(side == 0, final[0, :, :half], crossed[:, :half])
    right = jnp.where(side == 0, crossed[:, :half], final[0, :, :half])
    grad_normed = jnp.concatenate([left, right], axis=1)
    row_grads = final[0, :, half:] + crossed[:, half:]
    grad_down = down[0]
    sums = pool[0] + go_jump(pool[0], 8)
    mine_sums, cross_sums = sums[:8], sums[8:]
    sums = jnp.concatenate(
        [
            jnp.where(side == 0, mine_sums, cross_sums),
            jnp.where(side == 0, cross_sums, mine_sums),
        ],
        axis=1,
    )

    inputs = tokens[0].astype(f32)
    squashed = jnp.tanh(alpha[0] * inputs)
    pre_grad = grad_normed * gamma * (1.0 - squashed * squashed)
    grad_tokens = (cotangent[0].astype(f32) + alpha[0] * pre_grad).astype(bf16)
    grad_probs = jnp.sum(jnp.where(picks, row_grads[:, None, :], 0.0), axis=2).astype(bf16)
    grad_beta = sums[0]
    grad_gamma = sums[1]
    grad_alpha = jnp.sum(sums[2] * gamma).reshape(1)
    return (
        grad_tokens[None],
        grad_probs[None],
        grad_down[None],
        grad_gamma,
        grad_beta,
        grad_alpha,
    )


def slot_layout(ids_local, expert_count, capacity):
    token_count, top_count = ids_local.shape
    labels = jnp.arange(expert_count, dtype=jnp.int32)
    onehot = (ids_local[:, :, None] == labels[None, None, :]).astype(jnp.int32)
    picks = jnp.sum(onehot, axis=1)
    order = jnp.arange(token_count, dtype=jnp.int32)
    earlier = (order[None, :] < order[:, None]).astype(f32)
    before = jnp.dot(earlier, picks.astype(f32), precision=lax.Precision.HIGHEST)
    slots = jnp.sum(onehot * before.astype(jnp.int32)[:, None, :], axis=2)
    position = ids_local * capacity + slots
    pairs = jnp.arange(token_count * top_count, dtype=jnp.int32)
    table = jnp.full((expert_count * capacity,), token_count * top_count, jnp.int32)
    table = table.at[position.reshape(-1)].set(pairs)
    return (position, table)


def routed_shards(tokens, cotangent, expert_ids, gate_probs, alpha, gamma, beta, w_in, w_down):
    expert_count = lax.axis_size("expert")
    token_count = tokens.shape[1]
    top_count = expert_ids.shape[2]
    width = tokens.shape[2]
    capacity = 3 * token_count * top_count // (2 * expert_count)
    rows_total = expert_count * capacity
    inputs = tokens[0].astype(jnp.float32)
    squashed = jnp.tanh(alpha[0] * inputs)
    normed = (gamma * squashed + beta).astype(jnp.bfloat16)
    position, table = slot_layout(expert_ids[0], expert_count, capacity)
    source_token = table // top_count
    zero_row = jnp.zeros((1, width), jnp.bfloat16)
    normed_pad = jnp.concatenate([normed, zero_row], axis=0)
    cot_pad = jnp.concatenate([cotangent[0], zero_row], axis=0)
    prob_pad = jnp.concatenate([gate_probs[0].reshape(-1), jnp.zeros((1,), jnp.bfloat16)], axis=0)
    send_rows = normed_pad[source_token].reshape(expert_count, capacity, width)
    send_cot = cot_pad[source_token].reshape(expert_count, capacity, width)
    send_prob = prob_pad[table].reshape(expert_count, capacity)

    def swap(value):
        return lax.all_to_all(value, "expert", split_axis=0, concat_axis=0, tiled=True)

    in_rows = swap(send_rows).reshape(rows_total, width)
    cot_rows = swap(send_cot).reshape(rows_total, width)
    prob_rows = swap(send_prob).reshape(rows_total).astype(jnp.float32)
    gate_up = lax.all_gather(w_in, "dp", axis=2, tiled=True)
    w_lower = lax.all_gather(w_down, "dp", axis=1, tiled=True)[0]
    w_gate = gate_up[0, 0]
    w_upper = gate_up[0, 1]
    gate_pre = contract_width(in_rows, w_gate)
    up_value = contract_width(in_rows, w_upper)
    sigma = jax.nn.sigmoid(gate_pre)
    activation = (gate_pre * sigma * up_value).astype(jnp.bfloat16)
    back = contract_width(cot_rows, w_lower)
    weight_row = residual_scale * prob_rows
    scaled_cot = (weight_row[:, None] * cot_rows.astype(jnp.float32)).astype(jnp.bfloat16)
    row_grad = residual_scale * jnp.sum(activation.astype(jnp.float32) * back, axis=1)
    d_act = weight_row[:, None] * back
    d_gate = (d_act * up_value * sigma * (1.0 + gate_pre * (1.0 - sigma))).astype(jnp.bfloat16)
    d_up = (d_act * gate_pre * sigma).astype(jnp.bfloat16)
    d_rows = (
        jnp.dot(d_gate, w_gate, preferred_element_type=jnp.float32)
        + jnp.dot(d_up, w_upper, preferred_element_type=jnp.float32)
    ).astype(jnp.bfloat16)
    back_rows = swap(d_rows.reshape(expert_count, capacity, width))
    back_probs = swap(row_grad.astype(jnp.bfloat16).reshape(expert_count, capacity))
    partial_grad = lax.dot_general(
        activation, scaled_cot, (((0,), (0,)), ((), ())), preferred_element_type=jnp.float32
    )
    grad_down = lax.psum_scatter(
        partial_grad[None].astype(jnp.bfloat16), "dp", scatter_dimension=1, tiled=True
    )
    picked = back_rows.reshape(rows_total, width)[position]
    grad_normed = jnp.sum(picked.astype(jnp.float32), axis=1)
    grad_probs = back_probs.reshape(rows_total)[position]
    gamma_part = jnp.sum(grad_normed * squashed, axis=0)
    beta_part = jnp.sum(grad_normed, axis=0)
    pre_grad = grad_normed * gamma * (1.0 - squashed * squashed)
    alpha_part = jnp.sum(pre_grad * inputs).reshape(1)
    grad_gamma, grad_beta, grad_alpha = lax.psum(
        (gamma_part, beta_part, alpha_part), ("expert", "dp")
    )
    grad_tokens = (cotangent[0].astype(jnp.float32) + alpha[0] * pre_grad).astype(jnp.bfloat16)
    return (grad_tokens[None], grad_probs[None], grad_down, grad_gamma, grad_beta, grad_alpha)


def shards(*arrays):
    experts = lax.axis_size("expert")
    top_count = arrays[2].shape[2]
    dense = (
        lax.axis_size("dp") == 2
        and experts == 16
        and 2 * top_count >= experts
        and arrays[0].shape[2] % 2048 == 0
    )
    return (dense_shards if dense else routed_shards)(*arrays)


def solution(mesh):
    placed = (
        P("dp", "expert", None),
        P("dp", "expert", None),
        P("dp", "expert", None),
        P("dp", "expert", None),
        P(),
        P(),
        P(),
        P("expert", None, "dp", None),
        P("expert", "dp", None),
    )
    return jax.shard_map(
        shards,
        mesh=mesh,
        in_specs=placed,
        out_specs=(
            P("dp", "expert", None),
            P("dp", "expert", None),
            P("expert", "dp", None),
            P(),
            P(),
            P(),
        ),
        check_vma=False,
    )
```

```python
import functools
import jax
import jax.numpy as jnp
from jax import lax
from jax.experimental import pallas as pl
from jax.experimental.pallas import tpu as pltpu
from jax.sharding import PartitionSpec as P

residual_scale = 0.7071
LANES = 128
f32 = jnp.float32
bf16 = jnp.bfloat16


def contract_width(left, right):
    return lax.dot_general(
        left, right, (((1,), (1,)), ((), ())), preferred_element_type=f32
    )


def add16(left, right):
    return (left.astype(f32) + right.astype(f32)).astype(bf16)


def rows_kernel(segments, width, hidden, *refs):
    count = len(segments)
    blocks = refs[:count]
    (w_in, w_down, gamma, beta, alpha, expert) = refs[count : count + 6]
    (grads_out, kept_out, tail_out) = refs[count + 6 : count + 9]
    (normed, cot, weight, kept, sems) = refs[count + 9 :]
    rows = normed.shape[0]
    gain = alpha[0]
    mine = expert[0]
    gamma_row = gamma[...]
    beta_row = beta[...]
    for source, places in zip(blocks, segments):
        size = source.shape[0] // len(places)
        for part, to in enumerate(places):
            here, there = slice(part * size, (part + 1) * size), slice(to, to + size)
            squashed = jnp.tanh(gain * source[here, 0:width].astype(f32))
            normed[there, :] = (gamma_row * squashed + beta_row).astype(bf16)
            rows_cot = source[here, width : 2 * width]
            cot[there, :] = rows_cot
            gates = source[here, 2 * width :].astype(f32)
            lane = lax.broadcasted_iota(jnp.int32, gates.shape, 1)
            own = jnp.sum(jnp.where(lane == mine, gates, 0.0), axis=1, keepdims=True)
            own = residual_scale * own
            weight[there, :] = jnp.broadcast_to(own, (size, LANES))
            kept[there, hidden:] = (own * rows_cot.astype(f32)).astype(bf16)
    wide = slice(hidden, hidden + width)
    save_cot = pltpu.make_async_copy(kept.at[:, wide], kept_out.at[:, wide], sems.at[0])
    save_cot.start()
    pre = contract_width(normed[...], w_in[...])
    back = contract_width(cot[...], w_down[...])
    gate_pre = pre[:, :hidden]
    up_value = pre[:, hidden:]
    sigma = jax.nn.sigmoid(gate_pre)
    silu = gate_pre * sigma
    activation = (silu * up_value).astype(bf16)
    kept[:, :hidden] = activation
    save_act = pltpu.make_async_copy(
        kept.at[:, :hidden], kept_out.at[:, :hidden], sems.at[1]
    )
    save_act.start()
    row_grad = residual_scale * jnp.sum(activation.astype(f32) * back, axis=1, keepdims=True)
    d_act = weight[:, 0:1] * back
    d_gate = d_act * up_value * sigma * (1.0 + gate_pre * (1.0 - sigma))
    grads_out[:, :hidden] = d_gate.astype(bf16)
    grads_out[:, hidden:] = (d_act * gate_pre * sigma).astype(bf16)
    lane = lax.broadcasted_iota(jnp.int32, (rows, LANES), 1)
    tail_out[...] = jnp.where(lane == mine, row_grad, 0.0).astype(bf16)
    save_cot.wait()
    save_act.wait()


def grad_kernel(segments, half, *refs):
    count = len(segments)
    blocks = refs[:count]
    (near, far, w_in, w_far, tail, alpha, side) = refs[count : count + 7]
    (d_own, d_other, sums, squash, slope) = refs[count + 7 :]
    rows = near.shape[0]
    block = rows // 8
    gain = alpha[0]
    start = pl.multiple_of(side[0] * half, half)
    for source, places in zip(blocks, segments):
        size = source.shape[0] // len(places)
        for part, to in enumerate(places):
            inputs = source[part * size : (part + 1) * size, pl.ds(start, half)].astype(f32)
            squashed = jnp.tanh(gain * inputs)
            squash[to : to + size, :] = squashed
            slope[to : to + size, :] = (1.0 - squashed * squashed) * inputs
    mirrored = jnp.concatenate([far[rows // 2 :, :], far[: rows // 2, :]], axis=0)

    def place(cols, value):
        for x in range(2):
            for y in range(2):
                row = (x * 4 + y) * block
                d_own[x, y, :, cols] = value[row : row + block]
                row = (x * 4 + 2 + y) * block
                d_other[x, y, :, cols] = value[row : row + block]

    place(slice(half, half + LANES), tail[...])
    step = 512
    for at in range(0, half, step):
        cols = slice(at, at + step)
        part = jnp.dot(
            near[...],
            w_in[:, pl.ds(pl.multiple_of(start + at, step), step)],
            preferred_element_type=f32,
        )
        part = part + jnp.dot(mirrored, w_far[:, cols], preferred_element_type=f32)
        short = part.astype(bf16)
        place(cols, short)
        part = short.astype(f32)
        sums[0:1, cols] = jnp.sum(part, axis=0, keepdims=True)
        sums[1:2, cols] = jnp.sum(part * squash[:, cols], axis=0, keepdims=True)
        sums[2:3, cols] = jnp.sum(part * slope[:, cols], axis=0, keepdims=True)
        sums[3:8, cols] = jnp.zeros((5, step), f32)


def pack_kernel(tokens, cotangent, ids, probs, out):
    width = tokens.shape[1]
    top, block = ids.shape
    names = ids[...]
    shares = probs[...].astype(f32)
    label = lax.broadcasted_iota(jnp.int32, (LANES, block), 0)
    table = jnp.zeros((LANES, block), f32)
    for k in range(top):
        table = table + jnp.where(label == names[k : k + 1, :], shares[k : k + 1, :], 0.0)
    row = lax.broadcasted_iota(jnp.int32, (block, block), 0)
    column = lax.broadcasted_iota(jnp.int32, (block, block), 1)
    unit = jnp.where(row == column, 1.0, 0.0).astype(bf16)
    out[:, 2 * width :] = contract_width(unit, table.astype(bf16)).astype(bf16)
    out[:, :width] = tokens[...]
    out[:, width : 2 * width] = cotangent[...]


def down_kernel(count, hidden, *refs):
    kept = refs[:count]
    out, held, sems = refs[count:]
    half = kept[0].shape[0] // 2
    copies = []
    for batch in range(2):
        for k in range(count):
            copy = pltpu.make_async_copy(
                kept[k].at[batch * half : (batch + 1) * half, :],
                held.at[batch, k * half : (k + 1) * half, :],
                sems.at[batch, k],
            )
            copy.start()
            copies.append(copy)
    total = None
    for batch in range(2):
        for copy in copies[batch * count : (batch + 1) * count]:
            copy.wait()
        term = lax.dot_general(
            held[batch, :, :hidden],
            held[batch, :, hidden:],
            (((0,), (0,)), ((), ())),
            preferred_element_type=f32,
        )
        term = term.astype(bf16).astype(f32)
        total = term if total is None else total + term
    out[...] = total.astype(bf16)


def whole():
    return pl.BlockSpec(memory_space=pltpu.VMEM)


def scalar():
    return pl.BlockSpec(memory_space=pltpu.SMEM)


def dense_shards(tokens, cotangent, expert_ids, gate_probs, alpha, gamma, beta, w_in, w_down):
    experts = lax.axis_size("expert")
    planes = experts // 4
    block = tokens.shape[1]
    width = tokens.shape[2]
    hidden = w_down.shape[1]
    rows = 8 * block
    me = lax.axis_index("expert")

    def go_x(v):
        return lax.ppermute(v, "dp", [(0, 1), (1, 0)])

    def go_y(v):
        return lax.ppermute(v, "expert", [(e, e ^ 2) for e in range(experts)])

    def go_core(v):
        return lax.ppermute(v, "expert", [(e, e ^ 1) for e in range(experts)])

    def go_z(v):
        return lax.ppermute(v, "expert", [(e, (e + 4) % experts) for e in range(experts)])

    def go_jump(v, by):
        return lax.ppermute(v, "expert", [(e, e ^ by) for e in range(experts)])

    def go_far(v, by):
        pairs = [
            (2 * e + x, 2 * (e ^ by) + 1 - x) for e in range(experts) for x in range(2)
        ]
        return lax.ppermute(v, ("expert", "dp"), pairs)

    lanes = jnp.arange(LANES, dtype=jnp.int32)
    picks = expert_ids[0][:, :, None] == lanes[None, None, :]
    own = pl.pallas_call(
        pack_kernel,
        out_shape=jax.ShapeDtypeStruct((block, 2 * width + LANES), bf16),
        in_specs=[whole()] * 4,
        out_specs=whole(),
        name="pack",
    )(tokens[0], cotangent[0], expert_ids[0].T, gate_probs[0].T)

    flat_in = w_in[0].reshape(2 * hidden, width)
    flat_down = w_down[0]
    gamma_row = gamma.reshape(1, width)
    beta_row = beta.reshape(1, width)
    mine = me.reshape(1).astype(jnp.int32)
    half = width // 2
    side = lax.axis_index("dp").astype(jnp.int32)
    w_send = lax.dynamic_slice_in_dim(flat_in, (1 - side) * half, half, axis=1)

    segments = tuple(
        tuple((x * 4 + core * 2 + y) * block for x in range(2))
        for core in range(2)
        for y in range(2)
    )
    params = pltpu.CompilerParams(vmem_limit_bytes=14 << 20)

    def first_half(arrays):
        return pl.pallas_call(
            functools.partial(rows_kernel, segments, width, hidden),
            out_shape=(
                jax.ShapeDtypeStruct((rows, 2 * hidden), bf16),
                jax.ShapeDtypeStruct((rows, hidden + width), bf16),
                jax.ShapeDtypeStruct((rows, LANES), bf16),
            ),
            in_specs=[whole()] * 8 + [scalar(), scalar()],
            out_specs=(whole(), pl.BlockSpec(memory_space=pltpu.HBM), whole()),
            scratch_shapes=[
                pltpu.VMEM((rows, width), bf16),
                pltpu.VMEM((rows, width), bf16),
                pltpu.VMEM((rows, LANES), f32),
                pltpu.VMEM((rows, hidden + width), bf16),
                pltpu.SemaphoreType.DMA((2,)),
            ],
            compiler_params=params,
            name="rows",
        )(*arrays, flat_in, flat_down, gamma_row, beta_row, alpha, mine)

    def second_half(arrays, near, far, w_far, tail):
        return pl.pallas_call(
            functools.partial(grad_kernel, segments, half),
            out_shape=(
                jax.ShapeDtypeStruct((2, 2, block, half + LANES), bf16),
                jax.ShapeDtypeStruct((2, 2, block, half + LANES), bf16),
                jax.ShapeDtypeStruct((8, half), f32),
            ),
            in_specs=[whole()] * 9 + [scalar(), scalar()],
            out_specs=(whole(),) * 3,
            scratch_shapes=[
                pltpu.VMEM((rows, half), f32),
                pltpu.VMEM((rows, half), f32),
            ],
            compiler_params=params,
            name="grads",
        )(*arrays, near, far, flat_in, w_far, tail, alpha, side.reshape(1))

    fence = lax.optimization_barrier
    own = jnp.concatenate([own, go_x(own)], axis=0)
    near, far, near_c, far_c, w_far = {0: own}, {}, {}, {}, {}
    state = {"a": near, "b": far, "c": near_c, "d": far_c, "w": w_far}
    grads, kept, tails, other = {}, {}, {}, {}
    state.update(grads=grads, other=other)
    d_own, d_got, totals, sent, value = {}, {}, {}, {}, {}
    state.update(d_own=d_own, d_got=d_got, totals=totals, sent=sent, value=value)

    def make_down(held):
        return pl.pallas_call(
            functools.partial(down_kernel, planes, hidden),
            out_shape=jax.ShapeDtypeStruct((hidden, width), bf16),
            in_specs=[pl.BlockSpec(memory_space=pltpu.HBM)] * planes,
            out_specs=whole(),
            scratch_shapes=[
                pltpu.VMEM((2, planes * rows // 2, hidden + width), bf16),
                pltpu.SemaphoreType.DMA((2, planes)),
            ],
            compiler_params=pltpu.CompilerParams(vmem_limit_bytes=20 << 20),
            name="down",
        )(*held)

    def step(*late):
        now = {
            name: {k: v for k, v in held.items() if (name, k) not in late}
            for name, held in state.items()
        }
        new = fence(now)
        for name, held in state.items():
            held.update(new[name])

    def rows_of(k):
        arrays = (near[k], far[k], near_c[k], far_c[k])
        grads[k], kept[k], tails[k] = first_half(arrays)

    def grads_of(k):
        arrays = (near[k], far[k], near_c[k], far_c[k])
        d_own[k], moved, totals[k] = second_half(arrays, grads[k], other[k], w_far[0], tails[k])
        d_got[k] = go_core(moved)

    def send_y(k):
        sent[k] = go_y(add16(d_own[k][:, 1], d_got[k][:, 1]))

    def total_of(k):
        kept = d_own[k][:, 0].astype(f32) + d_got[k][:, 0].astype(f32)
        return kept + sent[k].astype(f32)

    def hop(k):
        carried = total_of(k)
        if k > 1:
            carried = carried + value[k].astype(f32)
        value[(k + 1) % planes] = go_z(carried.astype(bf16))

    for k in range(3):
        near[k + 1] = go_z(near[k])
        far[k] = go_y(near[k])
        near_c[k] = go_core(near[k])
        if k == 0:
            w_send, near_c[0] = fence((w_send, near_c[0]))
            w_far[0] = go_x(w_send)
        else:
            far_c[k - 1] = go_core(far[k - 1])
            rows_of(k - 1)
        if k == 2:
            other[0] = go_x(grads[0])
        step(*([("w", 0)] if k < 2 else []))
    other[1] = go_x(grads[1])
    far[3] = go_y(near[3])
    near_c[3] = go_core(near[3])
    far_c[2] = go_core(far[2])
    rows_of(2)
    grads_of(0)
    step()
    other[2] = go_x(grads[2])
    far_c[3] = go_core(far[3])
    send_y(0)
    rows_of(3)
    other[1], grads[3] = fence((other[1], grads[3]))
    grads_of(1)
    step()
    other[3] = go_x(grads[3])
    send_y(1)
    other[2], sent[1] = fence((other[2], sent[1]))
    grads_of(2)
    hop(1)
    send_y(2)
    step(("sent", 2), ("value", 2))
    grads_of(3)
    hop(2)
    pool = {}
    pool[0] = sum(totals[k] for k in range(1, planes)) + totals[0]
    pool[0] = pool[0] + go_core(pool[0])
    state["pool"] = pool
    step(("value", 3), ("sent", 2), ("value", 2))
    send_y(3)
    part = pool[0]
    mine_sums = part + go_y(part)
    cross_sums = go_x(part) + go_far(part, 2)
    pool[0] = jnp.concatenate([mine_sums, cross_sums], axis=0)
    step(("pool", 0))
    hop(3)
    kept[3], value[3] = fence((kept[3], value[3]))
    down = {0: make_down([kept[k] for k in range(planes)])}
    state["down"] = down
    pool[0] = pool[0] + go_jump(pool[0], 4)
    step()
    final = total_of(0) + value[0].astype(f32)
    crossed = go_x(final[1].astype(bf16)).astype(f32)
    left = jnp.where(side == 0, final[0, :, :half], crossed[:, :half])
    right = jnp.where(side == 0, crossed[:, :half], final[0, :, :half])
    grad_normed = jnp.concatenate([left, right], axis=1)
    row_grads = final[0, :, half:] + crossed[:, half:]
    grad_down = down[0]
    sums = pool[0] + go_jump(pool[0], 8)
    mine_sums, cross_sums = sums[:8], sums[8:]
    sums = jnp.concatenate(
        [
            jnp.where(side == 0, mine_sums, cross_sums),
            jnp.where(side == 0, cross_sums, mine_sums),
        ],
        axis=1,
    )

    inputs = tokens[0].astype(f32)
    squashed = jnp.tanh(alpha[0] * inputs)
    pre_grad = grad_normed * gamma * (1.0 - squashed * squashed)
    grad_tokens = (cotangent[0].astype(f32) + alpha[0] * pre_grad).astype(bf16)
    grad_probs = jnp.sum(jnp.where(picks, row_grads[:, None, :], 0.0), axis=2).astype(bf16)
    grad_beta = sums[0]
    grad_gamma = sums[1]
    grad_alpha = jnp.sum(sums[2] * gamma).reshape(1)
    return (
        grad_tokens[None],
        grad_probs[None],
        grad_down[None],
        grad_gamma,
        grad_beta,
        grad_alpha,
    )


def slot_layout(ids_local, expert_count, capacity):
    token_count, top_count = ids_local.shape
    labels = jnp.arange(expert_count, dtype=jnp.int32)
    onehot = (ids_local[:, :, None] == labels[None, None, :]).astype(jnp.int32)
    picks = jnp.sum(onehot, axis=1)
    order = jnp.arange(token_count, dtype=jnp.int32)
    earlier = (order[None, :] < order[:, None]).astype(f32)
    before = jnp.dot(earlier, picks.astype(f32), precision=lax.Precision.HIGHEST)
    slots = jnp.sum(onehot * before.astype(jnp.int32)[:, None, :], axis=2)
    position = ids_local * capacity + slots
    pairs = jnp.arange(token_count * top_count, dtype=jnp.int32)
    table = jnp.full((expert_count * capacity,), token_count * top_count, jnp.int32)
    table = table.at[position.reshape(-1)].set(pairs)
    return (position, table)


def routed_shards(tokens, cotangent, expert_ids, gate_probs, alpha, gamma, beta, w_in, w_down):
    expert_count = lax.axis_size("expert")
    token_count = tokens.shape[1]
    top_count = expert_ids.shape[2]
    width = tokens.shape[2]
    capacity = 3 * token_count * top_count // (2 * expert_count)
    rows_total = expert_count * capacity
    inputs = tokens[0].astype(jnp.float32)
    squashed = jnp.tanh(alpha[0] * inputs)
    normed = (gamma * squashed + beta).astype(jnp.bfloat16)
    position, table = slot_layout(expert_ids[0], expert_count, capacity)
    source_token = table // top_count
    zero_row = jnp.zeros((1, width), jnp.bfloat16)
    normed_pad = jnp.concatenate([normed, zero_row], axis=0)
    cot_pad = jnp.concatenate([cotangent[0], zero_row], axis=0)
    prob_pad = jnp.concatenate([gate_probs[0].reshape(-1), jnp.zeros((1,), jnp.bfloat16)], axis=0)
    send_rows = normed_pad[source_token].reshape(expert_count, capacity, width)
    send_cot = cot_pad[source_token].reshape(expert_count, capacity, width)
    send_prob = prob_pad[table].reshape(expert_count, capacity)

    def swap(value):
        return lax.all_to_all(value, "expert", split_axis=0, concat_axis=0, tiled=True)

    in_rows = swap(send_rows).reshape(rows_total, width)
    cot_rows = swap(send_cot).reshape(rows_total, width)
    prob_rows = swap(send_prob).reshape(rows_total).astype(jnp.float32)
    gate_up = lax.all_gather(w_in, "dp", axis=2, tiled=True)
    w_lower = lax.all_gather(w_down, "dp", axis=1, tiled=True)[0]
    w_gate = gate_up[0, 0]
    w_upper = gate_up[0, 1]
    gate_pre = contract_width(in_rows, w_gate)
    up_value = contract_width(in_rows, w_upper)
    sigma = jax.nn.sigmoid(gate_pre)
    activation = (gate_pre * sigma * up_value).astype(jnp.bfloat16)
    back = contract_width(cot_rows, w_lower)
    weight_row = residual_scale * prob_rows
    scaled_cot = (weight_row[:, None] * cot_rows.astype(jnp.float32)).astype(jnp.bfloat16)
    row_grad = residual_scale * jnp.sum(activation.astype(jnp.float32) * back, axis=1)
    d_act = weight_row[:, None] * back
    d_gate = (d_act * up_value * sigma * (1.0 + gate_pre * (1.0 - sigma))).astype(jnp.bfloat16)
    d_up = (d_act * gate_pre * sigma).astype(jnp.bfloat16)
    d_rows = (
        jnp.dot(d_gate, w_gate, preferred_element_type=jnp.float32)
        + jnp.dot(d_up, w_upper, preferred_element_type=jnp.float32)
    ).astype(jnp.bfloat16)
    back_rows = swap(d_rows.reshape(expert_count, capacity, width))
    back_probs = swap(row_grad.astype(jnp.bfloat16).reshape(expert_count, capacity))
    partial_grad = lax.dot_general(
        activation, scaled_cot, (((0,), (0,)), ((), ())), preferred_element_type=jnp.float32
    )
    grad_down = lax.psum_scatter(
        partial_grad[None].astype(jnp.bfloat16), "dp", scatter_dimension=1, tiled=True
    )
    picked = back_rows.reshape(rows_total, width)[position]
    grad_normed = jnp.sum(picked.astype(jnp.float32), axis=1)
    grad_probs = back_probs.reshape(rows_total)[position]
    gamma_part = jnp.sum(grad_normed * squashed, axis=0)
    beta_part = jnp.sum(grad_normed, axis=0)
    pre_grad = grad_normed * gamma * (1.0 - squashed * squashed)
    alpha_part = jnp.sum(pre_grad * inputs).reshape(1)
    grad_gamma, grad_beta, grad_alpha = lax.psum(
        (gamma_part, beta_part, alpha_part), ("expert", "dp")
    )
    grad_tokens = (cotangent[0].astype(jnp.float32) + alpha[0] * pre_grad).astype(jnp.bfloat16)
    return (grad_tokens[None], grad_probs[None], grad_down, grad_gamma, grad_beta, grad_alpha)


def shards(*arrays):
    experts = lax.axis_size("expert")
    top_count = arrays[2].shape[2]
    dense = (
        lax.axis_size("dp") == 2
        and experts == 16
        and 2 * top_count >= experts
        and arrays[0].shape[2] % 2048 == 0
    )
    return (dense_shards if dense else routed_shards)(*arrays)


def solution(mesh):
    placed = (
        P("dp", "expert", None),
        P("dp", "expert", None),
        P("dp", "expert", None),
        P("dp", "expert", None),
        P(),
        P(),
        P(),
        P("expert", None, "dp", None),
        P("expert", "dp", None),
    )
    return jax.shard_map(
        shards,
        mesh=mesh,
        in_specs=placed,
        out_specs=(
            P("dp", "expert", None),
            P("dp", "expert", None),
            P("expert", "dp", None),
            P(),
            P(),
            P(),
        ),
        check_vma=False,
    )
```

```python
import functools
import jax
import jax.numpy as jnp
from jax import lax
from jax.experimental import pallas as pl
from jax.experimental.pallas import tpu as pltpu
from jax.sharding import PartitionSpec as P

residual_scale = 0.7071
LANES = 128
f32 = jnp.float32
bf16 = jnp.bfloat16


def contract_width(left, right):
    return lax.dot_general(
        left, right, (((1,), (1,)), ((), ())), preferred_element_type=f32
    )


def add16(left, right):
    return (left.astype(f32) + right.astype(f32)).astype(bf16)


def rows_kernel(segments, width, hidden, *refs):
    count = len(segments)
    blocks = refs[:count]
    (w_in, w_down, gamma, beta, alpha, expert) = refs[count : count + 6]
    (grads_out, kept_out, tail_out) = refs[count + 6 : count + 9]
    (normed, cot, weight, kept, sems) = refs[count + 9 :]
    rows = normed.shape[0]
    gain = alpha[0]
    mine = expert[0]
    gamma_row = gamma[...]
    beta_row = beta[...]
    for source, places in zip(blocks, segments):
        size = source.shape[0] // len(places)
        for part, to in enumerate(places):
            here, there = slice(part * size, (part + 1) * size), slice(to, to + size)
            squashed = jnp.tanh(gain * source[here, 0:width].astype(f32))
            normed[there, :] = (gamma_row * squashed + beta_row).astype(bf16)
            rows_cot = source[here, width : 2 * width]
            cot[there, :] = rows_cot
            gates = source[here, 2 * width :].astype(f32)
            lane = lax.broadcasted_iota(jnp.int32, gates.shape, 1)
            own = jnp.sum(jnp.where(lane == mine, gates, 0.0), axis=1, keepdims=True)
            own = residual_scale * own
            weight[there, :] = jnp.broadcast_to(own, (size, LANES))
            kept[there, hidden:] = (own * rows_cot.astype(f32)).astype(bf16)
    wide = slice(hidden, hidden + width)
    save_cot = pltpu.make_async_copy(kept.at[:, wide], kept_out.at[:, wide], sems.at[0])
    save_cot.start()
    pre = contract_width(normed[...], w_in[...])
    back = contract_width(cot[...], w_down[...])
    gate_pre = pre[:, :hidden]
    up_value = pre[:, hidden:]
    sigma = jax.nn.sigmoid(gate_pre)
    silu = gate_pre * sigma
    activation = (silu * up_value).astype(bf16)
    kept[:, :hidden] = activation
    save_act = pltpu.make_async_copy(
        kept.at[:, :hidden], kept_out.at[:, :hidden], sems.at[1]
    )
    save_act.start()
    row_grad = residual_scale * jnp.sum(activation.astype(f32) * back, axis=1, keepdims=True)
    d_act = weight[:, 0:1] * back
    d_gate = d_act * up_value * sigma * (1.0 + gate_pre * (1.0 - sigma))
    grads_out[:, :hidden] = d_gate.astype(bf16)
    grads_out[:, hidden:] = (d_act * gate_pre * sigma).astype(bf16)
    lane = lax.broadcasted_iota(jnp.int32, (rows, LANES), 1)
    tail_out[...] = jnp.where(lane == mine, row_grad, 0.0).astype(bf16)
    save_cot.wait()
    save_act.wait()


def grad_kernel(segments, half, *refs):
    count = len(segments)
    blocks = refs[:count]
    (near, far, w_in, w_far, tail, alpha, side) = refs[count : count + 7]
    (d_own, d_other, sums, squash, slope) = refs[count + 7 :]
    rows = near.shape[0]
    block = rows // 8
    gain = alpha[0]
    start = pl.multiple_of(side[0] * half, half)
    for source, places in zip(blocks, segments):
        size = source.shape[0] // len(places)
        for part, to in enumerate(places):
            inputs = source[part * size : (part + 1) * size, pl.ds(start, half)].astype(f32)
            squashed = jnp.tanh(gain * inputs)
            squash[to : to + size, :] = squashed
            slope[to : to + size, :] = (1.0 - squashed * squashed) * inputs
    mirrored = jnp.concatenate([far[rows // 2 :, :], far[: rows // 2, :]], axis=0)

    def place(cols, value):
        for x in range(2):
            for y in range(2):
                row = (x * 4 + y) * block
                d_own[x, y, :, cols] = value[row : row + block]
                row = (x * 4 + 2 + y) * block
                d_other[x, y, :, cols] = value[row : row + block]

    place(slice(half, half + LANES), tail[...])
    step = 512
    for at in range(0, half, step):
        cols = slice(at, at + step)
        part = jnp.dot(
            near[...],
            w_in[:, pl.ds(pl.multiple_of(start + at, step), step)],
            preferred_element_type=f32,
        )
        part = part + jnp.dot(mirrored, w_far[:, cols], preferred_element_type=f32)
        short = part.astype(bf16)
        place(cols, short)
        part = short.astype(f32)
        sums[0:1, cols] = jnp.sum(part, axis=0, keepdims=True)
        sums[1:2, cols] = jnp.sum(part * squash[:, cols], axis=0, keepdims=True)
        sums[2:3, cols] = jnp.sum(part * slope[:, cols], axis=0, keepdims=True)
        sums[3:8, cols] = jnp.zeros((5, step), f32)


def pack_kernel(tokens, cotangent, ids, probs, out):
    width = tokens.shape[1]
    top, block = ids.shape
    names = ids[...]
    shares = probs[...].astype(f32)
    label = lax.broadcasted_iota(jnp.int32, (LANES, block), 0)
    table = jnp.zeros((LANES, block), f32)
    for k in range(top):
        table = table + jnp.where(label == names[k : k + 1, :], shares[k : k + 1, :], 0.0)
    row = lax.broadcasted_iota(jnp.int32, (block, block), 0)
    column = lax.broadcasted_iota(jnp.int32, (block, block), 1)
    unit = jnp.where(row == column, 1.0, 0.0).astype(bf16)
    out[:, 2 * width :] = contract_width(unit, table.astype(bf16)).astype(bf16)
    out[:, :width] = tokens[...]
    out[:, width : 2 * width] = cotangent[...]


def down_kernel(count, hidden, *refs):
    kept = refs[:count]
    out, held, sems = refs[count:]
    half = kept[0].shape[0] // 2
    copies = []
    for batch in range(2):
        for k in range(count):
            copy = pltpu.make_async_copy(
                kept[k].at[batch * half : (batch + 1) * half, :],
                held.at[batch, k * half : (k + 1) * half, :],
                sems.at[batch, k],
            )
            copy.start()
            copies.append(copy)
    total = None
    for batch in range(2):
        for copy in copies[batch * count : (batch + 1) * count]:
            copy.wait()
        term = lax.dot_general(
            held[batch, :, :hidden],
            held[batch, :, hidden:],
            (((0,), (0,)), ((), ())),
            preferred_element_type=f32,
        )
        term = term.astype(bf16).astype(f32)
        total = term if total is None else total + term
    out[...] = total.astype(bf16)


def whole():
    return pl.BlockSpec(memory_space=pltpu.VMEM)


def scalar():
    return pl.BlockSpec(memory_space=pltpu.SMEM)


def dense_shards(tokens, cotangent, expert_ids, gate_probs, alpha, gamma, beta, w_in, w_down):
    experts = lax.axis_size("expert")
    planes = experts // 4
    block = tokens.shape[1]
    width = tokens.shape[2]
    hidden = w_down.shape[1]
    rows = 8 * block
    me = lax.axis_index("expert")

    def go_x(v):
        return lax.ppermute(v, "dp", [(0, 1), (1, 0)])

    def go_y(v):
        return lax.ppermute(v, "expert", [(e, e ^ 2) for e in range(experts)])

    def go_core(v):
        return lax.ppermute(v, "expert", [(e, e ^ 1) for e in range(experts)])

    def go_z(v):
        return lax.ppermute(v, "expert", [(e, (e + 4) % experts) for e in range(experts)])

    def go_jump(v, by):
        return lax.ppermute(v, "expert", [(e, e ^ by) for e in range(experts)])

    def go_far(v, by):
        pairs = [
            (2 * e + x, 2 * (e ^ by) + 1 - x) for e in range(experts) for x in range(2)
        ]
        return lax.ppermute(v, ("expert", "dp"), pairs)

    lanes = jnp.arange(LANES, dtype=jnp.int32)
    picks = expert_ids[0][:, :, None] == lanes[None, None, :]
    own = pl.pallas_call(
        pack_kernel,
        out_shape=jax.ShapeDtypeStruct((block, 2 * width + LANES), bf16),
        in_specs=[whole()] * 4,
        out_specs=whole(),
        name="pack",
    )(tokens[0], cotangent[0], expert_ids[0].T, gate_probs[0].T)

    flat_in = w_in[0].reshape(2 * hidden, width)
    flat_down = w_down[0]
    gamma_row = gamma.reshape(1, width)
    beta_row = beta.reshape(1, width)
    mine = me.reshape(1).astype(jnp.int32)
    half = width // 2
    side = lax.axis_index("dp").astype(jnp.int32)
    w_send = lax.dynamic_slice_in_dim(flat_in, (1 - side) * half, half, axis=1)

    segments = tuple(
        tuple((x * 4 + core * 2 + y) * block for x in range(2))
        for core in range(2)
        for y in range(2)
    )
    params = pltpu.CompilerParams(vmem_limit_bytes=14 << 20)

    def first_half(arrays):
        return pl.pallas_call(
            functools.partial(rows_kernel, segments, width, hidden),
            out_shape=(
                jax.ShapeDtypeStruct((rows, 2 * hidden), bf16),
                pltpu.HBM((rows, hidden + width), bf16),
                jax.ShapeDtypeStruct((rows, LANES), bf16),
            ),
            in_specs=[whole()] * 8 + [scalar(), scalar()],
            out_specs=(whole(), pl.BlockSpec(memory_space=pltpu.HBM), whole()),
            scratch_shapes=[
                pltpu.VMEM((rows, width), bf16),
                pltpu.VMEM((rows, width), bf16),
                pltpu.VMEM((rows, LANES), f32),
                pltpu.VMEM((rows, hidden + width), bf16),
                pltpu.SemaphoreType.DMA((2,)),
            ],
            compiler_params=params,
            name="rows",
        )(*arrays, flat_in, flat_down, gamma_row, beta_row, alpha, mine)

    def second_half(arrays, near, far, w_far, tail):
        return pl.pallas_call(
            functools.partial(grad_kernel, segments, half),
            out_shape=(
                jax.ShapeDtypeStruct((2, 2, block, half + LANES), bf16),
                jax.ShapeDtypeStruct((2, 2, block, half + LANES), bf16),
                jax.ShapeDtypeStruct((8, half), f32),
            ),
            in_specs=[whole()] * 9 + [scalar(), scalar()],
            out_specs=(whole(),) * 3,
            scratch_shapes=[
                pltpu.VMEM((rows, half), f32),
                pltpu.VMEM((rows, half), f32),
            ],
            compiler_params=params,
            name="grads",
        )(*arrays, near, far, flat_in, w_far, tail, alpha, side.reshape(1))

    fence = lax.optimization_barrier
    own = jnp.concatenate([own, go_x(own)], axis=0)
    near, far, near_c, far_c, w_far = {0: own}, {}, {}, {}, {}
    state = {"a": near, "b": far, "c": near_c, "d": far_c, "w": w_far}
    grads, kept, tails, other = {}, {}, {}, {}
    state.update(grads=grads, other=other)
    d_own, d_got, totals, sent, value = {}, {}, {}, {}, {}
    state.update(d_own=d_own, d_got=d_got, totals=totals, sent=sent, value=value)

    def make_down(held):
        return pl.pallas_call(
            functools.partial(down_kernel, planes, hidden),
            out_shape=jax.ShapeDtypeStruct((hidden, width), bf16),
            in_specs=[pl.BlockSpec(memory_space=pltpu.HBM)] * planes,
            out_specs=whole(),
            scratch_shapes=[
                pltpu.VMEM((2, planes * rows // 2, hidden + width), bf16),
                pltpu.SemaphoreType.DMA((2, planes)),
            ],
            compiler_params=pltpu.CompilerParams(vmem_limit_bytes=20 << 20),
            name="down",
        )(*[pltpu.with_memory_space_constraint(one, pltpu.HBM) for one in held])

    def step(*late):
        now = {
            name: {k: v for k, v in held.items() if (name, k) not in late}
            for name, held in state.items()
        }
        new = fence(now)
        for name, held in state.items():
            held.update(new[name])

    def rows_of(k):
        arrays = (near[k], far[k], near_c[k], far_c[k])
        grads[k], kept[k], tails[k] = first_half(arrays)

    def grads_of(k):
        arrays = (near[k], far[k], near_c[k], far_c[k])
        d_own[k], moved, totals[k] = second_half(arrays, grads[k], other[k], w_far[0], tails[k])
        d_got[k] = go_core(moved)

    def send_y(k):
        sent[k] = go_y(add16(d_own[k][:, 1], d_got[k][:, 1]))

    def total_of(k):
        kept = d_own[k][:, 0].astype(f32) + d_got[k][:, 0].astype(f32)
        return kept + sent[k].astype(f32)

    def hop(k):
        carried = total_of(k)
        if k > 1:
            carried = carried + value[k].astype(f32)
        value[(k + 1) % planes] = go_z(carried.astype(bf16))

    for k in range(3):
        near[k + 1] = go_z(near[k])
        far[k] = go_y(near[k])
        near_c[k] = go_core(near[k])
        if k == 0:
            w_send, near_c[0] = fence((w_send, near_c[0]))
            w_far[0] = go_x(w_send)
        else:
            far_c[k - 1] = go_core(far[k - 1])
            rows_of(k - 1)
        if k == 2:
            other[0] = go_x(grads[0])
        step(*([("w", 0)] if k < 2 else []))
    other[1] = go_x(grads[1])
    far[3] = go_y(near[3])
    near_c[3] = go_core(near[3])
    far_c[2] = go_core(far[2])
    rows_of(2)
    grads_of(0)
    step()
    other[2] = go_x(grads[2])
    far_c[3] = go_core(far[3])
    send_y(0)
    rows_of(3)
    other[1], grads[3] = fence((other[1], grads[3]))
    grads_of(1)
    step(("sent", 0))
    other[3] = go_x(grads[3])
    send_y(1)
    other[2], sent[1] = fence((other[2], sent[1]))
    grads_of(2)
    hop(1)
    send_y(2)
    step(("sent", 2), ("value", 2))
    grads_of(3)
    hop(2)
    pool = {}
    pool[0] = sum(totals[k] for k in range(1, planes)) + totals[0]
    pool[0] = pool[0] + go_core(pool[0])
    state["pool"] = pool
    step(("value", 3), ("sent", 2), ("value", 2))
    send_y(3)
    part = pool[0]
    mine_sums = part + go_y(part)
    cross_sums = go_x(part) + go_far(part, 2)
    pool[0] = jnp.concatenate([mine_sums, cross_sums], axis=0)
    step(("pool", 0))
    hop(3)
    kept[3], value[3] = fence((kept[3], value[3]))
    down = {0: make_down([kept[k] for k in range(planes)])}
    state["down"] = down
    pool[0] = pool[0] + go_jump(pool[0], 4)
    step()
    final = total_of(0) + value[0].astype(f32)
    crossed = go_x(final[1].astype(bf16)).astype(f32)
    left = jnp.where(side == 0, final[0, :, :half], crossed[:, :half])
    right = jnp.where(side == 0, crossed[:, :half], final[0, :, :half])
    grad_normed = jnp.concatenate([left, right], axis=1)
    row_grads = final[0, :, half:] + crossed[:, half:]
    grad_down = down[0]
    sums = pool[0] + go_jump(pool[0], 8)
    mine_sums, cross_sums = sums[:8], sums[8:]
    sums = jnp.concatenate(
        [
            jnp.where(side == 0, mine_sums, cross_sums),
            jnp.where(side == 0, cross_sums, mine_sums),
        ],
        axis=1,
    )

    inputs = tokens[0].astype(f32)
    squashed = jnp.tanh(alpha[0] * inputs)
    pre_grad = grad_normed * gamma * (1.0 - squashed * squashed)
    grad_tokens = (cotangent[0].astype(f32) + alpha[0] * pre_grad).astype(bf16)
    grad_probs = jnp.sum(jnp.where(picks, row_grads[:, None, :], 0.0), axis=2).astype(bf16)
    grad_beta = sums[0]
    grad_gamma = sums[1]
    grad_alpha = jnp.sum(sums[2] * gamma).reshape(1)
    return (
        grad_tokens[None],
        grad_probs[None],
        grad_down[None],
        grad_gamma,
        grad_beta,
        grad_alpha,
    )


def slot_layout(ids_local, expert_count, capacity):
    token_count, top_count = ids_local.shape
    labels = jnp.arange(expert_count, dtype=jnp.int32)
    onehot = (ids_local[:, :, None] == labels[None, None, :]).astype(jnp.int32)
    picks = jnp.sum(onehot, axis=1)
    order = jnp.arange(token_count, dtype=jnp.int32)
    earlier = (order[None, :] < order[:, None]).astype(f32)
    before = jnp.dot(earlier, picks.astype(f32), precision=lax.Precision.HIGHEST)
    slots = jnp.sum(onehot * before.astype(jnp.int32)[:, None, :], axis=2)
    position = ids_local * capacity + slots
    pairs = jnp.arange(token_count * top_count, dtype=jnp.int32)
    table = jnp.full((expert_count * capacity,), token_count * top_count, jnp.int32)
    table = table.at[position.reshape(-1)].set(pairs)
    return (position, table)


def routed_shards(tokens, cotangent, expert_ids, gate_probs, alpha, gamma, beta, w_in, w_down):
    expert_count = lax.axis_size("expert")
    token_count = tokens.shape[1]
    top_count = expert_ids.shape[2]
    width = tokens.shape[2]
    capacity = 3 * token_count * top_count // (2 * expert_count)
    rows_total = expert_count * capacity
    inputs = tokens[0].astype(jnp.float32)
    squashed = jnp.tanh(alpha[0] * inputs)
    normed = (gamma * squashed + beta).astype(jnp.bfloat16)
    position, table = slot_layout(expert_ids[0], expert_count, capacity)
    source_token = table // top_count
    zero_row = jnp.zeros((1, width), jnp.bfloat16)
    normed_pad = jnp.concatenate([normed, zero_row], axis=0)
    cot_pad = jnp.concatenate([cotangent[0], zero_row], axis=0)
    prob_pad = jnp.concatenate([gate_probs[0].reshape(-1), jnp.zeros((1,), jnp.bfloat16)], axis=0)
    send_rows = normed_pad[source_token].reshape(expert_count, capacity, width)
    send_cot = cot_pad[source_token].reshape(expert_count, capacity, width)
    send_prob = prob_pad[table].reshape(expert_count, capacity)

    def swap(value):
        return lax.all_to_all(value, "expert", split_axis=0, concat_axis=0, tiled=True)

    in_rows = swap(send_rows).reshape(rows_total, width)
    cot_rows = swap(send_cot).reshape(rows_total, width)
    prob_rows = swap(send_prob).reshape(rows_total).astype(jnp.float32)
    gate_up = lax.all_gather(w_in, "dp", axis=2, tiled=True)
    w_lower = lax.all_gather(w_down, "dp", axis=1, tiled=True)[0]
    w_gate = gate_up[0, 0]
    w_upper = gate_up[0, 1]
    gate_pre = contract_width(in_rows, w_gate)
    up_value = contract_width(in_rows, w_upper)
    sigma = jax.nn.sigmoid(gate_pre)
    activation = (gate_pre * sigma * up_value).astype(jnp.bfloat16)
    back = contract_width(cot_rows, w_lower)
    weight_row = residual_scale * prob_rows
    scaled_cot = (weight_row[:, None] * cot_rows.astype(jnp.float32)).astype(jnp.bfloat16)
    row_grad = residual_scale * jnp.sum(activation.astype(jnp.float32) * back, axis=1)
    d_act = weight_row[:, None] * back
    d_gate = (d_act * up_value * sigma * (1.0 + gate_pre * (1.0 - sigma))).astype(jnp.bfloat16)
    d_up = (d_act * gate_pre * sigma).astype(jnp.bfloat16)
    d_rows = (
        jnp.dot(d_gate, w_gate, preferred_element_type=jnp.float32)
        + jnp.dot(d_up, w_upper, preferred_element_type=jnp.float32)
    ).astype(jnp.bfloat16)
    back_rows = swap(d_rows.reshape(expert_count, capacity, width))
    back_probs = swap(row_grad.astype(jnp.bfloat16).reshape(expert_count, capacity))
    partial_grad = lax.dot_general(
        activation, scaled_cot, (((0,), (0,)), ((), ())), preferred_element_type=jnp.float32
    )
    grad_down = lax.psum_scatter(
        partial_grad[None].astype(jnp.bfloat16), "dp", scatter_dimension=1, tiled=True
    )
    picked = back_rows.reshape(rows_total, width)[position]
    grad_normed = jnp.sum(picked.astype(jnp.float32), axis=1)
    grad_probs = back_probs.reshape(rows_total)[position]
    gamma_part = jnp.sum(grad_normed * squashed, axis=0)
    beta_part = jnp.sum(grad_normed, axis=0)
    pre_grad = grad_normed * gamma * (1.0 - squashed * squashed)
    alpha_part = jnp.sum(pre_grad * inputs).reshape(1)
    grad_gamma, grad_beta, grad_alpha = lax.psum(
        (gamma_part, beta_part, alpha_part), ("expert", "dp")
    )
    grad_tokens = (cotangent[0].astype(jnp.float32) + alpha[0] * pre_grad).astype(jnp.bfloat16)
    return (grad_tokens[None], grad_probs[None], grad_down, grad_gamma, grad_beta, grad_alpha)


def shards(*arrays):
    experts = lax.axis_size("expert")
    top_count = arrays[2].shape[2]
    dense = (
        lax.axis_size("dp") == 2
        and experts == 16
        and 2 * top_count >= experts
        and arrays[0].shape[2] % 2048 == 0
    )
    return (dense_shards if dense else routed_shards)(*arrays)


def solution(mesh):
    placed = (
        P("dp", "expert", None),
        P("dp", "expert", None),
        P("dp", "expert", None),
        P("dp", "expert", None),
        P(),
        P(),
        P(),
        P("expert", None, "dp", None),
        P("expert", "dp", None),
    )
    return jax.shard_map(
        shards,
        mesh=mesh,
        in_specs=placed,
        out_specs=(
            P("dp", "expert", None),
            P("dp", "expert", None),
            P("expert", "dp", None),
            P(),
            P(),
            P(),
        ),
        check_vma=False,
    )
```

```python
import functools
import jax
import jax.numpy as jnp
from jax import lax
from jax.experimental import pallas as pl
from jax.experimental.pallas import tpu as pltpu
from jax.sharding import PartitionSpec as P

residual_scale = 0.7071
LANES = 128
f32 = jnp.float32
bf16 = jnp.bfloat16


def contract_width(left, right):
    return lax.dot_general(
        left, right, (((1,), (1,)), ((), ())), preferred_element_type=f32
    )


def add16(left, right):
    return (left.astype(f32) + right.astype(f32)).astype(bf16)


def one_hot(spot, slots):
    label = lax.broadcasted_iota(jnp.int32, (spot.shape[0], slots), 1).astype(f32)
    return jnp.where(label == spot[:, 0:1], 1.0, 0.0).astype(bf16)


def rows_kernel(segments, width, hidden, *refs):
    count = len(segments)
    blocks = refs[:count]
    (w_in, w_down, gamma, beta, alpha, expert) = refs[count : count + 6]
    (grads_out, packed_out, spot_out, kept_out, tail_out) = refs[count + 6 : count + 11]
    (normed, cot, weight, kept, sems) = refs[count + 11 :]
    rows = normed.shape[0]
    gain = alpha[0]
    mine = expert[0]
    gamma_row = gamma[...]
    beta_row = beta[...]
    for source, places in zip(blocks, segments):
        size = source.shape[0] // len(places)
        for part, to in enumerate(places):
            here, there = slice(part * size, (part + 1) * size), slice(to, to + size)
            squashed = jnp.tanh(gain * source[here, 0:width].astype(f32))
            normed[there, :] = (gamma_row * squashed + beta_row).astype(bf16)
            rows_cot = source[here, width : 2 * width]
            cot[there, :] = rows_cot
            gates = source[here, 2 * width :].astype(f32)
            lane = lax.broadcasted_iota(jnp.int32, gates.shape, 1)
            own = jnp.sum(jnp.where(lane == mine, gates, 0.0), axis=1, keepdims=True)
            own = residual_scale * own
            weight[there, :] = jnp.broadcast_to(own, (size, LANES))
            kept[there, hidden:] = (own * rows_cot.astype(f32)).astype(bf16)
    wide = slice(hidden, hidden + width)
    save_cot = pltpu.make_async_copy(kept.at[:, wide], kept_out.at[:, wide], sems.at[0])
    save_cot.start()
    pre = contract_width(normed[...], w_in[...])
    back = contract_width(cot[...], w_down[...])
    gate_pre = pre[:, :hidden]
    up_value = pre[:, hidden:]
    sigma = jax.nn.sigmoid(gate_pre)
    silu = gate_pre * sigma
    activation = (silu * up_value).astype(bf16)
    kept[:, :hidden] = activation
    save_act = pltpu.make_async_copy(
        kept.at[:, :hidden], kept_out.at[:, :hidden], sems.at[1]
    )
    save_act.start()
    row_grad = residual_scale * jnp.sum(activation.astype(f32) * back, axis=1, keepdims=True)
    d_act = weight[:, 0:1] * back
    d_gate = d_act * up_value * sigma * (1.0 + gate_pre * (1.0 - sigma))
    grads_out[:, :hidden] = d_gate.astype(bf16)
    grads_out[:, hidden:] = (d_act * gate_pre * sigma).astype(bf16)
    routed = weight[...] > 0.0
    block = rows // 8
    row = lax.broadcasted_iota(jnp.int32, (rows, rows), 0)
    column = lax.broadcasted_iota(jnp.int32, (rows, rows), 1)
    earlier = (column < row) & (column >= row - lax.rem(row, block))
    count_before = jnp.dot(
        jnp.where(earlier, 1.0, 0.0).astype(bf16),
        jnp.where(routed, 1.0, 0.0).astype(bf16),
        preferred_element_type=f32,
    )
    slots = packed_out.shape[0] // 8
    row = lax.broadcasted_iota(jnp.int32, (rows, LANES), 0)
    base = (lax.div(row, block) * slots).astype(f32)
    spot = jnp.where(routed, base + count_before, -1.0)
    spot_out[...] = spot
    packed_out[...] = lax.dot_general(
        one_hot(spot, 8 * slots), grads_out[...], (((0,), (0,)), ((), ())),
        preferred_element_type=f32,
    ).astype(bf16)
    lane = lax.broadcasted_iota(jnp.int32, (rows, LANES), 1)
    tail_out[...] = jnp.where(lane == mine, row_grad, 0.0).astype(bf16)
    save_cot.wait()
    save_act.wait()


def grad_kernel(segments, half, *refs):
    count = len(segments)
    blocks = refs[:count]
    (near, far, spot, w_in, w_far, tail, alpha, side) = refs[count : count + 8]
    (d_own, d_other, sums, squash, slope) = refs[count + 8 :]
    rows = near.shape[0]
    block = rows // 8
    gain = alpha[0]
    start = pl.multiple_of(side[0] * half, half)
    for source, places in zip(blocks, segments):
        size = source.shape[0] // len(places)
        for part, to in enumerate(places):
            inputs = source[part * size : (part + 1) * size, pl.ds(start, half)].astype(f32)
            squashed = jnp.tanh(gain * inputs)
            squash[to : to + size, :] = squashed
            slope[to : to + size, :] = (1.0 - squashed * squashed) * inputs
    slots = far.shape[0]
    mirrored = jnp.concatenate([far[slots // 2 :, :], far[: slots // 2, :]], axis=0)
    mirrored = jnp.dot(
        one_hot(spot[...], slots), mirrored, preferred_element_type=f32
    ).astype(bf16)

    def place(cols, value):
        for x in range(2):
            for y in range(2):
                row = (x * 4 + y) * block
                d_own[x, y, :, cols] = value[row : row + block]
                row = (x * 4 + 2 + y) * block
                d_other[x, y, :, cols] = value[row : row + block]

    place(slice(half, half + LANES), tail[...])
    step = 512
    for at in range(0, half, step):
        cols = slice(at, at + step)
        part = jnp.dot(
            near[...],
            w_in[:, pl.ds(pl.multiple_of(start + at, step), step)],
            preferred_element_type=f32,
        )
        part = part + jnp.dot(mirrored, w_far[:, cols], preferred_element_type=f32)
        short = part.astype(bf16)
        place(cols, short)
        part = short.astype(f32)
        sums[0:1, cols] = jnp.sum(part, axis=0, keepdims=True)
        sums[1:2, cols] = jnp.sum(part * squash[:, cols], axis=0, keepdims=True)
        sums[2:3, cols] = jnp.sum(part * slope[:, cols], axis=0, keepdims=True)
        sums[3:8, cols] = jnp.zeros((5, step), f32)


def pack_kernel(tokens, cotangent, ids, probs, out):
    width = tokens.shape[1]
    top, block = ids.shape
    names = ids[...]
    shares = probs[...].astype(f32)
    label = lax.broadcasted_iota(jnp.int32, (LANES, block), 0)
    table = jnp.zeros((LANES, block), f32)
    for k in range(top):
        table = table + jnp.where(label == names[k : k + 1, :], shares[k : k + 1, :], 0.0)
    row = lax.broadcasted_iota(jnp.int32, (block, block), 0)
    column = lax.broadcasted_iota(jnp.int32, (block, block), 1)
    unit = jnp.where(row == column, 1.0, 0.0).astype(bf16)
    out[:, 2 * width :] = contract_width(unit, table.astype(bf16)).astype(bf16)
    out[:, :width] = tokens[...]
    out[:, width : 2 * width] = cotangent[...]


def join_kernel(first, second, out):
    size = first.shape[0]
    out[:size, :] = first[...]
    out[size:, :] = second[...]


def down_kernel(count, hidden, *refs):
    kept = refs[:count]
    out, held, sems = refs[count:]
    half = kept[0].shape[0] // 2
    copies = []
    for batch in range(2):
        for k in range(count):
            copy = pltpu.make_async_copy(
                kept[k].at[batch * half : (batch + 1) * half, :],
                held.at[batch, k * half : (k + 1) * half, :],
                sems.at[batch, k],
            )
            copy.start()
            copies.append(copy)
    total = None
    for batch in range(2):
        for copy in copies[batch * count : (batch + 1) * count]:
            copy.wait()
        term = lax.dot_general(
            held[batch, :, :hidden],
            held[batch, :, hidden:],
            (((0,), (0,)), ((), ())),
            preferred_element_type=f32,
        )
        term = term.astype(bf16).astype(f32)
        total = term if total is None else total + term
    out[...] = total.astype(bf16)


def whole():
    return pl.BlockSpec(memory_space=pltpu.VMEM)


def scalar():
    return pl.BlockSpec(memory_space=pltpu.SMEM)


def dense_shards(tokens, cotangent, expert_ids, gate_probs, alpha, gamma, beta, w_in, w_down):
    experts = lax.axis_size("expert")
    planes = experts // 4
    block = tokens.shape[1]
    width = tokens.shape[2]
    hidden = w_down.shape[1]
    rows = 8 * block
    slots = 3 * block * expert_ids.shape[2] // (2 * experts)
    me = lax.axis_index("expert")

    def go_x(v):
        return lax.ppermute(v, "dp", [(0, 1), (1, 0)])

    def go_y(v):
        return lax.ppermute(v, "expert", [(e, e ^ 2) for e in range(experts)])

    def go_core(v):
        return lax.ppermute(v, "expert", [(e, e ^ 1) for e in range(experts)])

    def go_z(v):
        return lax.ppermute(v, "expert", [(e, (e + 4) % experts) for e in range(experts)])

    def go_jump(v, by):
        return lax.ppermute(v, "expert", [(e, e ^ by) for e in range(experts)])

    def go_far(v, by):
        pairs = [
            (2 * e + x, 2 * (e ^ by) + 1 - x) for e in range(experts) for x in range(2)
        ]
        return lax.ppermute(v, ("expert", "dp"), pairs)

    lanes = jnp.arange(LANES, dtype=jnp.int32)
    picks = expert_ids[0][:, :, None] == lanes[None, None, :]
    own = pl.pallas_call(
        pack_kernel,
        out_shape=jax.ShapeDtypeStruct((block, 2 * width + LANES), bf16),
        in_specs=[whole()] * 4,
        out_specs=whole(),
        name="pack",
    )(tokens[0], cotangent[0], expert_ids[0].T, gate_probs[0].T)

    flat_in = w_in[0].reshape(2 * hidden, width)
    flat_down = w_down[0]
    gamma_row = gamma.reshape(1, width)
    beta_row = beta.reshape(1, width)
    mine = me.reshape(1).astype(jnp.int32)
    half = width // 2
    side = lax.axis_index("dp").astype(jnp.int32)
    w_send = lax.dynamic_slice_in_dim(flat_in, (1 - side) * half, half, axis=1)

    segments = tuple(
        tuple((x * 4 + core * 2 + y) * block for x in range(2))
        for core in range(2)
        for y in range(2)
    )
    params = pltpu.CompilerParams(vmem_limit_bytes=14 << 20)

    def first_half(arrays):
        return pl.pallas_call(
            functools.partial(rows_kernel, segments, width, hidden),
            out_shape=(
                jax.ShapeDtypeStruct((rows, 2 * hidden), bf16),
                jax.ShapeDtypeStruct((8 * slots, 2 * hidden), bf16),
                jax.ShapeDtypeStruct((rows, LANES), f32),
                pltpu.HBM((rows, hidden + width), bf16),
                jax.ShapeDtypeStruct((rows, LANES), bf16),
            ),
            in_specs=[whole()] * 8 + [scalar(), scalar()],
            out_specs=(whole(),) * 3 + (pl.BlockSpec(memory_space=pltpu.HBM), whole()),
            scratch_shapes=[
                pltpu.VMEM((rows, width), bf16),
                pltpu.VMEM((rows, width), bf16),
                pltpu.VMEM((rows, LANES), f32),
                pltpu.VMEM((rows, hidden + width), bf16),
                pltpu.SemaphoreType.DMA((2,)),
            ],
            compiler_params=params,
            name="rows",
        )(*arrays, flat_in, flat_down, gamma_row, beta_row, alpha, mine)

    def second_half(arrays, near, far, spot, w_far, tail):
        return pl.pallas_call(
            functools.partial(grad_kernel, segments, half),
            out_shape=(
                jax.ShapeDtypeStruct((2, 2, block, half + LANES), bf16),
                jax.ShapeDtypeStruct((2, 2, block, half + LANES), bf16),
                jax.ShapeDtypeStruct((8, half), f32),
            ),
            in_specs=[whole()] * 10 + [scalar(), scalar()],
            out_specs=(whole(),) * 3,
            scratch_shapes=[
                pltpu.VMEM((rows, half), f32),
                pltpu.VMEM((rows, half), f32),
            ],
            compiler_params=params,
            name="grads",
        )(*arrays, near, far, spot, flat_in, w_far, tail, alpha, side.reshape(1))

    fence = lax.optimization_barrier
    own = pl.pallas_call(
        join_kernel,
        out_shape=jax.ShapeDtypeStruct((2 * block, 2 * width + LANES), bf16),
        in_specs=[whole()] * 2,
        out_specs=whole(),
        name="join",
    )(own, go_x(own))
    near, far, near_c, far_c, w_far = {0: own}, {}, {}, {}, {}
    state = {"a": near, "b": far, "c": near_c, "d": far_c, "w": w_far}
    grads, kept, tails, other, packed, spots = {}, {}, {}, {}, {}, {}
    state.update(grads=grads, other=other, packed=packed)
    d_own, d_got, totals, sent, value = {}, {}, {}, {}, {}
    state.update(d_own=d_own, d_got=d_got, totals=totals, sent=sent, value=value)

    def make_down(held):
        return pl.pallas_call(
            functools.partial(down_kernel, planes, hidden),
            out_shape=jax.ShapeDtypeStruct((hidden, width), bf16),
            in_specs=[pl.BlockSpec(memory_space=pltpu.HBM)] * planes,
            out_specs=whole(),
            scratch_shapes=[
                pltpu.VMEM((2, planes * rows // 2, hidden + width), bf16),
                pltpu.SemaphoreType.DMA((2, planes)),
            ],
            compiler_params=pltpu.CompilerParams(vmem_limit_bytes=20 << 20),
            name="down",
        )(*[pltpu.with_memory_space_constraint(one, pltpu.HBM) for one in held])

    def step(*late):
        now = {
            name: {k: v for k, v in held.items() if (name, k) not in late}
            for name, held in state.items()
        }
        new = fence(now)
        for name, held in state.items():
            held.update(new[name])

    def rows_of(k):
        arrays = (near[k], far[k], near_c[k], far_c[k])
        grads[k], packed[k], spots[k], kept[k], tails[k] = first_half(arrays)

    def grads_of(k):
        arrays = (near[k], far[k], near_c[k], far_c[k])
        d_own[k], moved, totals[k] = second_half(
            arrays, grads[k], other[k], spots[k], w_far[0], tails[k]
        )
        d_got[k] = go_core(moved)

    def send_y(k):
        sent[k] = go_y(add16(d_own[k][:, 1], d_got[k][:, 1]))

    def total_of(k):
        kept = d_own[k][:, 0].astype(f32) + d_got[k][:, 0].astype(f32)
        return kept + sent[k].astype(f32)

    def hop(k):
        carried = total_of(k)
        if k > 1:
            carried = carried + value[k].astype(f32)
        value[(k + 1) % planes] = go_z(carried.astype(bf16))

    for k in range(3):
        near[k + 1] = go_z(near[k])
        far[k] = go_y(near[k])
        near_c[k] = go_core(near[k])
        if k == 0:
            w_send, near_c[0] = fence((w_send, near_c[0]))
            w_far[0] = go_x(w_send)
        else:
            far_c[k - 1] = go_core(far[k - 1])
            rows_of(k - 1)
        if k == 2:
            other[0] = go_x(packed[0])
        step(*([("w", 0)] if k < 2 else []))
    other[1] = go_x(packed[1])
    far[3] = go_y(near[3])
    near_c[3] = go_core(near[3])
    far_c[2] = go_core(far[2])
    rows_of(2)
    grads_of(0)
    step()
    other[2] = go_x(packed[2])
    far_c[3] = go_core(far[3])
    rows_of(3)
    other[1], packed[3] = fence((other[1], packed[3]))
    grads_of(1)
    step()
    other[3] = go_x(packed[3])
    send_y(1)
    other[2], sent[1] = fence((other[2], sent[1]))
    grads_of(2)
    hop(1)
    send_y(2)
    step(("sent", 2), ("value", 2))
    grads_of(3)
    hop(2)
    pool = {}
    pool[0] = sum(totals[k] for k in range(1, planes)) + totals[0]
    pool[0] = pool[0] + go_core(pool[0])
    state["pool"] = pool
    step(("value", 3), ("sent", 2), ("value", 2))
    send_y(3)
    part = pool[0]
    mine_sums = part + go_y(part)
    cross_sums = go_x(part) + go_far(part, 2)
    pool[0] = jnp.concatenate([mine_sums, cross_sums], axis=0)
    step(("pool", 0))
    hop(3)
    send_y(0)
    pool[0] = pool[0] + go_jump(pool[0], 4)
    step()
    kept[3], pool[0] = fence((kept[3], pool[0]))
    final = total_of(0) + value[0].astype(f32)
    crossed = go_x(final[1].astype(bf16)).astype(f32)
    left = jnp.where(side == 0, final[0, :, :half], crossed[:, :half])
    right = jnp.where(side == 0, crossed[:, :half], final[0, :, :half])
    grad_normed = jnp.concatenate([left, right], axis=1)
    row_grads = final[0, :, half:] + crossed[:, half:]
    grad_down = make_down([kept[k] for k in range(planes)])
    sums = pool[0] + go_jump(pool[0], 8)
    mine_sums, cross_sums = sums[:8], sums[8:]
    sums = jnp.concatenate(
        [
            jnp.where(side == 0, mine_sums, cross_sums),
            jnp.where(side == 0, cross_sums, mine_sums),
        ],
        axis=1,
    )

    inputs = tokens[0].astype(f32)
    squashed = jnp.tanh(alpha[0] * inputs)
    pre_grad = grad_normed * gamma * (1.0 - squashed * squashed)
    grad_tokens = (cotangent[0].astype(f32) + alpha[0] * pre_grad).astype(bf16)
    grad_probs = jnp.sum(jnp.where(picks, row_grads[:, None, :], 0.0), axis=2).astype(bf16)
    grad_beta = sums[0]
    grad_gamma = sums[1]
    grad_alpha = jnp.sum(sums[2] * gamma).reshape(1)
    return (
        grad_tokens[None],
        grad_probs[None],
        grad_down[None],
        grad_gamma,
        grad_beta,
        grad_alpha,
    )


def slot_layout(ids_local, expert_count, capacity):
    token_count, top_count = ids_local.shape
    labels = jnp.arange(expert_count, dtype=jnp.int32)
    onehot = (ids_local[:, :, None] == labels[None, None, :]).astype(jnp.int32)
    picks = jnp.sum(onehot, axis=1)
    order = jnp.arange(token_count, dtype=jnp.int32)
    earlier = (order[None, :] < order[:, None]).astype(f32)
    before = jnp.dot(earlier, picks.astype(f32), precision=lax.Precision.HIGHEST)
    slots = jnp.sum(onehot * before.astype(jnp.int32)[:, None, :], axis=2)
    position = ids_local * capacity + slots
    pairs = jnp.arange(token_count * top_count, dtype=jnp.int32)
    table = jnp.full((expert_count * capacity,), token_count * top_count, jnp.int32)
    table = table.at[position.reshape(-1)].set(pairs)
    return (position, table)


def routed_shards(tokens, cotangent, expert_ids, gate_probs, alpha, gamma, beta, w_in, w_down):
    expert_count = lax.axis_size("expert")
    token_count = tokens.shape[1]
    top_count = expert_ids.shape[2]
    width = tokens.shape[2]
    capacity = 3 * token_count * top_count // (2 * expert_count)
    rows_total = expert_count * capacity
    inputs = tokens[0].astype(jnp.float32)
    squashed = jnp.tanh(alpha[0] * inputs)
    normed = (gamma * squashed + beta).astype(jnp.bfloat16)
    position, table = slot_layout(expert_ids[0], expert_count, capacity)
    source_token = table // top_count
    zero_row = jnp.zeros((1, width), jnp.bfloat16)
    normed_pad = jnp.concatenate([normed, zero_row], axis=0)
    cot_pad = jnp.concatenate([cotangent[0], zero_row], axis=0)
    prob_pad = jnp.concatenate([gate_probs[0].reshape(-1), jnp.zeros((1,), jnp.bfloat16)], axis=0)
    send_rows = normed_pad[source_token].reshape(expert_count, capacity, width)
    send_cot = cot_pad[source_token].reshape(expert_count, capacity, width)
    send_prob = prob_pad[table].reshape(expert_count, capacity)

    def swap(value):
        return lax.all_to_all(value, "expert", split_axis=0, concat_axis=0, tiled=True)

    in_rows = swap(send_rows).reshape(rows_total, width)
    cot_rows = swap(send_cot).reshape(rows_total, width)
    prob_rows = swap(send_prob).reshape(rows_total).astype(jnp.float32)
    gate_up = lax.all_gather(w_in, "dp", axis=2, tiled=True)
    w_lower = lax.all_gather(w_down, "dp", axis=1, tiled=True)[0]
    w_gate = gate_up[0, 0]
    w_upper = gate_up[0, 1]
    gate_pre = contract_width(in_rows, w_gate)
    up_value = contract_width(in_rows, w_upper)
    sigma = jax.nn.sigmoid(gate_pre)
    activation = (gate_pre * sigma * up_value).astype(jnp.bfloat16)
    back = contract_width(cot_rows, w_lower)
    weight_row = residual_scale * prob_rows
    scaled_cot = (weight_row[:, None] * cot_rows.astype(jnp.float32)).astype(jnp.bfloat16)
    row_grad = residual_scale * jnp.sum(activation.astype(jnp.float32) * back, axis=1)
    d_act = weight_row[:, None] * back
    d_gate = (d_act * up_value * sigma * (1.0 + gate_pre * (1.0 - sigma))).astype(jnp.bfloat16)
    d_up = (d_act * gate_pre * sigma).astype(jnp.bfloat16)
    d_rows = (
        jnp.dot(d_gate, w_gate, preferred_element_type=jnp.float32)
        + jnp.dot(d_up, w_upper, preferred_element_type=jnp.float32)
    ).astype(jnp.bfloat16)
    back_rows = swap(d_rows.reshape(expert_count, capacity, width))
    back_probs = swap(row_grad.astype(jnp.bfloat16).reshape(expert_count, capacity))
    partial_grad = lax.dot_general(
        activation, scaled_cot, (((0,), (0,)), ((), ())), preferred_element_type=jnp.float32
    )
    grad_down = lax.psum_scatter(
        partial_grad[None].astype(jnp.bfloat16), "dp", scatter_dimension=1, tiled=True
    )
    picked = back_rows.reshape(rows_total, width)[position]
    grad_normed = jnp.sum(picked.astype(jnp.float32), axis=1)
    grad_probs = back_probs.reshape(rows_total)[position]
    gamma_part = jnp.sum(grad_normed * squashed, axis=0)
    beta_part = jnp.sum(grad_normed, axis=0)
    pre_grad = grad_normed * gamma * (1.0 - squashed * squashed)
    alpha_part = jnp.sum(pre_grad * inputs).reshape(1)
    grad_gamma, grad_beta, grad_alpha = lax.psum(
        (gamma_part, beta_part, alpha_part), ("expert", "dp")
    )
    grad_tokens = (cotangent[0].astype(jnp.float32) + alpha[0] * pre_grad).astype(jnp.bfloat16)
    return (grad_tokens[None], grad_probs[None], grad_down, grad_gamma, grad_beta, grad_alpha)


def shards(*arrays):
    experts = lax.axis_size("expert")
    top_count = arrays[2].shape[2]
    dense = (
        lax.axis_size("dp") == 2
        and experts == 16
        and arrays[0].shape[1] == 32
        and top_count == 8
        and 2 * top_count >= experts
        and arrays[0].shape[2] % 2048 == 0
    )
    return (dense_shards if dense else routed_shards)(*arrays)


def solution(mesh):
    placed = (
        P("dp", "expert", None),
        P("dp", "expert", None),
        P("dp", "expert", None),
        P("dp", "expert", None),
        P(),
        P(),
        P(),
        P("expert", None, "dp", None),
        P("expert", "dp", None),
    )
    return jax.shard_map(
        shards,
        mesh=mesh,
        in_specs=placed,
        out_specs=(
            P("dp", "expert", None),
            P("dp", "expert", None),
            P("expert", "dp", None),
            P(),
            P(),
            P(),
        ),
        check_vma=False,
    )
```

```python
import functools
import jax
import jax.numpy as jnp
from jax import lax
from jax.experimental import pallas as pl
from jax.experimental.pallas import tpu as pltpu
from jax.sharding import PartitionSpec as P

residual_scale = 0.7071
LANES = 128
f32 = jnp.float32
bf16 = jnp.bfloat16


def contract_width(left, right):
    return lax.dot_general(
        left, right, (((1,), (1,)), ((), ())), preferred_element_type=f32
    )


def add16(left, right):
    return (left.astype(f32) + right.astype(f32)).astype(bf16)


def one_hot(spot, slots):
    label = lax.broadcasted_iota(jnp.int32, (spot.shape[0], slots), 1).astype(f32)
    return jnp.where(label == spot[:, 0:1], 1.0, 0.0).astype(bf16)


def rows_kernel(segments, width, hidden, *refs):
    count = len(segments)
    blocks = refs[:count]
    (w_in, w_down, gamma, beta, alpha, expert) = refs[count : count + 6]
    (grads_out, packed_out, spot_out, kept_out, tail_out) = refs[count + 6 : count + 11]
    (normed, cot, weight, kept, sems) = refs[count + 11 :]
    rows = normed.shape[0]
    gain = alpha[0]
    mine = expert[0]
    gamma_row = gamma[...]
    beta_row = beta[...]
    for source, places in zip(blocks, segments):
        size = source.shape[0] // len(places)
        for part, to in enumerate(places):
            here, there = slice(part * size, (part + 1) * size), slice(to, to + size)
            squashed = jnp.tanh(gain * source[here, 0:width].astype(f32))
            normed[there, :] = (gamma_row * squashed + beta_row).astype(bf16)
            rows_cot = source[here, width : 2 * width]
            cot[there, :] = rows_cot
            gates = source[here, 2 * width :].astype(f32)
            lane = lax.broadcasted_iota(jnp.int32, gates.shape, 1)
            own = jnp.sum(jnp.where(lane == mine, gates, 0.0), axis=1, keepdims=True)
            own = residual_scale * own
            weight[there, :] = jnp.broadcast_to(own, (size, LANES))
            kept[there, hidden:] = (own * rows_cot.astype(f32)).astype(bf16)
    wide = slice(hidden, hidden + width)
    save_cot = pltpu.make_async_copy(kept.at[:, wide], kept_out.at[:, wide], sems.at[0])
    save_cot.start()
    pre = contract_width(normed[...], w_in[...])
    back = contract_width(cot[...], w_down[...])
    gate_pre = pre[:, :hidden]
    up_value = pre[:, hidden:]
    sigma = jax.nn.sigmoid(gate_pre)
    silu = gate_pre * sigma
    activation = (silu * up_value).astype(bf16)
    kept[:, :hidden] = activation
    save_act = pltpu.make_async_copy(
        kept.at[:, :hidden], kept_out.at[:, :hidden], sems.at[1]
    )
    save_act.start()
    row_grad = residual_scale * jnp.sum(activation.astype(f32) * back, axis=1, keepdims=True)
    d_act = weight[:, 0:1] * back
    d_gate = d_act * up_value * sigma * (1.0 + gate_pre * (1.0 - sigma))
    grads_out[:, :hidden] = d_gate.astype(bf16)
    grads_out[:, hidden:] = (d_act * gate_pre * sigma).astype(bf16)
    routed = weight[...] > 0.0
    block = rows // 8
    row = lax.broadcasted_iota(jnp.int32, (rows, rows), 0)
    column = lax.broadcasted_iota(jnp.int32, (rows, rows), 1)
    earlier = (column < row) & (column >= row - lax.rem(row, block))
    count_before = jnp.dot(
        jnp.where(earlier, 1.0, 0.0).astype(bf16),
        jnp.where(routed, 1.0, 0.0).astype(bf16),
        preferred_element_type=f32,
    )
    slots = packed_out.shape[0] // 8
    row = lax.broadcasted_iota(jnp.int32, (rows, LANES), 0)
    base = (lax.div(row, block) * slots).astype(f32)
    spot = jnp.where(routed, base + count_before, -1.0)
    spot_out[...] = spot
    packed_out[...] = lax.dot_general(
        one_hot(spot, 8 * slots), grads_out[...], (((0,), (0,)), ((), ())),
        preferred_element_type=f32,
    ).astype(bf16)
    lane = lax.broadcasted_iota(jnp.int32, (rows, LANES), 1)
    tail_out[...] = jnp.where(lane == mine, row_grad, 0.0).astype(bf16)
    save_cot.wait()
    save_act.wait()


def grad_kernel(segments, half, *refs):
    count = len(segments)
    blocks = refs[:count]
    (near, far, spot, w_in, w_far, tail, alpha, side) = refs[count : count + 8]
    (d_own, d_other, sums, squash, slope) = refs[count + 8 :]
    rows = near.shape[0]
    block = rows // 8
    gain = alpha[0]
    start = pl.multiple_of(side[0] * half, half)
    for source, places in zip(blocks, segments):
        size = source.shape[0] // len(places)
        for part, to in enumerate(places):
            inputs = source[part * size : (part + 1) * size, pl.ds(start, half)].astype(f32)
            squashed = jnp.tanh(gain * inputs)
            squash[to : to + size, :] = squashed
            slope[to : to + size, :] = (1.0 - squashed * squashed) * inputs
    slots = far.shape[0]
    mirrored = jnp.concatenate([far[slots // 2 :, :], far[: slots // 2, :]], axis=0)
    mirrored = jnp.dot(
        one_hot(spot[...], slots), mirrored, preferred_element_type=f32
    ).astype(bf16)

    def place(cols, value):
        for x in range(2):
            for y in range(2):
                row = (x * 4 + y) * block
                d_own[x, y, :, cols] = value[row : row + block]
                row = (x * 4 + 2 + y) * block
                d_other[x, y, :, cols] = value[row : row + block]

    place(slice(half, half + LANES), tail[...])
    step = 512
    for at in range(0, half, step):
        cols = slice(at, at + step)
        part = jnp.dot(
            near[...],
            w_in[:, pl.ds(pl.multiple_of(start + at, step), step)],
            preferred_element_type=f32,
        )
        part = part + jnp.dot(mirrored, w_far[:, cols], preferred_element_type=f32)
        short = part.astype(bf16)
        place(cols, short)
        part = short.astype(f32)
        sums[0:1, cols] = jnp.sum(part, axis=0, keepdims=True)
        sums[1:2, cols] = jnp.sum(part * squash[:, cols], axis=0, keepdims=True)
        sums[2:3, cols] = jnp.sum(part * slope[:, cols], axis=0, keepdims=True)
        sums[3:8, cols] = jnp.zeros((5, step), f32)


def pack_kernel(tokens, cotangent, ids, probs, out):
    width = tokens.shape[1]
    top, block = ids.shape
    names = ids[...]
    shares = probs[...].astype(f32)
    label = lax.broadcasted_iota(jnp.int32, (LANES, block), 0)
    table = jnp.zeros((LANES, block), f32)
    for k in range(top):
        table = table + jnp.where(label == names[k : k + 1, :], shares[k : k + 1, :], 0.0)
    row = lax.broadcasted_iota(jnp.int32, (block, block), 0)
    column = lax.broadcasted_iota(jnp.int32, (block, block), 1)
    unit = jnp.where(row == column, 1.0, 0.0).astype(bf16)
    out[:, 2 * width :] = contract_width(unit, table.astype(bf16)).astype(bf16)
    out[:, :width] = tokens[...]
    out[:, width : 2 * width] = cotangent[...]


def join_kernel(first, second, out):
    size = first.shape[0]
    out[:size, :] = first[...]
    out[size:, :] = second[...]


def down_kernel(count, hidden, *refs):
    kept = refs[:count]
    out, held, sems = refs[count:]
    half = kept[0].shape[0] // 2
    copies = []
    for batch in range(2):
        for k in range(count):
            copy = pltpu.make_async_copy(
                kept[k].at[batch * half : (batch + 1) * half, :],
                held.at[batch, k * half : (k + 1) * half, :],
                sems.at[batch, k],
            )
            copy.start()
            copies.append(copy)
    total = None
    for batch in range(2):
        for copy in copies[batch * count : (batch + 1) * count]:
            copy.wait()
        term = lax.dot_general(
            held[batch, :, :hidden],
            held[batch, :, hidden:],
            (((0,), (0,)), ((), ())),
            preferred_element_type=f32,
        )
        term = term.astype(bf16).astype(f32)
        total = term if total is None else total + term
    out[...] = total.astype(bf16)


def whole():
    return pl.BlockSpec(memory_space=pltpu.VMEM)


def scalar():
    return pl.BlockSpec(memory_space=pltpu.SMEM)


def dense_shards(tokens, cotangent, expert_ids, gate_probs, alpha, gamma, beta, w_in, w_down):
    experts = lax.axis_size("expert")
    planes = experts // 4
    block = tokens.shape[1]
    width = tokens.shape[2]
    hidden = w_down.shape[1]
    rows = 8 * block
    slots = 3 * block * expert_ids.shape[2] // (2 * experts)
    me = lax.axis_index("expert")

    def go_x(v):
        return lax.ppermute(v, "dp", [(0, 1), (1, 0)])

    def go_y(v):
        return lax.ppermute(v, "expert", [(e, e ^ 2) for e in range(experts)])

    def go_core(v):
        return lax.ppermute(v, "expert", [(e, e ^ 1) for e in range(experts)])

    def go_z(v):
        return lax.ppermute(v, "expert", [(e, (e + 4) % experts) for e in range(experts)])

    def go_jump(v, by):
        return lax.ppermute(v, "expert", [(e, e ^ by) for e in range(experts)])

    def go_far(v, by):
        pairs = [
            (2 * e + x, 2 * (e ^ by) + 1 - x) for e in range(experts) for x in range(2)
        ]
        return lax.ppermute(v, ("expert", "dp"), pairs)

    lanes = jnp.arange(LANES, dtype=jnp.int32)
    picks = expert_ids[0][:, :, None] == lanes[None, None, :]
    own = pl.pallas_call(
        pack_kernel,
        out_shape=jax.ShapeDtypeStruct((block, 2 * width + LANES), bf16),
        in_specs=[whole()] * 4,
        out_specs=whole(),
        name="pack",
    )(tokens[0], cotangent[0], expert_ids[0].T, gate_probs[0].T)

    flat_in = w_in[0].reshape(2 * hidden, width)
    flat_down = w_down[0]
    gamma_row = gamma.reshape(1, width)
    beta_row = beta.reshape(1, width)
    mine = me.reshape(1).astype(jnp.int32)
    half = width // 2
    side = lax.axis_index("dp").astype(jnp.int32)
    w_send = lax.dynamic_slice_in_dim(flat_in, (1 - side) * half, half, axis=1)

    def segments_of(arrays):
        places = [
            (x * 4 + core * 2 + y) * block
            for core in range(2)
            for y in range(2)
            for x in range(2)
        ]
        size = 8 // len(arrays)
        return tuple(tuple(places[k : k + size]) for k in range(0, 8, size))

    params = pltpu.CompilerParams(vmem_limit_bytes=14 << 20)

    def first_half(arrays):
        return pl.pallas_call(
            functools.partial(rows_kernel, segments_of(arrays), width, hidden),
            out_shape=(
                jax.ShapeDtypeStruct((rows, 2 * hidden), bf16),
                jax.ShapeDtypeStruct((8 * slots, 2 * hidden), bf16),
                jax.ShapeDtypeStruct((rows, LANES), f32),
                pltpu.HBM((rows, hidden + width), bf16),
                jax.ShapeDtypeStruct((rows, LANES), bf16),
            ),
            in_specs=[whole()] * (len(arrays) + 4) + [scalar(), scalar()],
            out_specs=(whole(),) * 3 + (pl.BlockSpec(memory_space=pltpu.HBM), whole()),
            scratch_shapes=[
                pltpu.VMEM((rows, width), bf16),
                pltpu.VMEM((rows, width), bf16),
                pltpu.VMEM((rows, LANES), f32),
                pltpu.VMEM((rows, hidden + width), bf16),
                pltpu.SemaphoreType.DMA((2,)),
            ],
            compiler_params=params,
            name="rows",
        )(*arrays, flat_in, flat_down, gamma_row, beta_row, alpha, mine)

    def second_half(arrays, near, far, spot, w_far, tail):
        return pl.pallas_call(
            functools.partial(grad_kernel, segments_of(arrays), half),
            out_shape=(
                jax.ShapeDtypeStruct((2, 2, block, half + LANES), bf16),
                jax.ShapeDtypeStruct((2, 2, block, half + LANES), bf16),
                jax.ShapeDtypeStruct((8, half), f32),
            ),
            in_specs=[whole()] * (len(arrays) + 6) + [scalar(), scalar()],
            out_specs=(whole(),) * 3,
            scratch_shapes=[
                pltpu.VMEM((rows, half), f32),
                pltpu.VMEM((rows, half), f32),
            ],
            compiler_params=params,
            name="grads",
        )(*arrays, near, far, spot, flat_in, w_far, tail, alpha, side.reshape(1))

    fence = lax.optimization_barrier
    def join(first, second):
        return pl.pallas_call(
            join_kernel,
            out_shape=jax.ShapeDtypeStruct((2 * block, 2 * width + LANES), bf16),
            in_specs=[whole()] * 2,
            out_specs=whole(),
            name="join",
        )(first, second)

    near, far, near_c, far_c, w_far = {0: [own]}, {}, {}, {}, {}
    state = {"a": near, "b": far, "c": near_c, "d": far_c, "w": w_far}
    grads, kept, tails, other, packed, spots = {}, {}, {}, {}, {}, {}
    state.update(grads=grads, other=other, packed=packed)
    d_own, d_got, totals, sent, value = {}, {}, {}, {}, {}
    state.update(d_own=d_own, d_got=d_got, totals=totals, sent=sent, value=value)

    def make_down(held):
        return pl.pallas_call(
            functools.partial(down_kernel, planes, hidden),
            out_shape=jax.ShapeDtypeStruct((hidden, width), bf16),
            in_specs=[pl.BlockSpec(memory_space=pltpu.HBM)] * planes,
            out_specs=whole(),
            scratch_shapes=[
                pltpu.VMEM((2, planes * rows // 2, hidden + width), bf16),
                pltpu.SemaphoreType.DMA((2, planes)),
            ],
            compiler_params=pltpu.CompilerParams(vmem_limit_bytes=20 << 20),
            name="down",
        )(*[pltpu.with_memory_space_constraint(one, pltpu.HBM) for one in held])

    def step(*late):
        now = {
            name: {k: v for k, v in held.items() if (name, k) not in late}
            for name, held in state.items()
        }
        new = fence(now)
        for name, held in state.items():
            held.update(new[name])

    def rows_of(k):
        arrays = near[k] + far[k] + near_c[k] + far_c[k]
        grads[k], packed[k], spots[k], kept[k], tails[k] = first_half(arrays)

    def grads_of(k):
        arrays = near[k] + far[k] + near_c[k] + far_c[k]
        d_own[k], moved, totals[k] = second_half(
            arrays, grads[k], other[k], spots[k], w_far[0], tails[k]
        )
        d_got[k] = go_core(moved)

    def send_y(k):
        sent[k] = go_y(add16(d_own[k][:, 1], d_got[k][:, 1]))

    def total_of(k):
        kept = d_own[k][:, 0].astype(f32) + d_got[k][:, 0].astype(f32)
        return kept + sent[k].astype(f32)

    def hop(k):
        carried = total_of(k)
        if k > 1:
            carried = carried + value[k].astype(f32)
        value[(k + 1) % planes] = go_z(carried.astype(bf16))

    near[0].append(go_x(own))
    near[1] = [go_z(own)]
    far[0] = [go_y(own)]
    near_c[0] = [go_core(own)]
    step()
    near[1].append(go_z(near[0][1]))
    far[0].append(go_y(near[0][1]))
    near_c[0].append(go_core(near[0][1]))
    far_c[0] = [go_core(far[0][0])]
    w_send, near_c[0] = fence((w_send, near_c[0]))
    w_far[0] = go_x(w_send)
    step(("w", 0))
    near[1] = [join(*near[1])]
    for k in range(1, 3):
        near[k + 1] = [go_z(near[k][0])]
        far[k] = [go_y(near[k][0])]
        near_c[k] = [go_core(near[k][0])]
        if k == 1:
            far_c[0].append(go_core(far[0][1]))
        else:
            far_c[1] = [go_core(far[1][0])]
        rows_of(k - 1)
        if k == 2:
            other[0] = go_x(packed[0])
        step(*([("w", 0)] if k == 1 else []))
    other[1] = go_x(packed[1])
    far[3] = [go_y(near[3][0])]
    near_c[3] = [go_core(near[3][0])]
    far_c[2] = [go_core(far[2][0])]
    rows_of(2)
    grads_of(0)
    step()
    other[2] = go_x(packed[2])
    far_c[3] = [go_core(far[3][0])]
    rows_of(3)
    other[1], packed[3] = fence((other[1], packed[3]))
    grads_of(1)
    step()
    other[3] = go_x(packed[3])
    send_y(1)
    other[2], sent[1], d_got[0] = fence((other[2], sent[1], d_got[0]))
    grads_of(2)
    hop(1)
    send_y(2)
    send_y(0)
    step(("sent", 0), ("sent", 2), ("value", 2))
    grads_of(3)
    hop(2)
    pool = {}
    pool[0] = sum(totals[k] for k in range(1, planes)) + totals[0]
    pool[0] = pool[0] + go_core(pool[0])
    state["pool"] = pool
    step(("value", 3), ("sent", 2), ("value", 2), ("sent", 0))
    send_y(3)
    part = pool[0]
    mine_sums = part + go_y(part)
    cross_sums = go_x(part) + go_far(part, 2)
    pool[0] = jnp.concatenate([mine_sums, cross_sums], axis=0)
    step(("pool", 0))
    hop(3)
    pool[0] = pool[0] + go_jump(pool[0], 4)
    step()
    kept[3], pool[0] = fence((kept[3], pool[0]))
    final = total_of(0) + value[0].astype(f32)
    crossed = go_x(final[1].astype(bf16)).astype(f32)
    left = jnp.where(side == 0, final[0, :, :half], crossed[:, :half])
    right = jnp.where(side == 0, crossed[:, :half], final[0, :, :half])
    grad_normed = jnp.concatenate([left, right], axis=1)
    row_grads = final[0, :, half:] + crossed[:, half:]
    grad_down = make_down([kept[k] for k in range(planes)])
    sums = pool[0] + go_jump(pool[0], 8)
    mine_sums, cross_sums = sums[:8], sums[8:]
    sums = jnp.concatenate(
        [
            jnp.where(side == 0, mine_sums, cross_sums),
            jnp.where(side == 0, cross_sums, mine_sums),
        ],
        axis=1,
    )

    inputs = tokens[0].astype(f32)
    squashed = jnp.tanh(alpha[0] * inputs)
    pre_grad = grad_normed * gamma * (1.0 - squashed * squashed)
    grad_tokens = (cotangent[0].astype(f32) + alpha[0] * pre_grad).astype(bf16)
    grad_probs = jnp.sum(jnp.where(picks, row_grads[:, None, :], 0.0), axis=2).astype(bf16)
    grad_beta = sums[0]
    grad_gamma = sums[1]
    grad_alpha = jnp.sum(sums[2] * gamma).reshape(1)
    return (
        grad_tokens[None],
        grad_probs[None],
        grad_down[None],
        grad_gamma,
        grad_beta,
        grad_alpha,
    )


def slot_layout(ids_local, expert_count, capacity):
    token_count, top_count = ids_local.shape
    labels = jnp.arange(expert_count, dtype=jnp.int32)
    onehot = (ids_local[:, :, None] == labels[None, None, :]).astype(jnp.int32)
    picks = jnp.sum(onehot, axis=1)
    order = jnp.arange(token_count, dtype=jnp.int32)
    earlier = (order[None, :] < order[:, None]).astype(f32)
    before = jnp.dot(earlier, picks.astype(f32), precision=lax.Precision.HIGHEST)
    slots = jnp.sum(onehot * before.astype(jnp.int32)[:, None, :], axis=2)
    position = ids_local * capacity + slots
    pairs = jnp.arange(token_count * top_count, dtype=jnp.int32)
    table = jnp.full((expert_count * capacity,), token_count * top_count, jnp.int32)
    table = table.at[position.reshape(-1)].set(pairs)
    return (position, table)


def routed_shards(tokens, cotangent, expert_ids, gate_probs, alpha, gamma, beta, w_in, w_down):
    expert_count = lax.axis_size("expert")
    token_count = tokens.shape[1]
    top_count = expert_ids.shape[2]
    width = tokens.shape[2]
    capacity = 3 * token_count * top_count // (2 * expert_count)
    rows_total = expert_count * capacity
    inputs = tokens[0].astype(jnp.float32)
    squashed = jnp.tanh(alpha[0] * inputs)
    normed = (gamma * squashed + beta).astype(jnp.bfloat16)
    position, table = slot_layout(expert_ids[0], expert_count, capacity)
    source_token = table // top_count
    zero_row = jnp.zeros((1, width), jnp.bfloat16)
    normed_pad = jnp.concatenate([normed, zero_row], axis=0)
    cot_pad = jnp.concatenate([cotangent[0], zero_row], axis=0)
    prob_pad = jnp.concatenate([gate_probs[0].reshape(-1), jnp.zeros((1,), jnp.bfloat16)], axis=0)
    send_rows = normed_pad[source_token].reshape(expert_count, capacity, width)
    send_cot = cot_pad[source_token].reshape(expert_count, capacity, width)
    send_prob = prob_pad[table].reshape(expert_count, capacity)

    def swap(value):
        return lax.all_to_all(value, "expert", split_axis=0, concat_axis=0, tiled=True)

    in_rows = swap(send_rows).reshape(rows_total, width)
    cot_rows = swap(send_cot).reshape(rows_total, width)
    prob_rows = swap(send_prob).reshape(rows_total).astype(jnp.float32)
    gate_up = lax.all_gather(w_in, "dp", axis=2, tiled=True)
    w_lower = lax.all_gather(w_down, "dp", axis=1, tiled=True)[0]
    w_gate = gate_up[0, 0]
    w_upper = gate_up[0, 1]
    gate_pre = contract_width(in_rows, w_gate)
    up_value = contract_width(in_rows, w_upper)
    sigma = jax.nn.sigmoid(gate_pre)
    activation = (gate_pre * sigma * up_value).astype(jnp.bfloat16)
    back = contract_width(cot_rows, w_lower)
    weight_row = residual_scale * prob_rows
    scaled_cot = (weight_row[:, None] * cot_rows.astype(jnp.float32)).astype(jnp.bfloat16)
    row_grad = residual_scale * jnp.sum(activation.astype(jnp.float32) * back, axis=1)
    d_act = weight_row[:, None] * back
    d_gate = (d_act * up_value * sigma * (1.0 + gate_pre * (1.0 - sigma))).astype(jnp.bfloat16)
    d_up = (d_act * gate_pre * sigma).astype(jnp.bfloat16)
    d_rows = (
        jnp.dot(d_gate, w_gate, preferred_element_type=jnp.float32)
        + jnp.dot(d_up, w_upper, preferred_element_type=jnp.float32)
    ).astype(jnp.bfloat16)
    back_rows = swap(d_rows.reshape(expert_count, capacity, width))
    back_probs = swap(row_grad.astype(jnp.bfloat16).reshape(expert_count, capacity))
    partial_grad = lax.dot_general(
        activation, scaled_cot, (((0,), (0,)), ((), ())), preferred_element_type=jnp.float32
    )
    grad_down = lax.psum_scatter(
        partial_grad[None].astype(jnp.bfloat16), "dp", scatter_dimension=1, tiled=True
    )
    picked = back_rows.reshape(rows_total, width)[position]
    grad_normed = jnp.sum(picked.astype(jnp.float32), axis=1)
    grad_probs = back_probs.reshape(rows_total)[position]
    gamma_part = jnp.sum(grad_normed * squashed, axis=0)
    beta_part = jnp.sum(grad_normed, axis=0)
    pre_grad = grad_normed * gamma * (1.0 - squashed * squashed)
    alpha_part = jnp.sum(pre_grad * inputs).reshape(1)
    grad_gamma, grad_beta, grad_alpha = lax.psum(
        (gamma_part, beta_part, alpha_part), ("expert", "dp")
    )
    grad_tokens = (cotangent[0].astype(jnp.float32) + alpha[0] * pre_grad).astype(jnp.bfloat16)
    return (grad_tokens[None], grad_probs[None], grad_down, grad_gamma, grad_beta, grad_alpha)


def shards(*arrays):
    experts = lax.axis_size("expert")
    top_count = arrays[2].shape[2]
    dense = (
        lax.axis_size("dp") == 2
        and experts == 16
        and arrays[0].shape[1] == 32
        and top_count == 8
        and 2 * top_count >= experts
        and arrays[0].shape[2] % 2048 == 0
    )
    return (dense_shards if dense else routed_shards)(*arrays)


def solution(mesh):
    placed = (
        P("dp", "expert", None),
        P("dp", "expert", None),
        P("dp", "expert", None),
        P("dp", "expert", None),
        P(),
        P(),
        P(),
        P("expert", None, "dp", None),
        P("expert", "dp", None),
    )
    return jax.shard_map(
        shards,
        mesh=mesh,
        in_specs=placed,
        out_specs=(
            P("dp", "expert", None),
            P("dp", "expert", None),
            P("expert", "dp", None),
            P(),
            P(),
            P(),
        ),
        check_vma=False,
    )
```

```python
import functools
import jax
import jax.numpy as jnp
from jax import lax
from jax.experimental import pallas as pl
from jax.experimental.pallas import tpu as pltpu
from jax.sharding import PartitionSpec as P

residual_scale = 0.7071
LANES = 128
f32 = jnp.float32
bf16 = jnp.bfloat16


def contract_width(left, right):
    return lax.dot_general(
        left, right, (((1,), (1,)), ((), ())), preferred_element_type=f32
    )


def add16(left, right):
    return (left.astype(f32) + right.astype(f32)).astype(bf16)


def one_hot(spot, slots):
    label = lax.broadcasted_iota(jnp.int32, (spot.shape[0], slots), 1).astype(f32)
    return jnp.where(label == spot[:, 0:1], 1.0, 0.0).astype(bf16)


def rows_kernel(segments, width, hidden, *refs):
    count = len(segments)
    blocks = refs[:count]
    (w_in, w_down, gamma, beta, alpha, expert) = refs[count : count + 6]
    (grads_out, packed_out, spot_out, kept_out, tail_out) = refs[count + 6 : count + 11]
    (normed, cot, weight, kept, sems) = refs[count + 11 :]
    rows = normed.shape[0]
    gain = alpha[0]
    mine = expert[0]
    gamma_row = gamma[...]
    beta_row = beta[...]
    for source, places in zip(blocks, segments):
        size = source.shape[0] // len(places)
        for part, to in enumerate(places):
            here, there = slice(part * size, (part + 1) * size), slice(to, to + size)
            squashed = jnp.tanh(gain * source[here, 0:width].astype(f32))
            normed[there, :] = (gamma_row * squashed + beta_row).astype(bf16)
            rows_cot = source[here, width : 2 * width]
            cot[there, :] = rows_cot
            gates = source[here, 2 * width :].astype(f32)
            lane = lax.broadcasted_iota(jnp.int32, gates.shape, 1)
            own = jnp.sum(jnp.where(lane == mine, gates, 0.0), axis=1, keepdims=True)
            own = residual_scale * own
            weight[there, :] = jnp.broadcast_to(own, (size, LANES))
            kept[there, hidden:] = (own * rows_cot.astype(f32)).astype(bf16)
    wide = slice(hidden, hidden + width)
    save_cot = pltpu.make_async_copy(kept.at[:, wide], kept_out.at[:, wide], sems.at[0])
    save_cot.start()
    pre = contract_width(normed[...], w_in[...])
    back = contract_width(cot[...], w_down[...])
    gate_pre = pre[:, :hidden]
    up_value = pre[:, hidden:]
    sigma = jax.nn.sigmoid(gate_pre)
    silu = gate_pre * sigma
    activation = (silu * up_value).astype(bf16)
    kept[:, :hidden] = activation
    save_act = pltpu.make_async_copy(
        kept.at[:, :hidden], kept_out.at[:, :hidden], sems.at[1]
    )
    save_act.start()
    row_grad = residual_scale * jnp.sum(activation.astype(f32) * back, axis=1, keepdims=True)
    d_act = weight[:, 0:1] * back
    d_gate = d_act * up_value * sigma * (1.0 + gate_pre * (1.0 - sigma))
    grads_out[:, :hidden] = d_gate.astype(bf16)
    grads_out[:, hidden:] = (d_act * gate_pre * sigma).astype(bf16)
    routed = weight[...] > 0.0
    block = rows // 8
    row = lax.broadcasted_iota(jnp.int32, (rows, rows), 0)
    column = lax.broadcasted_iota(jnp.int32, (rows, rows), 1)
    earlier = (column < row) & (column >= row - lax.rem(row, block))
    count_before = jnp.dot(
        jnp.where(earlier, 1.0, 0.0).astype(bf16),
        jnp.where(routed, 1.0, 0.0).astype(bf16),
        preferred_element_type=f32,
    )
    slots = packed_out.shape[0] // 8
    row = lax.broadcasted_iota(jnp.int32, (rows, LANES), 0)
    base = (lax.div(row, block) * slots).astype(f32)
    spot = jnp.where(routed, base + count_before, -1.0)
    spot_out[...] = spot
    packed_out[...] = lax.dot_general(
        one_hot(spot, 8 * slots), grads_out[...], (((0,), (0,)), ((), ())),
        preferred_element_type=f32,
    ).astype(bf16)
    lane = lax.broadcasted_iota(jnp.int32, (rows, LANES), 1)
    tail_out[...] = jnp.where(lane == mine, row_grad, 0.0).astype(bf16)
    save_cot.wait()
    save_act.wait()


def grad_kernel(segments, half, *refs):
    count = len(segments)
    blocks = refs[:count]
    (near, far, spot, w_in, w_far, tail, alpha, side) = refs[count : count + 8]
    (d_own, d_other, sums, squash, slope) = refs[count + 8 :]
    rows = near.shape[0]
    block = rows // 8
    gain = alpha[0]
    start = pl.multiple_of(side[0] * half, half)
    for source, places in zip(blocks, segments):
        size = source.shape[0] // len(places)
        for part, to in enumerate(places):
            inputs = source[part * size : (part + 1) * size, pl.ds(start, half)].astype(f32)
            squashed = jnp.tanh(gain * inputs)
            squash[to : to + size, :] = squashed
            slope[to : to + size, :] = (1.0 - squashed * squashed) * inputs
    slots = far.shape[0]
    mirrored = jnp.concatenate([far[slots // 2 :, :], far[: slots // 2, :]], axis=0)
    mirrored = jnp.dot(
        one_hot(spot[...], slots), mirrored, preferred_element_type=f32
    ).astype(bf16)

    def place(cols, value):
        for x in range(2):
            for y in range(2):
                row = (x * 4 + y) * block
                d_own[x, y, :, cols] = value[row : row + block]
                row = (x * 4 + 2 + y) * block
                d_other[x, y, :, cols] = value[row : row + block]

    place(slice(half, half + LANES), tail[...])
    step = 512
    for at in range(0, half, step):
        cols = slice(at, at + step)
        part = jnp.dot(
            near[...],
            w_in[:, pl.ds(pl.multiple_of(start + at, step), step)],
            preferred_element_type=f32,
        )
        part = part + jnp.dot(mirrored, w_far[:, cols], preferred_element_type=f32)
        short = part.astype(bf16)
        place(cols, short)
        part = short.astype(f32)
        sums[0:1, cols] = jnp.sum(part, axis=0, keepdims=True)
        sums[1:2, cols] = jnp.sum(part * squash[:, cols], axis=0, keepdims=True)
        sums[2:3, cols] = jnp.sum(part * slope[:, cols], axis=0, keepdims=True)
        sums[3:8, cols] = jnp.zeros((5, step), f32)


def pack_kernel(tokens, cotangent, ids, probs, out):
    width = tokens.shape[1]
    top, block = ids.shape
    names = ids[...]
    shares = probs[...].astype(f32)
    label = lax.broadcasted_iota(jnp.int32, (LANES, block), 0)
    table = jnp.zeros((LANES, block), f32)
    for k in range(top):
        table = table + jnp.where(label == names[k : k + 1, :], shares[k : k + 1, :], 0.0)
    row = lax.broadcasted_iota(jnp.int32, (block, block), 0)
    column = lax.broadcasted_iota(jnp.int32, (block, block), 1)
    unit = jnp.where(row == column, 1.0, 0.0).astype(bf16)
    out[:, 2 * width :] = contract_width(unit, table.astype(bf16)).astype(bf16)
    out[:, :width] = tokens[...]
    out[:, width : 2 * width] = cotangent[...]


def join_kernel(first, second, out):
    size = first.shape[0]
    out[:size, :] = first[...]
    out[size:, :] = second[...]


def down_kernel(count, hidden, *refs):
    kept = refs[:count]
    out, held, sems = refs[count:]
    half = kept[0].shape[0] // 2
    copies = []
    for batch in range(2):
        for k in range(count):
            copy = pltpu.make_async_copy(
                kept[k].at[batch * half : (batch + 1) * half, :],
                held.at[batch, k * half : (k + 1) * half, :],
                sems.at[batch, k],
            )
            copy.start()
            copies.append(copy)
    total = None
    for batch in range(2):
        for copy in copies[batch * count : (batch + 1) * count]:
            copy.wait()
        term = lax.dot_general(
            held[batch, :, :hidden],
            held[batch, :, hidden:],
            (((0,), (0,)), ((), ())),
            preferred_element_type=f32,
        )
        term = term.astype(bf16).astype(f32)
        total = term if total is None else total + term
    out[...] = total.astype(bf16)


def whole():
    return pl.BlockSpec(memory_space=pltpu.VMEM)


def scalar():
    return pl.BlockSpec(memory_space=pltpu.SMEM)


def dense_shards(tokens, cotangent, expert_ids, gate_probs, alpha, gamma, beta, w_in, w_down):
    experts = lax.axis_size("expert")
    planes = experts // 4
    block = tokens.shape[1]
    width = tokens.shape[2]
    hidden = w_down.shape[1]
    rows = 8 * block
    slots = 3 * block * expert_ids.shape[2] // (2 * experts)
    me = lax.axis_index("expert")

    def go_x(v):
        return lax.ppermute(v, "dp", [(0, 1), (1, 0)])

    def go_y(v):
        return lax.ppermute(v, "expert", [(e, e ^ 2) for e in range(experts)])

    def go_core(v):
        return lax.ppermute(v, "expert", [(e, e ^ 1) for e in range(experts)])

    def go_z(v):
        return lax.ppermute(v, "expert", [(e, (e + 4) % experts) for e in range(experts)])

    def go_jump(v, by):
        return lax.ppermute(v, "expert", [(e, e ^ by) for e in range(experts)])

    def go_far(v, by):
        pairs = [
            (2 * e + x, 2 * (e ^ by) + 1 - x) for e in range(experts) for x in range(2)
        ]
        return lax.ppermute(v, ("expert", "dp"), pairs)

    lanes = jnp.arange(LANES, dtype=jnp.int32)
    picks = expert_ids[0][:, :, None] == lanes[None, None, :]
    own = pl.pallas_call(
        pack_kernel,
        out_shape=jax.ShapeDtypeStruct((block, 2 * width + LANES), bf16),
        in_specs=[whole()] * 4,
        out_specs=whole(),
        name="pack",
    )(tokens[0], cotangent[0], expert_ids[0].T, gate_probs[0].T)

    flat_in = w_in[0].reshape(2 * hidden, width)
    flat_down = w_down[0]
    gamma_row = gamma.reshape(1, width)
    beta_row = beta.reshape(1, width)
    mine = me.reshape(1).astype(jnp.int32)
    half = width // 2
    side = lax.axis_index("dp").astype(jnp.int32)
    w_send = lax.dynamic_slice_in_dim(flat_in, (1 - side) * half, half, axis=1)

    def segments_of(arrays):
        places = [
            (x * 4 + core * 2 + y) * block
            for core in range(2)
            for y in range(2)
            for x in range(2)
        ]
        size = 8 // len(arrays)
        return tuple(tuple(places[k : k + size]) for k in range(0, 8, size))

    params = pltpu.CompilerParams(vmem_limit_bytes=14 << 20)

    def first_half(arrays):
        return pl.pallas_call(
            functools.partial(rows_kernel, segments_of(arrays), width, hidden),
            out_shape=(
                jax.ShapeDtypeStruct((rows, 2 * hidden), bf16),
                jax.ShapeDtypeStruct((8 * slots, 2 * hidden), bf16),
                jax.ShapeDtypeStruct((rows, LANES), f32),
                pltpu.HBM((rows, hidden + width), bf16),
                jax.ShapeDtypeStruct((rows, LANES), bf16),
            ),
            in_specs=[whole()] * (len(arrays) + 4) + [scalar(), scalar()],
            out_specs=(whole(),) * 3 + (pl.BlockSpec(memory_space=pltpu.HBM), whole()),
            scratch_shapes=[
                pltpu.VMEM((rows, width), bf16),
                pltpu.VMEM((rows, width), bf16),
                pltpu.VMEM((rows, LANES), f32),
                pltpu.VMEM((rows, hidden + width), bf16),
                pltpu.SemaphoreType.DMA((2,)),
            ],
            compiler_params=params,
            name="rows",
        )(*arrays, flat_in, flat_down, gamma_row, beta_row, alpha, mine)

    def second_half(arrays, near, far, spot, w_far, tail):
        return pl.pallas_call(
            functools.partial(grad_kernel, segments_of(arrays), half),
            out_shape=(
                jax.ShapeDtypeStruct((2, 2, block, half + LANES), bf16),
                jax.ShapeDtypeStruct((2, 2, block, half + LANES), bf16),
                jax.ShapeDtypeStruct((8, half), f32),
            ),
            in_specs=[whole()] * (len(arrays) + 6) + [scalar(), scalar()],
            out_specs=(whole(),) * 3,
            scratch_shapes=[
                pltpu.VMEM((rows, half), f32),
                pltpu.VMEM((rows, half), f32),
            ],
            compiler_params=params,
            name="grads",
        )(*arrays, near, far, spot, flat_in, w_far, tail, alpha, side.reshape(1))

    fence = lax.optimization_barrier
    def join(first, second):
        return pl.pallas_call(
            join_kernel,
            out_shape=jax.ShapeDtypeStruct((2 * block, 2 * width + LANES), bf16),
            in_specs=[whole()] * 2,
            out_specs=whole(),
            name="join",
        )(first, second)

    near, far, near_c, far_c, w_far = {0: [own]}, {}, {}, {}, {}
    state = {"a": near, "b": far, "c": near_c, "d": far_c, "w": w_far}
    grads, kept, tails, other, packed, spots = {}, {}, {}, {}, {}, {}
    state.update(grads=grads, other=other, packed=packed)
    d_own, d_got, totals, sent, value = {}, {}, {}, {}, {}
    state.update(d_own=d_own, d_got=d_got, totals=totals, sent=sent, value=value)

    def make_down(held):
        return pl.pallas_call(
            functools.partial(down_kernel, planes, hidden),
            out_shape=jax.ShapeDtypeStruct((hidden, width), bf16),
            in_specs=[pl.BlockSpec(memory_space=pltpu.HBM)] * planes,
            out_specs=whole(),
            scratch_shapes=[
                pltpu.VMEM((2, planes * rows // 2, hidden + width), bf16),
                pltpu.SemaphoreType.DMA((2, planes)),
            ],
            compiler_params=pltpu.CompilerParams(vmem_limit_bytes=20 << 20),
            name="down",
        )(*[pltpu.with_memory_space_constraint(one, pltpu.HBM) for one in held])

    def step(*late):
        now = {
            name: {k: v for k, v in held.items() if (name, k) not in late}
            for name, held in state.items()
        }
        new = fence(now)
        for name, held in state.items():
            held.update(new[name])

    def rows_of(k):
        arrays = near[k] + far[k] + near_c[k] + far_c[k]
        grads[k], packed[k], spots[k], kept[k], tails[k] = first_half(arrays)

    def grads_of(k):
        arrays = near[k] + far[k] + near_c[k] + far_c[k]
        d_own[k], moved, totals[k] = second_half(
            arrays, grads[k], other[k], spots[k], w_far[0], tails[k]
        )
        d_got[k] = go_core(moved)

    def send_y(k):
        sent[k] = go_y(add16(d_own[k][:, 1], d_got[k][:, 1]))

    def total_of(k):
        kept = d_own[k][:, 0].astype(f32) + d_got[k][:, 0].astype(f32)
        return kept + sent[k].astype(f32)

    def hop(k):
        carried = total_of(k)
        if k > 1:
            carried = carried + value[k].astype(f32)
        value[(k + 1) % planes] = go_z(carried.astype(bf16))

    near[0].append(go_x(own))
    near[1] = [go_z(own)]
    far[0] = [go_y(own)]
    near_c[0] = [go_core(own)]
    state["s"] = {0: w_send}
    step()
    w_send = state.pop("s")[0]
    near[1].append(go_z(near[0][1]))
    far[0].append(go_y(near[0][1]))
    near_c[0].append(go_core(near[0][1]))
    far_c[0] = [go_core(far[0][0])]
    w_far[0] = go_x(w_send)
    step(("w", 0))
    near[1] = [join(*near[1])]
    for k in range(1, 3):
        near[k + 1] = [go_z(near[k][0])]
        far[k] = [go_y(near[k][0])]
        near_c[k] = [go_core(near[k][0])]
        if k == 1:
            far_c[0].append(go_core(far[0][1]))
        else:
            far_c[1] = [go_core(far[1][0])]
        rows_of(k - 1)
        if k == 2:
            other[0] = go_x(packed[0])
        step(("w", 0) if k == 1 else ("other", 0))
    other[1] = go_x(packed[1])
    far[3] = [go_y(near[3][0])]
    near_c[3] = [go_core(near[3][0])]
    far_c[2] = [go_core(far[2][0])]
    rows_of(2)
    grads_of(0)
    step()
    other[2] = go_x(packed[2])
    far_c[3] = [go_core(far[3][0])]
    rows_of(3)
    other[1], packed[3] = fence((other[1], packed[3]))
    grads_of(1)
    step()
    other[3] = go_x(packed[3])
    send_y(1)
    sent[1], d_got[0] = fence((sent[1], d_got[0]))
    early = totals[1] + go_core(totals[1])
    other[2], early = fence((other[2], early))
    grads_of(2)
    hop(1)
    send_y(2)
    send_y(0)
    step(("sent", 0), ("sent", 2), ("value", 2))
    grads_of(3)
    hop(2)
    pool = {}
    late = totals[2] + totals[3] + totals[0]
    pool[0] = early + (late + go_core(late))
    state["pool"] = pool
    step(("value", 3), ("sent", 2), ("value", 2), ("sent", 0))
    send_y(3)
    part = pool[0]
    mine_sums = part + go_y(part)
    cross_sums = go_x(part) + go_far(part, 2)
    pool[0] = jnp.concatenate([mine_sums, cross_sums], axis=0)
    step(("pool", 0))
    hop(3)
    pool[0] = pool[0] + go_jump(pool[0], 4)
    step()
    kept[3], pool[0] = fence((kept[3], pool[0]))
    final = total_of(0) + value[0].astype(f32)
    crossed = go_x(final[1].astype(bf16)).astype(f32)
    left = jnp.where(side == 0, final[0, :, :half], crossed[:, :half])
    right = jnp.where(side == 0, crossed[:, :half], final[0, :, :half])
    grad_normed = jnp.concatenate([left, right], axis=1)
    row_grads = final[0, :, half:] + crossed[:, half:]
    grad_down = make_down([kept[k] for k in range(planes)])
    sums = pool[0] + go_jump(pool[0], 8)
    mine_sums, cross_sums = sums[:8], sums[8:]
    sums = jnp.concatenate(
        [
            jnp.where(side == 0, mine_sums, cross_sums),
            jnp.where(side == 0, cross_sums, mine_sums),
        ],
        axis=1,
    )

    inputs = tokens[0].astype(f32)
    squashed = jnp.tanh(alpha[0] * inputs)
    pre_grad = grad_normed * gamma * (1.0 - squashed * squashed)
    grad_tokens = (cotangent[0].astype(f32) + alpha[0] * pre_grad).astype(bf16)
    grad_probs = jnp.sum(jnp.where(picks, row_grads[:, None, :], 0.0), axis=2).astype(bf16)
    grad_beta = sums[0]
    grad_gamma = sums[1]
    grad_alpha = jnp.sum(sums[2] * gamma).reshape(1)
    return (
        grad_tokens[None],
        grad_probs[None],
        grad_down[None],
        grad_gamma,
        grad_beta,
        grad_alpha,
    )


def slot_layout(ids_local, expert_count, capacity):
    token_count, top_count = ids_local.shape
    labels = jnp.arange(expert_count, dtype=jnp.int32)
    onehot = (ids_local[:, :, None] == labels[None, None, :]).astype(jnp.int32)
    picks = jnp.sum(onehot, axis=1)
    order = jnp.arange(token_count, dtype=jnp.int32)
    earlier = (order[None, :] < order[:, None]).astype(f32)
    before = jnp.dot(earlier, picks.astype(f32), precision=lax.Precision.HIGHEST)
    slots = jnp.sum(onehot * before.astype(jnp.int32)[:, None, :], axis=2)
    position = ids_local * capacity + slots
    pairs = jnp.arange(token_count * top_count, dtype=jnp.int32)
    table = jnp.full((expert_count * capacity,), token_count * top_count, jnp.int32)
    table = table.at[position.reshape(-1)].set(pairs)
    return (position, table)


def routed_shards(tokens, cotangent, expert_ids, gate_probs, alpha, gamma, beta, w_in, w_down):
    expert_count = lax.axis_size("expert")
    token_count = tokens.shape[1]
    top_count = expert_ids.shape[2]
    width = tokens.shape[2]
    capacity = 3 * token_count * top_count // (2 * expert_count)
    rows_total = expert_count * capacity
    inputs = tokens[0].astype(jnp.float32)
    squashed = jnp.tanh(alpha[0] * inputs)
    normed = (gamma * squashed + beta).astype(jnp.bfloat16)
    position, table = slot_layout(expert_ids[0], expert_count, capacity)
    source_token = table // top_count
    zero_row = jnp.zeros((1, width), jnp.bfloat16)
    normed_pad = jnp.concatenate([normed, zero_row], axis=0)
    cot_pad = jnp.concatenate([cotangent[0], zero_row], axis=0)
    prob_pad = jnp.concatenate([gate_probs[0].reshape(-1), jnp.zeros((1,), jnp.bfloat16)], axis=0)
    send_rows = normed_pad[source_token].reshape(expert_count, capacity, width)
    send_cot = cot_pad[source_token].reshape(expert_count, capacity, width)
    send_prob = prob_pad[table].reshape(expert_count, capacity)

    def swap(value):
        return lax.all_to_all(value, "expert", split_axis=0, concat_axis=0, tiled=True)

    in_rows = swap(send_rows).reshape(rows_total, width)
    cot_rows = swap(send_cot).reshape(rows_total, width)
    prob_rows = swap(send_prob).reshape(rows_total).astype(jnp.float32)
    gate_up = lax.all_gather(w_in, "dp", axis=2, tiled=True)
    w_lower = lax.all_gather(w_down, "dp", axis=1, tiled=True)[0]
    w_gate = gate_up[0, 0]
    w_upper = gate_up[0, 1]
    gate_pre = contract_width(in_rows, w_gate)
    up_value = contract_width(in_rows, w_upper)
    sigma = jax.nn.sigmoid(gate_pre)
    activation = (gate_pre * sigma * up_value).astype(jnp.bfloat16)
    back = contract_width(cot_rows, w_lower)
    weight_row = residual_scale * prob_rows
    scaled_cot = (weight_row[:, None] * cot_rows.astype(jnp.float32)).astype(jnp.bfloat16)
    row_grad = residual_scale * jnp.sum(activation.astype(jnp.float32) * back, axis=1)
    d_act = weight_row[:, None] * back
    d_gate = (d_act * up_value * sigma * (1.0 + gate_pre * (1.0 - sigma))).astype(jnp.bfloat16)
    d_up = (d_act * gate_pre * sigma).astype(jnp.bfloat16)
    d_rows = (
        jnp.dot(d_gate, w_gate, preferred_element_type=jnp.float32)
        + jnp.dot(d_up, w_upper, preferred_element_type=jnp.float32)
    ).astype(jnp.bfloat16)
    back_rows = swap(d_rows.reshape(expert_count, capacity, width))
    back_probs = swap(row_grad.astype(jnp.bfloat16).reshape(expert_count, capacity))
    partial_grad = lax.dot_general(
        activation, scaled_cot, (((0,), (0,)), ((), ())), preferred_element_type=jnp.float32
    )
    grad_down = lax.psum_scatter(
        partial_grad[None].astype(jnp.bfloat16), "dp", scatter_dimension=1, tiled=True
    )
    picked = back_rows.reshape(rows_total, width)[position]
    grad_normed = jnp.sum(picked.astype(jnp.float32), axis=1)
    grad_probs = back_probs.reshape(rows_total)[position]
    gamma_part = jnp.sum(grad_normed * squashed, axis=0)
    beta_part = jnp.sum(grad_normed, axis=0)
    pre_grad = grad_normed * gamma * (1.0 - squashed * squashed)
    alpha_part = jnp.sum(pre_grad * inputs).reshape(1)
    grad_gamma, grad_beta, grad_alpha = lax.psum(
        (gamma_part, beta_part, alpha_part), ("expert", "dp")
    )
    grad_tokens = (cotangent[0].astype(jnp.float32) + alpha[0] * pre_grad).astype(jnp.bfloat16)
    return (grad_tokens[None], grad_probs[None], grad_down, grad_gamma, grad_beta, grad_alpha)


def shards(*arrays):
    experts = lax.axis_size("expert")
    top_count = arrays[2].shape[2]
    dense = (
        lax.axis_size("dp") == 2
        and experts == 16
        and arrays[0].shape[1] == 32
        and top_count == 8
        and 2 * top_count >= experts
        and arrays[0].shape[2] % 2048 == 0
    )
    return (dense_shards if dense else routed_shards)(*arrays)


def solution(mesh):
    placed = (
        P("dp", "expert", None),
        P("dp", "expert", None),
        P("dp", "expert", None),
        P("dp", "expert", None),
        P(),
        P(),
        P(),
        P("expert", None, "dp", None),
        P("expert", "dp", None),
    )
    return jax.shard_map(
        shards,
        mesh=mesh,
        in_specs=placed,
        out_specs=(
            P("dp", "expert", None),
            P("dp", "expert", None),
            P("expert", "dp", None),
            P(),
            P(),
            P(),
        ),
        check_vma=False,
    )
```

```python
import functools
import jax
import jax.numpy as jnp
from jax import lax
from jax.experimental import pallas as pl
from jax.experimental.pallas import tpu as pltpu
from jax.sharding import PartitionSpec as P

residual_scale = 0.7071
LANES = 128
f32 = jnp.float32
bf16 = jnp.bfloat16


def contract_width(left, right):
    return lax.dot_general(
        left, right, (((1,), (1,)), ((), ())), preferred_element_type=f32
    )


def add16(left, right):
    return (left.astype(f32) + right.astype(f32)).astype(bf16)


def one_hot(spot, slots):
    label = lax.broadcasted_iota(jnp.int32, (spot.shape[0], slots), 1).astype(f32)
    return jnp.where(label == spot[:, 0:1], 1.0, 0.0).astype(bf16)


def rows_kernel(segments, width, hidden, *refs):
    count = len(segments)
    blocks = refs[:count]
    (w_in, w_down, gamma, beta, alpha, expert) = refs[count : count + 6]
    (grads_out, packed_out, spot_out, kept_out, tail_out) = refs[count + 6 : count + 11]
    (normed, cot, weight, kept, sems) = refs[count + 11 :]
    rows = normed.shape[0]
    gain = alpha[0]
    mine = expert[0]
    gamma_row = gamma[...]
    beta_row = beta[...]
    for source, places in zip(blocks, segments):
        size = source.shape[0] // len(places)
        for part, to in enumerate(places):
            here, there = slice(part * size, (part + 1) * size), slice(to, to + size)
            squashed = jnp.tanh(gain * source[here, 0:width].astype(f32))
            normed[there, :] = (gamma_row * squashed + beta_row).astype(bf16)
            rows_cot = source[here, width : 2 * width]
            cot[there, :] = rows_cot
            gates = source[here, 2 * width :].astype(f32)
            lane = lax.broadcasted_iota(jnp.int32, gates.shape, 1)
            own = jnp.sum(jnp.where(lane == mine, gates, 0.0), axis=1, keepdims=True)
            own = residual_scale * own
            weight[there, :] = jnp.broadcast_to(own, (size, LANES))
            kept[there, hidden:] = (own * rows_cot.astype(f32)).astype(bf16)
    wide = slice(hidden, hidden + width)
    save_cot = pltpu.make_async_copy(kept.at[:, wide], kept_out.at[:, wide], sems.at[0])
    save_cot.start()
    pre = contract_width(normed[...], w_in[...])
    back = contract_width(cot[...], w_down[...])
    gate_pre = pre[:, :hidden]
    up_value = pre[:, hidden:]
    sigma = jax.nn.sigmoid(gate_pre)
    silu = gate_pre * sigma
    activation = (silu * up_value).astype(bf16)
    kept[:, :hidden] = activation
    save_act = pltpu.make_async_copy(
        kept.at[:, :hidden], kept_out.at[:, :hidden], sems.at[1]
    )
    save_act.start()
    row_grad = residual_scale * jnp.sum(activation.astype(f32) * back, axis=1, keepdims=True)
    d_act = weight[:, 0:1] * back
    d_gate = d_act * up_value * sigma * (1.0 + gate_pre * (1.0 - sigma))
    grads_out[:, :hidden] = d_gate.astype(bf16)
    grads_out[:, hidden:] = (d_act * gate_pre * sigma).astype(bf16)
    routed = weight[...] > 0.0
    block = rows // 8
    row = lax.broadcasted_iota(jnp.int32, (rows, rows), 0)
    column = lax.broadcasted_iota(jnp.int32, (rows, rows), 1)
    earlier = (column < row) & (column >= row - lax.rem(row, block))
    count_before = jnp.dot(
        jnp.where(earlier, 1.0, 0.0).astype(bf16),
        jnp.where(routed, 1.0, 0.0).astype(bf16),
        preferred_element_type=f32,
    )
    slots = packed_out.shape[0] // 8
    row = lax.broadcasted_iota(jnp.int32, (rows, LANES), 0)
    base = (lax.div(row, block) * slots).astype(f32)
    spot = jnp.where(routed, base + count_before, -1.0)
    spot_out[...] = spot
    packed_out[...] = lax.dot_general(
        one_hot(spot, 8 * slots), grads_out[...], (((0,), (0,)), ((), ())),
        preferred_element_type=f32,
    ).astype(bf16)
    lane = lax.broadcasted_iota(jnp.int32, (rows, LANES), 1)
    tail_out[...] = jnp.where(lane == mine, row_grad, 0.0).astype(bf16)
    save_cot.wait()
    save_act.wait()


def grad_kernel(segments, half, *refs):
    count = len(segments)
    blocks = refs[:count]
    (near, far, spot, w_in, w_far, tail, alpha, side) = refs[count : count + 8]
    (d_own, d_other, sums, squash, slope) = refs[count + 8 :]
    rows = near.shape[0]
    block = rows // 8
    gain = alpha[0]
    start = pl.multiple_of(side[0] * half, half)
    for source, places in zip(blocks, segments):
        size = source.shape[0] // len(places)
        for part, to in enumerate(places):
            inputs = source[part * size : (part + 1) * size, pl.ds(start, half)].astype(f32)
            squashed = jnp.tanh(gain * inputs)
            squash[to : to + size, :] = squashed
            slope[to : to + size, :] = (1.0 - squashed * squashed) * inputs
    slots = far.shape[0]
    mirrored = jnp.concatenate([far[slots // 2 :, :], far[: slots // 2, :]], axis=0)
    mirrored = jnp.dot(
        one_hot(spot[...], slots), mirrored, preferred_element_type=f32
    ).astype(bf16)

    def place(cols, value):
        for x in range(2):
            for y in range(2):
                row = (x * 4 + y) * block
                d_own[x, y, :, cols] = value[row : row + block]
                row = (x * 4 + 2 + y) * block
                d_other[x, y, :, cols] = value[row : row + block]

    place(slice(half, half + LANES), tail[...])
    step = 512
    for at in range(0, half, step):
        cols = slice(at, at + step)
        part = jnp.dot(
            near[...],
            w_in[:, pl.ds(pl.multiple_of(start + at, step), step)],
            preferred_element_type=f32,
        )
        part = part + jnp.dot(mirrored, w_far[:, cols], preferred_element_type=f32)
        short = part.astype(bf16)
        place(cols, short)
        part = short.astype(f32)
        sums[0:1, cols] = jnp.sum(part, axis=0, keepdims=True)
        sums[1:2, cols] = jnp.sum(part * squash[:, cols], axis=0, keepdims=True)
        sums[2:3, cols] = jnp.sum(part * slope[:, cols], axis=0, keepdims=True)
        sums[3:8, cols] = jnp.zeros((5, step), f32)


def pack_kernel(tokens, cotangent, ids, probs, out):
    width = tokens.shape[1]
    top, block = ids.shape
    names = ids[...]
    shares = probs[...].astype(f32)
    label = lax.broadcasted_iota(jnp.int32, (LANES, block), 0)
    table = jnp.zeros((LANES, block), f32)
    for k in range(top):
        table = table + jnp.where(label == names[k : k + 1, :], shares[k : k + 1, :], 0.0)
    row = lax.broadcasted_iota(jnp.int32, (block, block), 0)
    column = lax.broadcasted_iota(jnp.int32, (block, block), 1)
    unit = jnp.where(row == column, 1.0, 0.0).astype(bf16)
    out[:, 2 * width :] = contract_width(unit, table.astype(bf16)).astype(bf16)
    out[:, :width] = tokens[...]
    out[:, width : 2 * width] = cotangent[...]


def join_kernel(first, second, out):
    size = first.shape[0]
    out[:size, :] = first[...]
    out[size:, :] = second[...]


def down_kernel(count, hidden, *refs):
    kept = refs[:count]
    out, held, sems = refs[count:]
    half = kept[0].shape[0] // 2
    copies = []
    for batch in range(2):
        for k in range(count):
            copy = pltpu.make_async_copy(
                kept[k].at[batch * half : (batch + 1) * half, :],
                held.at[batch, k * half : (k + 1) * half, :],
                sems.at[batch, k],
            )
            copy.start()
            copies.append(copy)
    total = None
    for batch in range(2):
        for copy in copies[batch * count : (batch + 1) * count]:
            copy.wait()
        term = lax.dot_general(
            held[batch, :, :hidden],
            held[batch, :, hidden:],
            (((0,), (0,)), ((), ())),
            preferred_element_type=f32,
        )
        term = term.astype(bf16).astype(f32)
        total = term if total is None else total + term
    out[...] = total.astype(bf16)


def whole():
    return pl.BlockSpec(memory_space=pltpu.VMEM)


def scalar():
    return pl.BlockSpec(memory_space=pltpu.SMEM)


def dense_shards(tokens, cotangent, expert_ids, gate_probs, alpha, gamma, beta, w_in, w_down):
    experts = lax.axis_size("expert")
    planes = experts // 4
    block = tokens.shape[1]
    width = tokens.shape[2]
    hidden = w_down.shape[1]
    rows = 8 * block
    slots = 3 * block * expert_ids.shape[2] // (2 * experts)
    me = lax.axis_index("expert")

    def go_x(v):
        return lax.ppermute(v, "dp", [(0, 1), (1, 0)])

    def go_y(v):
        return lax.ppermute(v, "expert", [(e, e ^ 2) for e in range(experts)])

    def go_core(v):
        return lax.ppermute(v, "expert", [(e, e ^ 1) for e in range(experts)])

    def go_z(v):
        return lax.ppermute(v, "expert", [(e, (e + 4) % experts) for e in range(experts)])

    def go_jump(v, by):
        return lax.ppermute(v, "expert", [(e, e ^ by) for e in range(experts)])

    def go_far(v, by):
        pairs = [
            (2 * e + x, 2 * (e ^ by) + 1 - x) for e in range(experts) for x in range(2)
        ]
        return lax.ppermute(v, ("expert", "dp"), pairs)

    lanes = jnp.arange(LANES, dtype=jnp.int32)
    picks = expert_ids[0][:, :, None] == lanes[None, None, :]
    own = pl.pallas_call(
        pack_kernel,
        out_shape=jax.ShapeDtypeStruct((block, 2 * width + LANES), bf16),
        in_specs=[whole()] * 4,
        out_specs=whole(),
        name="pack",
    )(tokens[0], cotangent[0], expert_ids[0].T, gate_probs[0].T)

    flat_in = w_in[0].reshape(2 * hidden, width)
    flat_down = w_down[0]
    gamma_row = gamma.reshape(1, width)
    beta_row = beta.reshape(1, width)
    mine = me.reshape(1).astype(jnp.int32)
    half = width // 2
    side = lax.axis_index("dp").astype(jnp.int32)
    w_send = lax.dynamic_slice_in_dim(flat_in, (1 - side) * half, half, axis=1)

    def segments_of(arrays):
        places = [
            (x * 4 + core * 2 + y) * block
            for core in range(2)
            for y in range(2)
            for x in range(2)
        ]
        size = 8 // len(arrays)
        return tuple(tuple(places[k : k + size]) for k in range(0, 8, size))

    params = pltpu.CompilerParams(vmem_limit_bytes=14 << 20)

    def first_half(arrays):
        return pl.pallas_call(
            functools.partial(rows_kernel, segments_of(arrays), width, hidden),
            out_shape=(
                jax.ShapeDtypeStruct((rows, 2 * hidden), bf16),
                jax.ShapeDtypeStruct((8 * slots, 2 * hidden), bf16),
                jax.ShapeDtypeStruct((rows, LANES), f32),
                pltpu.HBM((rows, hidden + width), bf16),
                jax.ShapeDtypeStruct((rows, LANES), bf16),
            ),
            in_specs=[whole()] * (len(arrays) + 4) + [scalar(), scalar()],
            out_specs=(whole(),) * 3 + (pl.BlockSpec(memory_space=pltpu.HBM), whole()),
            scratch_shapes=[
                pltpu.VMEM((rows, width), bf16),
                pltpu.VMEM((rows, width), bf16),
                pltpu.VMEM((rows, LANES), f32),
                pltpu.VMEM((rows, hidden + width), bf16),
                pltpu.SemaphoreType.DMA((2,)),
            ],
            compiler_params=params,
            name="rows",
        )(*arrays, flat_in, flat_down, gamma_row, beta_row, alpha, mine)

    def second_half(arrays, near, far, spot, w_far, tail):
        return pl.pallas_call(
            functools.partial(grad_kernel, segments_of(arrays), half),
            out_shape=(
                jax.ShapeDtypeStruct((2, 2, block, half + LANES), bf16),
                jax.ShapeDtypeStruct((2, 2, block, half + LANES), bf16),
                jax.ShapeDtypeStruct((8, half), f32),
            ),
            in_specs=[whole()] * (len(arrays) + 6) + [scalar(), scalar()],
            out_specs=(whole(),) * 3,
            scratch_shapes=[
                pltpu.VMEM((rows, half), f32),
                pltpu.VMEM((rows, half), f32),
            ],
            compiler_params=params,
            name="grads",
        )(*arrays, near, far, spot, flat_in, w_far, tail, alpha, side.reshape(1))

    fence = lax.optimization_barrier
    def join(first, second):
        return pl.pallas_call(
            join_kernel,
            out_shape=jax.ShapeDtypeStruct((2 * block, 2 * width + LANES), bf16),
            in_specs=[whole()] * 2,
            out_specs=whole(),
            name="join",
        )(first, second)

    near, far, near_c, far_c, w_far = {0: [own]}, {}, {}, {}, {}
    state = {"a": near, "b": far, "c": near_c, "d": far_c, "w": w_far}
    grads, kept, tails, other, packed, spots = {}, {}, {}, {}, {}, {}
    state.update(grads=grads, other=other, packed=packed)
    d_own, d_got, totals, sent, value = {}, {}, {}, {}, {}
    state.update(d_own=d_own, d_got=d_got, totals=totals, sent=sent, value=value)

    def make_down(held):
        return pl.pallas_call(
            functools.partial(down_kernel, planes, hidden),
            out_shape=jax.ShapeDtypeStruct((hidden, width), bf16),
            in_specs=[pl.BlockSpec(memory_space=pltpu.HBM)] * planes,
            out_specs=whole(),
            scratch_shapes=[
                pltpu.VMEM((2, planes * rows // 2, hidden + width), bf16),
                pltpu.SemaphoreType.DMA((2, planes)),
            ],
            compiler_params=pltpu.CompilerParams(vmem_limit_bytes=20 << 20),
            name="down",
        )(*[pltpu.with_memory_space_constraint(one, pltpu.HBM) for one in held])

    def step(*late):
        now = {
            name: {k: v for k, v in held.items() if (name, k) not in late}
            for name, held in state.items()
        }
        new = fence(now)
        for name, held in state.items():
            held.update(new[name])

    def rows_of(k):
        arrays = near[k] + far[k] + near_c[k] + far_c[k]
        grads[k], packed[k], spots[k], kept[k], tails[k] = first_half(arrays)

    def grads_of(k):
        arrays = near[k] + far[k] + near_c[k] + far_c[k]
        d_own[k], moved, totals[k] = second_half(
            arrays, grads[k], other[k], spots[k], w_far[0], tails[k]
        )
        d_got[k] = go_core(moved)

    def send_y(k):
        sent[k] = go_y(add16(d_own[k][:, 1], d_got[k][:, 1]))

    def total_of(k):
        kept = d_own[k][:, 0].astype(f32) + d_got[k][:, 0].astype(f32)
        return kept + sent[k].astype(f32)

    def hop(k):
        carried = total_of(k)
        if k > 1:
            carried = carried + value[k].astype(f32)
        value[(k + 1) % planes] = go_z(carried.astype(bf16))

    near[0].append(go_x(own))
    near[1] = [go_z(own)]
    far[0] = [go_y(own)]
    near_c[0] = [go_core(own)]
    state["s"] = {0: w_send}
    step()
    w_send = state.pop("s")[0]
    near[1].append(go_z(near[0][1]))
    far[0].append(go_y(near[0][1]))
    near_c[0].append(go_core(near[0][1]))
    far_c[0] = [go_core(far[0][0])]
    w_far[0] = go_x(w_send)
    step(("w", 0))
    near[1] = [join(*near[1])]
    for k in range(1, 3):
        near[k + 1] = [go_z(near[k][0])]
        far[k] = [go_y(near[k][0])]
        near_c[k] = [go_core(near[k][0])]
        if k == 1:
            far_c[0].append(go_core(far[0][1]))
        else:
            far_c[1] = [go_core(far[1][0])]
        rows_of(k - 1)
        if k == 2:
            other[0] = go_x(packed[0])
        step(("w", 0) if k == 1 else ("other", 0))
    other[1] = go_x(packed[1])
    far[3] = [go_y(near[3][0])]
    near_c[3] = [go_core(near[3][0])]
    far_c[2] = [go_core(far[2][0])]
    rows_of(2)
    grads_of(0)
    step()
    other[2] = go_x(packed[2])
    far_c[3] = [go_core(far[3][0])]
    rows_of(3)
    other[1], packed[3] = fence((other[1], packed[3]))
    grads_of(1)
    step()
    other[3] = go_x(packed[3])
    send_y(1)
    early = totals[1] + go_core(totals[1])
    other[2], early = fence((other[2], early))
    grads_of(2)
    hop(1)
    send_y(2)
    d_got[0], d_got[2] = fence((d_got[0], d_got[2]))
    send_y(0)
    step(("sent", 0), ("value", 2))
    grads_of(3)
    hop(2)
    pool = {}
    late = totals[2] + totals[3] + totals[0]
    pool[0] = early + (late + go_core(late))
    state["pool"] = pool
    step(("value", 3), ("sent", 2), ("value", 2), ("sent", 0))
    send_y(3)
    part = pool[0]
    mine_sums = part + go_y(part)
    cross_sums = go_x(part) + go_far(part, 2)
    pool[0] = jnp.concatenate([mine_sums, cross_sums], axis=0)
    step(("pool", 0))
    hop(3)
    pool[0] = pool[0] + go_jump(pool[0], 4)
    step()
    kept[3], pool[0] = fence((kept[3], pool[0]))
    final = total_of(0) + value[0].astype(f32)
    crossed = go_x(final[1].astype(bf16)).astype(f32)
    left = jnp.where(side == 0, final[0, :, :half], crossed[:, :half])
    right = jnp.where(side == 0, crossed[:, :half], final[0, :, :half])
    grad_normed = jnp.concatenate([left, right], axis=1)
    row_grads = final[0, :, half:] + crossed[:, half:]
    grad_down = make_down([kept[k] for k in range(planes)])
    sums = pool[0] + go_jump(pool[0], 8)
    mine_sums, cross_sums = sums[:8], sums[8:]
    sums = jnp.concatenate(
        [
            jnp.where(side == 0, mine_sums, cross_sums),
            jnp.where(side == 0, cross_sums, mine_sums),
        ],
        axis=1,
    )

    inputs = tokens[0].astype(f32)
    squashed = jnp.tanh(alpha[0] * inputs)
    pre_grad = grad_normed * gamma * (1.0 - squashed * squashed)
    grad_tokens = (cotangent[0].astype(f32) + alpha[0] * pre_grad).astype(bf16)
    grad_probs = jnp.sum(jnp.where(picks, row_grads[:, None, :], 0.0), axis=2).astype(bf16)
    grad_beta = sums[0]
    grad_gamma = sums[1]
    grad_alpha = jnp.sum(sums[2] * gamma).reshape(1)
    return (
        grad_tokens[None],
        grad_probs[None],
        grad_down[None],
        grad_gamma,
        grad_beta,
        grad_alpha,
    )


def slot_layout(ids_local, expert_count, capacity):
    token_count, top_count = ids_local.shape
    labels = jnp.arange(expert_count, dtype=jnp.int32)
    onehot = (ids_local[:, :, None] == labels[None, None, :]).astype(jnp.int32)
    picks = jnp.sum(onehot, axis=1)
    order = jnp.arange(token_count, dtype=jnp.int32)
    earlier = (order[None, :] < order[:, None]).astype(f32)
    before = jnp.dot(earlier, picks.astype(f32), precision=lax.Precision.HIGHEST)
    slots = jnp.sum(onehot * before.astype(jnp.int32)[:, None, :], axis=2)
    position = ids_local * capacity + slots
    pairs = jnp.arange(token_count * top_count, dtype=jnp.int32)
    table = jnp.full((expert_count * capacity,), token_count * top_count, jnp.int32)
    table = table.at[position.reshape(-1)].set(pairs)
    return (position, table)


def routed_shards(tokens, cotangent, expert_ids, gate_probs, alpha, gamma, beta, w_in, w_down):
    expert_count = lax.axis_size("expert")
    token_count = tokens.shape[1]
    top_count = expert_ids.shape[2]
    width = tokens.shape[2]
    capacity = 3 * token_count * top_count // (2 * expert_count)
    rows_total = expert_count * capacity
    inputs = tokens[0].astype(jnp.float32)
    squashed = jnp.tanh(alpha[0] * inputs)
    normed = (gamma * squashed + beta).astype(jnp.bfloat16)
    position, table = slot_layout(expert_ids[0], expert_count, capacity)
    source_token = table // top_count
    zero_row = jnp.zeros((1, width), jnp.bfloat16)
    normed_pad = jnp.concatenate([normed, zero_row], axis=0)
    cot_pad = jnp.concatenate([cotangent[0], zero_row], axis=0)
    prob_pad = jnp.concatenate([gate_probs[0].reshape(-1), jnp.zeros((1,), jnp.bfloat16)], axis=0)
    send_rows = normed_pad[source_token].reshape(expert_count, capacity, width)
    send_cot = cot_pad[source_token].reshape(expert_count, capacity, width)
    send_prob = prob_pad[table].reshape(expert_count, capacity)

    def swap(value):
        return lax.all_to_all(value, "expert", split_axis=0, concat_axis=0, tiled=True)

    in_rows = swap(send_rows).reshape(rows_total, width)
    cot_rows = swap(send_cot).reshape(rows_total, width)
    prob_rows = swap(send_prob).reshape(rows_total).astype(jnp.float32)
    gate_up = lax.all_gather(w_in, "dp", axis=2, tiled=True)
    w_lower = lax.all_gather(w_down, "dp", axis=1, tiled=True)[0]
    w_gate = gate_up[0, 0]
    w_upper = gate_up[0, 1]
    gate_pre = contract_width(in_rows, w_gate)
    up_value = contract_width(in_rows, w_upper)
    sigma = jax.nn.sigmoid(gate_pre)
    activation = (gate_pre * sigma * up_value).astype(jnp.bfloat16)
    back = contract_width(cot_rows, w_lower)
    weight_row = residual_scale * prob_rows
    scaled_cot = (weight_row[:, None] * cot_rows.astype(jnp.float32)).astype(jnp.bfloat16)
    row_grad = residual_scale * jnp.sum(activation.astype(jnp.float32) * back, axis=1)
    d_act = weight_row[:, None] * back
    d_gate = (d_act * up_value * sigma * (1.0 + gate_pre * (1.0 - sigma))).astype(jnp.bfloat16)
    d_up = (d_act * gate_pre * sigma).astype(jnp.bfloat16)
    d_rows = (
        jnp.dot(d_gate, w_gate, preferred_element_type=jnp.float32)
        + jnp.dot(d_up, w_upper, preferred_element_type=jnp.float32)
    ).astype(jnp.bfloat16)
    back_rows = swap(d_rows.reshape(expert_count, capacity, width))
    back_probs = swap(row_grad.astype(jnp.bfloat16).reshape(expert_count, capacity))
    partial_grad = lax.dot_general(
        activation, scaled_cot, (((0,), (0,)), ((), ())), preferred_element_type=jnp.float32
    )
    grad_down = lax.psum_scatter(
        partial_grad[None].astype(jnp.bfloat16), "dp", scatter_dimension=1, tiled=True
    )
    picked = back_rows.reshape(rows_total, width)[position]
    grad_normed = jnp.sum(picked.astype(jnp.float32), axis=1)
    grad_probs = back_probs.reshape(rows_total)[position]
    gamma_part = jnp.sum(grad_normed * squashed, axis=0)
    beta_part = jnp.sum(grad_normed, axis=0)
    pre_grad = grad_normed * gamma * (1.0 - squashed * squashed)
    alpha_part = jnp.sum(pre_grad * inputs).reshape(1)
    grad_gamma, grad_beta, grad_alpha = lax.psum(
        (gamma_part, beta_part, alpha_part), ("expert", "dp")
    )
    grad_tokens = (cotangent[0].astype(jnp.float32) + alpha[0] * pre_grad).astype(jnp.bfloat16)
    return (grad_tokens[None], grad_probs[None], grad_down, grad_gamma, grad_beta, grad_alpha)


def shards(*arrays):
    experts = lax.axis_size("expert")
    top_count = arrays[2].shape[2]
    dense = (
        lax.axis_size("dp") == 2
        and experts == 16
        and arrays[0].shape[1] == 32
        and top_count == 8
        and 2 * top_count >= experts
        and arrays[0].shape[2] % 2048 == 0
    )
    return (dense_shards if dense else routed_shards)(*arrays)


def solution(mesh):
    placed = (
        P("dp", "expert", None),
        P("dp", "expert", None),
        P("dp", "expert", None),
        P("dp", "expert", None),
        P(),
        P(),
        P(),
        P("expert", None, "dp", None),
        P("expert", "dp", None),
    )
    return jax.shard_map(
        shards,
        mesh=mesh,
        in_specs=placed,
        out_specs=(
            P("dp", "expert", None),
            P("dp", "expert", None),
            P("expert", "dp", None),
            P(),
            P(),
            P(),
        ),
        check_vma=False,
    )
```
